32 devices in a mesh: dp: 8 (over z, x), seq: 4 (over y, core).
Axes of the slice: x: 2, y: 2, z: 4, core: 2. Of those that a mesh axis runs over, the one named last changes fastest.
Arguments:
- inputs: bfloat16 [192, 1024, 512], P('dp', 'seq'), may hold values from -6 to 6
- lengths: int32 [192], P('dp'), may hold values from 256 to 1024, as said below
- cotangent: bfloat16 [192, 1024, 512], P('dp', 'seq'), may hold values from -6 to 6
- w_query: bfloat16 [512, 512], P(('dp', 'seq')), may hold values from -0.25 to 0.25
- w_key: bfloat16 [512, 512], P(('dp', 'seq')), may hold values from -0.25 to 0.25
- w_value: bfloat16 [512, 512], P(('dp', 'seq')), may hold values from -0.25 to 0.25
- w_out: bfloat16 [512, 512], P(('dp', 'seq')), may hold values from -0.5 to 0.5
- w_up: bfloat16 [512, 2048], P(('dp', 'seq')), may hold values from -0.25 to 0.25
- w_down: bfloat16 [2048, 512], P(('dp', 'seq')), may hold values from -0.125 to 0.125
- gain_attn: bfloat16 [512], P(('dp', 'seq')), may hold values from 0.25 to 1.75
- gain_mlp: bfloat16 [512], P(('dp', 'seq')), may hold values from 0.25 to 1.75
Outputs:
- output: bfloat16 [192, 1024, 512], P('dp', 'seq')
- grad_input: float32 [192, 1024, 512], P('dp', 'seq')
- grad_query: float32 [512, 512], P(('dp', 'seq'))
- grad_key: float32 [512, 512], P(('dp', 'seq'))
- grad_value: float32 [512, 512], P(('dp', 'seq'))
- grad_out: float32 [512, 512], P(('dp', 'seq'))
- grad_up: float32 [512, 2048], P(('dp', 'seq'))
- grad_down: float32 [2048, 512], P(('dp', 'seq'))
- grad_gain_attn: float32 [512], P(('dp', 'seq'))
- grad_gain_mlp: float32 [512], P(('dp', 'seq'))
The draws below stay inside these ranges and needn't reach their ends.
Inputs may be any that keep to these rules, and one draw needn't show every extreme that they name: Sequence b's valid slots are its first lengths[b]; some sequence has 1024 of them and some has 256.
All inputs are finite; a program needn't handle non-finite values.
Results may differ from the reference program's by a relative error of at most 0.012.
Values may be sent and summed in bfloat16 or wider, within the bound.
A program may use at most 320 MiB of HBM per device.

```python
import math
import jax
import jax.numpy as jnp
from jax import lax

D = 512
H = 8
HD = 64
FF = 2048
SPAN = 128
LEN = 1024
SEQS = 192


def draw_inputs(key, part):
    key_own, key_common = jax.random.split(jax.random.fold_in(key, 11), 2)
    span_count = LEN // SPAN
    own_part = jax.random.normal(key_own, (SEQS, LEN, D), jnp.float32)
    common = jax.random.normal(key_common, (SEQS, span_count, 1, D), jnp.float32)
    common = jnp.broadcast_to(common, (SEQS, span_count, SPAN, D)).reshape(SEQS, LEN, D)
    mixed_draw = jnp.clip(0.75 * own_part + 0.75 * common, -6.0, 6.0)
    return mixed_draw.astype(jnp.bfloat16)


def draw_lengths(key, part):
    drawn = jax.random.randint(jax.random.fold_in(key, 5), (SEQS,), LEN // 4, LEN + 1, dtype=jnp.int32)
    drawn = drawn.at[0].set(LEN)
    drawn = drawn.at[1].set(LEN // 4)
    return drawn


def block_scale(own_key, extent, shards, low, largest):
    level, own = 1.0, jax.random.fold_in(own_key, 6)
    for dim, parts in shards:
        draws = jnp.exp(jax.random.uniform(jax.random.fold_in(own, dim), (parts,), jnp.float32, low / len(shards), largest / len(shards)))
        level = level * jnp.repeat(draws, extent[dim] // parts).reshape([-1 if axis == dim else 1 for axis in range(len(extent))])
    return level


def gaussian(key, dims, deviation, most, pieces=(), kind=jnp.bfloat16):
    result = jax.random.normal(key, dims, jnp.float32) * deviation
    if len(pieces) > 0:
        result = block_scale(key, dims, pieces, -0.22, 0.18) * result
    return jnp.clip(result, min=-most, max=most).astype(kind)


def setup_inputs(seed: int = 0) -> dict:
    keys = jax.random.split(jax.random.key(seed), 12)
    inputs = draw_inputs(jax.random.fold_in(keys[11], 71), 0)
    lengths = draw_lengths(jax.random.fold_in(keys[11], 71), 0)
    cotangent = gaussian(keys[2], (SEQS, LEN, D), 1.0, 6.0, ((0, 8), (1, 4)))
    w_query = gaussian(keys[3], (D, D), D ** -0.5, 0.25, ((0, 32),))
    w_key = gaussian(keys[4], (D, D), D ** -0.5, 0.25, ((0, 32),))
    w_value = gaussian(keys[5], (D, D), D ** -0.5, 0.25, ((0, 32),))
    w_out = gaussian(keys[6], (D, D), (D // 4) ** -0.5, 0.5, ((0, 32),))
    w_up = gaussian(keys[7], (D, FF), D ** -0.5, 0.25, ((0, 32),))
    w_down = gaussian(keys[8], (FF, D), FF ** -0.5, 0.125, ((0, 32),))
    gain_attn = jnp.clip(1.0 + 0.15 * jax.random.normal(keys[9], (D,), jnp.float32), 0.25, 1.75).astype(jnp.bfloat16)
    gain_mlp = jnp.clip(1.0 + 0.15 * jax.random.normal(keys[10], (D,), jnp.float32), 0.25, 1.75).astype(jnp.bfloat16)
    return dict(inputs=inputs, lengths=lengths, cotangent=cotangent, w_query=w_query, w_key=w_key, w_value=w_value, w_out=w_out, w_up=w_up, w_down=w_down, gain_attn=gain_attn, gain_mlp=gain_mlp)


@jax.custom_vjp
def low(v):
    return lax.optimization_barrier(v.astype(jnp.bfloat16)).astype(jnp.float32)

@jax.custom_vjp
def low_back(v):
    return v

def low_keep(v):
    return (low(v), None)

def low_pass(kept, grad):
    return (grad,)

def back_keep(v):
    return (v, None)

def back_low(kept, grad):
    return (low(grad),)
low.defvjp(low_keep, low_pass)
low_back.defvjp(back_keep, back_low)

def matmul_high(left, right):
    return jnp.einsum('bld,de->ble', left, right, precision=lax.Precision.HIGHEST)

def normed(values, gain_vec):
    return values * lax.rsqrt(lax.optimization_barrier(jnp.mean(values * values, axis=-1, keepdims=True)) + 1e-06) * gain_vec

def forward(params, inputs_blk, valid_mask):
    w_query, w_key, w_value, w_out, w_up, w_down, gain_attn, gain_mlp = params
    seq_count, length_all, model_width = inputs_blk.shape
    span_count = length_all // SPAN
    normal_in = low(normed(inputs_blk, gain_attn))
    query = low(low_back(matmul_high(normal_in, w_query)))
    keys_all = low(low_back(matmul_high(normal_in, w_key)))
    values_all = low(low_back(matmul_high(normal_in, w_value)))
    key_summary = low(lax.optimization_barrier(jnp.mean(keys_all.reshape(seq_count, span_count, SPAN, model_width), axis=2)))
    value_summary = low(lax.optimization_barrier(jnp.mean(values_all.reshape(seq_count, span_count, SPAN, model_width), axis=2)))
    shape_five = (seq_count, span_count, SPAN, H, HD)
    query_h = query.reshape(shape_five)
    key_h = keys_all.reshape(shape_five)
    value_h = values_all.reshape(shape_five)
    key_sh = key_summary.reshape(seq_count, span_count, H, HD)
    value_sh = value_summary.reshape(seq_count, span_count, H, HD)
    near_score = jnp.einsum('bsihd,bsjhd->bshij', query_h, key_h, precision=lax.Precision.HIGHEST)
    far_score = jnp.einsum('bsihd,bthd->bshit', query_h, key_sh, precision=lax.Precision.HIGHEST)
    scores = low_back(HD ** (-0.5) * jnp.concatenate([near_score, far_score], axis=-1))
    row_index = lax.broadcasted_iota(jnp.int32, (SPAN, SPAN), 0)
    col_index = lax.broadcasted_iota(jnp.int32, (SPAN, SPAN), 1)
    causal = jnp.broadcast_to((row_index >= col_index)[None, None], (span_count, 1, SPAN, SPAN))
    span_index = jnp.arange(span_count, dtype=jnp.int32)
    earlier = jnp.broadcast_to((span_index[None, :] < span_index[:, None])[:, None, None, :], (span_count, 1, SPAN, span_count))
    allowed = jnp.concatenate([causal, earlier], axis=-1)
    probs = low(jax.nn.softmax(jnp.where(allowed, scores, -1e+30), axis=-1))
    near_prob = probs[..., :SPAN]
    far_prob = probs[..., SPAN:]
    attended = jnp.einsum('bshij,bsjhd->bsihd', near_prob, value_h, precision=lax.Precision.HIGHEST)
    attended = attended + jnp.einsum('bshit,bthd->bsihd', far_prob, value_sh, precision=lax.Precision.HIGHEST)
    attended = low(low_back(attended.reshape(seq_count, length_all, model_width)))
    residual_mid = inputs_blk + low_back(matmul_high(attended, w_out))
    normal_mid = low(normed(residual_mid, gain_mlp))
    up_proj = low_back(matmul_high(normal_mid, w_up))
    activated = low(jax.nn.gelu(up_proj))
    return (residual_mid + low_back(matmul_high(activated, w_down))) * valid_mask

def reference(inputs, lengths, cotangent, w_query, w_key, w_value, w_out, w_up, w_down, gain_attn, gain_mlp):
    params = tuple((weights.astype(jnp.float32) for weights in (w_query, w_key, w_value, w_out, w_up, w_down, gain_attn, gain_mlp)))
    seq_group = math.gcd(SEQS, max(1, 4096 // LEN))
    group_count = SEQS // seq_group
    inputs_all = inputs.astype(jnp.float32).reshape(group_count, seq_group, LEN, D)
    cot_all = cotangent.astype(jnp.float32).reshape(group_count, seq_group, LEN, D)
    length_all = lengths.reshape(group_count, seq_group)

    def group_step(running, entry):
        inputs_blk, cot_blk, length_blk = entry
        valid_mask = (jnp.arange(LEN, dtype=jnp.int32)[None, :] < length_blk[:, None]).astype(jnp.float32)[..., None]
        result_blk, pullback = jax.vjp(lambda weights, values: forward(weights, values, valid_mask), params, inputs_blk)
        grad_params, grad_inputs = pullback(cot_blk)
        running = jax.tree.map(jnp.add, running, grad_params)
        return (running, (result_blk.astype(jnp.bfloat16), grad_inputs))
    zeros_init = tuple((jnp.zeros_like(weights) for weights in params))
    grads_total, (results, grad_inputs) = lax.scan(group_step, zeros_init, (inputs_all, cot_all, length_all))
    output = results.reshape(SEQS, LEN, D)
    grad_input = grad_inputs.reshape(SEQS, LEN, D)
    return (output, grad_input, grads_total[0], grads_total[1], grads_total[2], grads_total[3], grads_total[4], grads_total[5], grads_total[6], grads_total[7])
```

```python
from functools import partial

import jax
import jax.numpy as jnp
from jax import lax
from jax.experimental import pallas as pl
from jax.experimental.pallas import tpu as pltpu
from jax.sharding import PartitionSpec as P

H = 8
HD = 64
SPAN = 128
EPS = 1e-06
K0 = 0.7978845608028654
K1 = 0.044715
FARP = 16
f32 = jnp.float32
bf = jnp.bfloat16
MESH = pl.DeviceIdType.MESH
VMEM_LIMIT = 62 << 20


def dot(a, b, ca=1, cb=0):
    return lax.dot_general(a, b, (((ca,), (cb,)), ((), ())), preferred_element_type=f32)


def sds(shape, dtype):
    return jax.ShapeDtypeStruct(shape, dtype)


def full(shape):
    return pl.BlockSpec(shape, lambda i: (0,) * len(shape), pipeline_mode=pl.Buffered(1))


def pair_diag(a):
    lane = lax.broadcasted_iota(jnp.int32, a.shape, 1)
    zero = jnp.zeros_like(a)
    return jnp.concatenate([jnp.where(lane < HD, a, zero), jnp.where(lane >= HD, a, zero)], axis=0)


def causal_mask():
    j = lax.broadcasted_iota(jnp.int32, (SPAN, 2 * SPAN), 0)
    i = lax.broadcasted_iota(jnp.int32, (SPAN, 2 * SPAN), 1)
    return j <= jnp.where(i >= SPAN, i - SPAN, i)


def gain_row(tiles, which, ndev, rows):
    width = ndev * rows
    r = lax.broadcasted_iota(jnp.int32, (ndev * 8, 128), 0)
    l = lax.broadcasted_iota(jnp.int32, (ndev * 8, 128), 1)
    keep = jnp.where((r % 8 == which) & (l < rows), tiles, 0.0).astype(bf)
    a = lax.broadcasted_iota(jnp.int32, (128, width), 0)
    b = lax.broadcasted_iota(jnp.int32, (128, width), 1)
    spread = dot(keep, jnp.where(b % rows == a, 1.0, 0.0).astype(bf))
    d = lax.broadcasted_iota(jnp.int32, (ndev * 8, width), 0)
    c = lax.broadcasted_iota(jnp.int32, (ndev * 8, width), 1)
    return jnp.sum(jnp.where(d // 8 == c // rows, spread, 0.0), axis=0, keepdims=True)


class Place:
    def __init__(self, dims):
        self.nz, self.nx, self.ny, self.nc = dims
        dp, seq = lax.axis_index("dp"), lax.axis_index("seq")
        self.z, self.x = dp // self.nx, dp % self.nx
        self.y, self.c = seq // self.nc, seq % self.nc

    def at(self, z=None, x=None, y=None, c=None):
        z = self.z if z is None else z
        x = self.x if x is None else x
        y = self.y if y is None else y
        c = self.c if c is None else c
        return (z * self.nx + x, y * self.nc + c)

    def line(self, axis):
        return getattr(self, axis), getattr(self, "n" + axis)

    def partners(self, axis):
        me, n = self.line(axis)
        return [(o, (me + o) % n, (me + n - o) % n) for o in range(1, n)]

    def greet(self, others):
        barrier = pltpu.get_barrier_semaphore()
        for other in others:
            pl.semaphore_signal(barrier, inc=1, device_id=other, device_id_type=MESH)
        pl.semaphore_wait(barrier, len(others))

    def others(self):
        return [self.at(**{a: to}) for a in ("z", "x", "y", "c") for _, to, _ in self.partners(a)]


class Copies:
    def __init__(self, send_sem, recv_sem):
        self.send_sem, self.recv_sem, self.used = send_sem, recv_sem, 0

    def make(self, src, dst, landed, device):
        k = self.used
        self.used += 1
        out = pltpu.make_async_remote_copy(
            src_ref=src, dst_ref=dst, send_sem=self.send_sem.at[k], recv_sem=self.recv_sem.at[k],
            device_id=device, device_id_type=MESH,
        )
        into = pltpu.make_async_remote_copy(
            src_ref=src, dst_ref=landed, send_sem=self.send_sem.at[k], recv_sem=self.recv_sem.at[k],
            device_id=device, device_id_type=MESH,
        )
        return out, into


def start(copies):
    for out, _ in copies:
        out.start()


def finish(copies):
    for out, into in copies:
        out.wait_send()
        into.wait_recv()


def halves(ref):
    n = ref.shape[-1] // 2
    return pl.ds(0, n), pl.ds(n, n)


def gather_phases(pc, cp, pieces, wholes):
    z, x, y, c = pc.z, pc.x, pc.y, pc.c
    first, second, third, last = [], [], [], []
    for piece, whole in zip(pieces, wholes):
        for _, to, fr in pc.partners("z"):
            first.append(cp.make(piece, whole.at[z, x, y, c], whole.at[fr, x, y, c], pc.at(z=to)))
    for whole in wholes:
        a, b = halves(whole)
        for _, to, fr in pc.partners("x"):
            v = whole.at[:, x, y, c, :, a]
            second.append(cp.make(v, v, whole.at[:, fr, y, c, :, a], pc.at(x=to)))
        for _, to, fr in pc.partners("y"):
            v = whole.at[:, x, y, c, :, b]
            second.append(cp.make(v, v, whole.at[:, x, fr, c, :, b], pc.at(y=to)))
    for whole in wholes:
        a, b = halves(whole)
        for _, to, fr in pc.partners("y"):
            v = whole.at[:, :, y, c, :, a]
            third.append(cp.make(v, v, whole.at[:, :, fr, c, :, a], pc.at(y=to)))
        for _, to, fr in pc.partners("x"):
            v = whole.at[:, x, :, c, :, b]
            third.append(cp.make(v, v, whole.at[:, fr, :, c, :, b], pc.at(x=to)))
    for whole in wholes:
        for _, to, fr in pc.partners("c"):
            v = whole.at[:, :, :, c]
            last.append(cp.make(v, v, whole.at[:, :, :, fr], pc.at(c=to)))
    return first, second, third, last


def gather_kernel(dims, spans_dev, n_w, *refs):
    x_ref = refs[0]
    pieces = refs[1 : 1 + n_w]
    wholes = refs[1 + n_w : 1 + 2 * n_w]
    mean_out = refs[1 + 2 * n_w]
    mean_ref, local_sem, send_sem, recv_sem = refs[2 + 2 * n_w :]
    pc = Place(dims)
    cp = Copies(send_sem, recv_sem)
    phases = gather_phases(pc, cp, pieces, wholes)
    seq = lax.axis_index("seq")
    seqn = pc.ny * pc.nc
    t0 = seq * spans_dev
    i, n = pl.program_id(0), pl.num_programs(0)
    means = []
    for o in range(1, seqn):
        to, fr = (seq + o) % seqn, (seq + seqn - o) % seqn
        v = mean_ref.at[pl.ds(t0, spans_dev)]
        means.append(
            cp.make(v, v, mean_ref.at[pl.ds(fr * spans_dev, spans_dev)], (lax.axis_index("dp"), to))
        )
    own = [
        pltpu.make_async_copy(piece, whole.at[pc.z, pc.x, pc.y, pc.c], local_sem.at[k])
        for k, (piece, whole) in enumerate(zip(pieces, wholes))
    ]

    @pl.when(i == 0)
    def _():
        seq_peers = [(lax.axis_index("dp"), (seq + o) % seqn) for o in range(1, seqn)]
        zx = [pc.at(**{a: to}) for a in ("z", "x") for _, to, _ in pc.partners(a)]
        pc.greet(zx + seq_peers)
        for copy in own:
            copy.start()
        start(phases[0])

    T = x_ref.shape[0]
    x = x_ref[...].astype(f32)
    r = lax.rsqrt(jnp.mean(x * x, axis=1, keepdims=True) + EPS)
    xr = x * r
    nseq = T // (SPAN * spans_dev)
    for s in range(T // SPAN):
        row = jnp.sum(xr[s * SPAN : (s + 1) * SPAN], axis=0, keepdims=True) * (1.0 / SPAN)
        mean_ref[t0 + s % spans_dev, pl.ds(i * nseq + s // spans_dev, 1), :] = row

    @pl.when(i == n - 1)
    def _():
        start(means)
        for copy in own:
            copy.wait()
        finish(phases[0])
        for k in range(1, 4):
            start(phases[k])
            finish(phases[k])
        finish(means)
        mean_out[...] = mean_ref[...]


def gather_call(dims, slots, block, x, pieces):
    n_tok, width = x.shape
    spans_dev = slots // SPAN
    seqs = n_tok // slots
    nz, nx, ny, nc = dims
    spans_all = spans_dev * ny * nc
    n_w = len(pieces)
    hbm = pl.BlockSpec(memory_space=pl.ANY)
    copies = n_w * ((nz - 1) + 2 * (nx - 1) + 2 * (ny - 1) + (nc - 1)) + ny * nc - 1
    return pl.pallas_call(
        partial(gather_kernel, dims, spans_dev, n_w),
        grid=(n_tok // block,),
        in_specs=[pl.BlockSpec((block, width), lambda i: (i, 0))] + [hbm] * n_w,
        out_specs=[hbm] * n_w + [full((spans_all, seqs, width))],
        out_shape=[sds(dims + p.shape, p.dtype) for p in pieces] + [sds((spans_all, seqs, width), f32)],
        scratch_shapes=[
            pltpu.VMEM((spans_all, seqs, width), f32),
            pltpu.SemaphoreType.DMA((n_w,)),
            pltpu.SemaphoreType.DMA((copies,)),
            pltpu.SemaphoreType.DMA((copies,)),
        ],
        compiler_params=pltpu.CompilerParams(
            vmem_limit_bytes=VMEM_LIMIT, collective_id=0, has_side_effects=True,
            dimension_semantics=("arbitrary",),
        ),
    )(x, *pieces)


def scatter_kernel(dims, spans_dev, g_ref, dks_ref, dvs_ref, sum_ref, own_k_ref, own_v_ref,
                   got1, held1, got2a, got2b, held2, got3a, got3b, held3, got4,
                   far_send, far_got, send_sem, recv_sem):
    pc = Place(dims)
    cp = Copies(send_sem, recv_sem)
    z, x, y, c = pc.z, pc.x, pc.y, pc.c
    seq, dp = lax.axis_index("seq"), lax.axis_index("dp")
    seqn = pc.ny * pc.nc
    seq_peers = [(dp, (seq + o) % seqn) for o in range(1, seqn)]
    zx = [pc.at(**{a: to}) for a in ("z", "x") for _, to, _ in pc.partners(a)]
    pc.greet(zx + seq_peers)
    a, b = halves(g_ref)
    one = [
        cp.make(g_ref.at[:, :, :, to], got1.at[o - 1], got1.at[o - 1], pc.at(c=to))
        for o, to, _ in pc.partners("c")
    ]
    start(one)
    far_send[0] = dks_ref[...].astype(bf)
    far_send[1] = dvs_ref[...].astype(bf)
    far = []
    for o in range(1, seqn):
        to = (seq + o) % seqn
        far.append(
            cp.make(
                far_send.at[:, pl.ds(to * spans_dev, spans_dev)], far_got.at[o - 1], far_got.at[o - 1], (dp, to)
            )
        )
    start(far)
    finish(one)
    acc = g_ref[:, :, :, c].astype(f32)
    for o in range(pc.nc - 1):
        acc = acc + got1[o].astype(f32)
    held1[...] = acc.astype(bf)
    two = [
        cp.make(held1.at[:, to, :, :, a], got2a.at[o - 1], got2a.at[o - 1], pc.at(x=to))
        for o, to, _ in pc.partners("x")
    ] + [
        cp.make(held1.at[:, :, to, :, b], got2b.at[o - 1], got2b.at[o - 1], pc.at(y=to))
        for o, to, _ in pc.partners("y")
    ]
    start(two)
    finish(far)
    own = pl.ds(seq * spans_dev, spans_dev)
    tot_k, tot_v = dks_ref[own], dvs_ref[own]
    for o in range(seqn - 1):
        tot_k = tot_k + far_got[o, 0].astype(f32)
        tot_v = tot_v + far_got[o, 1].astype(f32)
    own_k_ref[...] = tot_k.astype(bf)
    own_v_ref[...] = tot_v.astype(bf)
    finish(two)
    half = g_ref.shape[-1] // 2
    acc = held1[:, x, :, :, :half].astype(f32)
    for o in range(pc.nx - 1):
        acc = acc + got2a[o].astype(f32)
    held2[0, :, : pc.ny] = acc.astype(bf)
    acc = held1[:, :, y, :, half:].astype(f32)
    for o in range(pc.ny - 1):
        acc = acc + got2b[o].astype(f32)
    held2[1, :, : pc.nx] = acc.astype(bf)
    three = [
        cp.make(held2.at[0, :, to], got3a.at[o - 1], got3a.at[o - 1], pc.at(y=to))
        for o, to, _ in pc.partners("y")
    ] + [
        cp.make(held2.at[1, :, to], got3b.at[o - 1], got3b.at[o - 1], pc.at(x=to))
        for o, to, _ in pc.partners("x")
    ]
    start(three)
    finish(three)
    acc = held2[0, :, y].astype(f32)
    for o in range(pc.ny - 1):
        acc = acc + got3a[o].astype(f32)
    held3[:, :, :half] = acc.astype(bf)
    acc = held2[1, :, x].astype(f32)
    for o in range(pc.nx - 1):
        acc = acc + got3b[o].astype(f32)
    held3[:, :, half:] = acc.astype(bf)
    four = [
        cp.make(held3.at[to], got4.at[o - 1], got4.at[o - 1], pc.at(z=to)) for o, to, _ in pc.partners("z")
    ]
    start(four)
    finish(four)
    acc = held3[z].astype(f32)
    for o in range(pc.nz - 1):
        acc = acc + got4[o].astype(f32)
    sum_ref[...] = acc


def scatter_call(dims, slots, grads, dks, dvs):
    nz, nx, ny, nc = dims
    rows, width = grads.shape[1:]
    half = width // 2
    spans_dev = slots // SPAN
    spans_all, seqs, _ = dks.shape
    seqn = ny * nc
    most = max(nx, ny)
    copies = (nc - 1) + 2 * (nx - 1) + 2 * (ny - 1) + (nz - 1) + (seqn - 1)
    vm = pl.BlockSpec(memory_space=pltpu.VMEM)
    return pl.pallas_call(
        partial(scatter_kernel, dims, spans_dev),
        in_specs=[vm] * 3,
        out_specs=[vm] * 3,
        out_shape=[sds((rows, width), f32)] + [sds((spans_dev, seqs, dks.shape[2]), bf)] * 2,
        scratch_shapes=[
            pltpu.VMEM((nc - 1, nz, nx, ny, rows, width), bf),
            pltpu.VMEM((nz, nx, ny, rows, width), bf),
            pltpu.VMEM((nx - 1, nz, ny, rows, half), bf),
            pltpu.VMEM((ny - 1, nz, nx, rows, half), bf),
            pltpu.VMEM((2, nz, most, rows, half), bf),
            pltpu.VMEM((ny - 1, nz, rows, half), bf),
            pltpu.VMEM((nx - 1, nz, rows, half), bf),
            pltpu.VMEM((nz, rows, width), bf),
            pltpu.VMEM((nz - 1, rows, width), bf),
            pltpu.VMEM((2, spans_all, seqs, dks.shape[2]), bf),
            pltpu.VMEM((seqn - 1, 2, spans_dev, seqs, dks.shape[2]), bf),
            pltpu.SemaphoreType.DMA((copies,)),
            pltpu.SemaphoreType.DMA((copies,)),
        ],
        compiler_params=pltpu.CompilerParams(
            vmem_limit_bytes=VMEM_LIMIT, collective_id=1, has_side_effects=True
        ),
    )(grads.reshape(dims + (rows, width)), dks, dvs)


def attend_forward_kernel(slots, x_ref, mean_ref, wq_ref, wk_ref, wv_ref, ga_ref,
                          q_ref, k_ref, v_ref, att_ref, lse_ref, ks_ref, vs_ref, tmp_ref):
    T, D = x_ref.shape
    spans_all, seqs, _ = mean_ref.shape
    i = pl.program_id(0)
    spt, nseq = slots // SPAN, T // slots
    ga = ga_ref[...]

    @pl.when(i == 0)
    def _():
        mb = (mean_ref[...].reshape(spans_all * seqs, D) * ga).astype(bf)
        for w_ref, out in ((wk_ref, ks_ref), (wv_ref, vs_ref)):
            sums = dot(mb, w_ref[...])
            tmp_ref[...] = jnp.zeros_like(tmp_ref)
            for t in range(spans_all):
                tmp_ref[:, t, :] = sums[t * seqs : (t + 1) * seqs]
            out[...] = tmp_ref[...].astype(bf)

    x = x_ref[...].astype(f32)
    r = lax.rsqrt(jnp.mean(x * x, axis=1, keepdims=True) + EPS)
    xn = (x * r * ga).astype(bf)
    q_ref[...] = (dot(xn, wq_ref[...]).astype(bf) * (HD**-0.5)).astype(bf)
    k_ref[...] = dot(xn, wk_ref[...]).astype(bf)
    v_ref[...] = dot(xn, wv_ref[...]).astype(bf)
    causal = causal_mask()
    t_row = lax.broadcasted_iota(jnp.int32, (FARP, 2 * SPAN), 0)
    first = lax.axis_index("seq") * spt
    for s in range(T // SPAN):
        seq = i * nseq + s // spt
        far = t_row < (first + s % spt)
        rows = slice(s * SPAN, (s + 1) * SPAN)
        for p in range(D // 128):
            ln = slice(p * 128, (p + 1) * 128)
            ke = jnp.concatenate([k_ref[rows, ln], ks_ref[seq, :, ln]], axis=0)
            ve = jnp.concatenate([v_ref[rows, ln], vs_ref[seq, :, ln]], axis=0)
            sc = dot(ke, pair_diag(q_ref[rows, ln]), 1, 1)
            sn = jnp.where(causal, sc[:SPAN], -1e30)
            sf = jnp.where(far, sc[SPAN:], -1e30)
            m = jnp.maximum(jnp.max(sn, axis=0, keepdims=True), jnp.max(sf, axis=0, keepdims=True))
            en = jnp.exp(sn - m)
            ef = jnp.exp(sf - m)
            l = jnp.sum(en, axis=0, keepdims=True) + jnp.sum(ef, axis=0, keepdims=True)
            rl = 1.0 / l
            pb = jnp.concatenate([(en * rl).astype(bf), (ef * rl).astype(bf)], axis=0)
            at = dot(ve, pb, 0, 0)
            att_ref[rows, ln] = jnp.concatenate([at[:HD, :SPAN], at[HD:, SPAN:]], axis=0).astype(bf).T
            total = m + jnp.log(l)
            lse_ref[2 * p : 2 * p + 1, rows] = total[:, :SPAN]
            lse_ref[2 * p + 1 : 2 * p + 2, rows] = total[:, SPAN:]


def attend_forward_call(slots, block, x, mean, wq, wk, wv, ga):
    n_tok, D = x.shape
    seqs = n_tok // slots
    tok = pl.BlockSpec((block, D), lambda i: (i, 0))
    summ = (seqs, FARP, D)
    return pl.pallas_call(
        partial(attend_forward_kernel, slots),
        grid=(n_tok // block,),
        in_specs=[tok, full(mean.shape), full((D, D)), full((D, D)), full((D, D)), full((1, D))],
        out_specs=[tok] * 4 + [pl.BlockSpec((H, block), lambda i: (0, i)), full(summ), full(summ)],
        out_shape=[sds((n_tok, D), bf)] * 4 + [sds((H, n_tok), f32), sds(summ, bf), sds(summ, bf)],
        scratch_shapes=[pltpu.VMEM(summ, f32)],
        compiler_params=pltpu.CompilerParams(
            vmem_limit_bytes=VMEM_LIMIT, dimension_semantics=("arbitrary",)
        ),
    )(x, mean, wq, wk, wv, ga)


def mlp_kernel(chunk, slots, ndev, len_ref, x_ref, att_ref, cot_ref, wo_ref, wu_ref, wd_ref, gm_ref,
               out_ref, datt_ref, dmid_ref, gsum_ref, adown, aup, aout, agm):
    T, D = x_ref.shape
    FF = wu_ref.shape[1]
    i, n = pl.program_id(0), pl.num_programs(0)

    @pl.when(i == 0)
    def _():
        for acc in (adown, aup, aout, agm):
            acc[...] = jnp.zeros_like(acc)

    att = att_ref[...]
    mid = x_ref[...].astype(f32) + dot(att, wo_ref[...])
    r = lax.rsqrt(jnp.mean(mid * mid, axis=1, keepdims=True) + EPS)
    gm = gm_ref[...]
    hn = (mid * r * gm).astype(bf)
    nseq = T // slots
    row = lax.broadcasted_iota(jnp.int32, (slots, 1), 0) + lax.axis_index("seq") * slots
    valid = jnp.concatenate(
        [jnp.where(row < len_ref[i * nseq + s], 1.0, 0.0) for s in range(nseq)], axis=0
    )
    g = cot_ref[...].astype(f32) * valid
    gb = g.astype(bf)
    gbt = gb.T
    hnt = hn.T
    y = jnp.zeros((T, D), f32)
    dhn = jnp.zeros((T, D), f32)
    for j in range(FF // chunk):
        sl = slice(j * chunk, (j + 1) * chunk)
        u = dot(hn, wu_ref[:, sl])
        u2 = u * u
        h = 0.5 + 0.5 * jnp.tanh(u * (K0 + (K0 * K1) * u2))
        act = (u * h).astype(bf)
        da = dot(gb, wd_ref[sl, :], 1, 1)
        slope = h + (u * (K0 + (3 * K0 * K1) * u2)) * ((h + h) * (1.0 - h))
        du = (da * slope).astype(bf)
        y = y + dot(act, wd_ref[sl, :])
        dhn = dhn + dot(du, wu_ref[:, sl], 1, 1)
        adown[:, sl] += dot(gbt, act)
        aup[:, sl] += dot(hnt, du)
    out_ref[...] = ((mid + y) * valid).astype(bf)
    mr = mid * r
    dm = dhn * mr
    agm[...] += jnp.sum(dm.reshape(T // 8, 8, D), axis=0)
    coef = jnp.mean(dm * gm, axis=1, keepdims=True)
    db = (g + r * (dhn * gm - mr * coef)).astype(bf)
    dmid_ref[...] = db
    aout[...] += dot(att, db, 0, 0)
    datt_ref[...] = dot(db, wo_ref[...], 1, 1).astype(bf)

    @pl.when(i == n - 1)
    def _():
        rd, rf = D // ndev, FF // ndev
        gsum_ref[:, :rd, :] = aout[...].reshape(ndev, rd, D).astype(bf)
        for j in range(FF // D):
            gsum_ref[:, rd * (j + 1) : rd * (j + 2), :] = (
                aup[:, j * D : (j + 1) * D].reshape(ndev, rd, D).astype(bf)
            )
            part = adown[:, j * D : (j + 1) * D].T.astype(bf)
            nd = D // rf
            gsum_ref[j * nd : (j + 1) * nd, rd * (FF // D + 1) : rd * (FF // D + 1) + rf, :] = part.reshape(
                nd, rf, D
            )
        gsum_ref[:, rd * (FF // D + 1) + rf :, :] = spread_gain(agm[...], ndev, rd).astype(bf)


def spread_gain(parts, ndev, rd):
    D = parts.shape[1]
    total = jnp.sum(parts, axis=0, keepdims=True)
    d = lax.broadcasted_iota(jnp.int32, (ndev, 16, D), 0)
    s = lax.broadcasted_iota(jnp.int32, (ndev, 16, D), 1)
    l = lax.broadcasted_iota(jnp.int32, (ndev, 16, D), 2)
    return jnp.where((s == 0) & (l // rd == d), total.reshape(1, 1, D), 0.0)


def mlp_call(chunk, slots, block, ndev, lens, x, att, cot, wo, wu, wd, gm):
    n_tok, D = x.shape
    FF = wu.shape[1]
    tok = pl.BlockSpec((block, D), lambda i: (i, 0))
    rows = D // ndev * (FF // D + 1) + FF // ndev + 16
    return pl.pallas_call(
        partial(mlp_kernel, chunk, slots, ndev),
        grid=(n_tok // block,),
        in_specs=[pl.BlockSpec(memory_space=pltpu.SMEM), tok, tok, tok]
        + [full((D, D)), full((D, FF)), full((FF, D)), full((1, D))],
        out_specs=[tok, tok, tok, full((ndev, rows, D))],
        out_shape=[sds((n_tok, D), bf)] * 3 + [sds((ndev, rows, D), bf)],
        scratch_shapes=[pltpu.VMEM((D, FF), f32), pltpu.VMEM((D, FF), f32), pltpu.VMEM((D, D), f32),
                        pltpu.VMEM((8, D), f32)],
        compiler_params=pltpu.CompilerParams(
            vmem_limit_bytes=VMEM_LIMIT, dimension_semantics=("arbitrary",)
        ),
    )(lens, x, att, cot, wo, wu, wd, gm)


def attend_backward_kernel(slots, ndev, x_ref, q_ref, k_ref, v_ref, da_ref, lse_ref, mean_ref, ks_ref, vs_ref,
                           wq_ref, wk_ref, wv_ref, ga_ref, dxn_ref, gsum_ref, dks_ref, dvs_ref, aq, ak, av, aga):
    T, D = x_ref.shape
    spans_all, seqs, _ = mean_ref.shape
    i, n = pl.program_id(0), pl.num_programs(0)
    ga = ga_ref[...]

    @pl.when(i == 0)
    def _():
        for acc in (aq, ak, av, aga):
            acc[...] = jnp.zeros_like(acc)

    x = x_ref[...].astype(f32)
    r = lax.rsqrt(jnp.mean(x * x, axis=1, keepdims=True) + EPS)
    xr = x * r
    xn = (xr * ga).astype(bf)
    causal = causal_mask()
    spt, nseq = slots // SPAN, T // slots
    t_row = lax.broadcasted_iota(jnp.int32, (FARP, 2 * SPAN), 0)
    first = lax.axis_index("seq") * spt
    dqs, dks, dvs = [], [], []
    for s in range(T // SPAN):
        seq = i * nseq + s // spt
        far = t_row < (first + s % spt)
        rows = slice(s * SPAN, (s + 1) * SPAN)
        dq_p, dk_p, dv_p, fk, fv = [], [], [], [], []
        for p in range(D // 128):
            ln = slice(p * 128, (p + 1) * 128)
            qbd = pair_diag(q_ref[rows, ln])
            dbd = pair_diag(da_ref[rows, ln])
            ke = jnp.concatenate([k_ref[rows, ln], ks_ref[seq, :, ln]], axis=0)
            ve = jnp.concatenate([v_ref[rows, ln], vs_ref[seq, :, ln]], axis=0)
            sc = dot(ke, qbd, 1, 1)
            dp = dot(ve, dbd, 1, 1)
            lse = jnp.concatenate([lse_ref[2 * p : 2 * p + 1, rows], lse_ref[2 * p + 1 : 2 * p + 2, rows]], axis=1)
            pn = jnp.where(causal, jnp.exp(sc[:SPAN] - lse), 0.0)
            pf = jnp.where(far, jnp.exp(sc[SPAN:] - lse), 0.0)
            dpn, dpf = dp[:SPAN], dp[SPAN:]
            delta = jnp.sum(pn * dpn, axis=0, keepdims=True) + jnp.sum(pf * dpf, axis=0, keepdims=True)
            ds = jnp.concatenate([(pn * (dpn - delta)).astype(bf), (pf * (dpf - delta)).astype(bf)], axis=0)
            pb = jnp.concatenate([pn.astype(bf), pf.astype(bf)], axis=0)
            dv = dot(pb, dbd)
            dk = dot(ds, qbd)
            dq = dot(ke, ds, 0, 0)
            dq = jnp.concatenate([dq[:HD, :SPAN], dq[HD:, SPAN:]], axis=0) * (HD**-0.5)
            dq_p.append(dq.astype(bf).T)
            dk_p.append(dk[:SPAN].astype(bf))
            dv_p.append(dv[:SPAN].astype(bf))
            fk.append(dk[SPAN : SPAN + spans_all])
            fv.append(dv[SPAN : SPAN + spans_all])
        dqs.append(jnp.concatenate(dq_p, axis=1))
        dks.append(jnp.concatenate(dk_p, axis=1))
        dvs.append(jnp.concatenate(dv_p, axis=1))
        fk, fv = jnp.concatenate(fk, axis=1), jnp.concatenate(fv, axis=1)
        if s % spt == 0:
            sum_k, sum_v = fk, fv
        else:
            sum_k, sum_v = sum_k + fk, sum_v + fv
        if s % spt == spt - 1:
            for t in range(spans_all):
                dks_ref[t, pl.ds(seq, 1), :] = sum_k[t : t + 1]
                dvs_ref[t, pl.ds(seq, 1), :] = sum_v[t : t + 1]
    dq, dk, dv = (jnp.concatenate(parts, axis=0) for parts in (dqs, dks, dvs))
    xt = xn.T
    aq[...] += dot(xt, dq)
    ak[...] += dot(xt, dk)
    av[...] += dot(xt, dv)
    dxn = dot(dq, wq_ref[...], 1, 1) + dot(dk, wk_ref[...], 1, 1) + dot(dv, wv_ref[...], 1, 1)
    dxn_ref[...] = dxn.astype(bf)
    aga[...] += jnp.sum((dxn * xr).reshape(T // 8, 8, D), axis=0)

    @pl.when(i == n - 1)
    def _():
        rd = D // ndev
        mean = mean_ref[...].reshape(spans_all * seqs, D)
        mb = (mean * ga).astype(bf)
        fk = dks_ref[...].reshape(spans_all * seqs, D).astype(bf)
        fv = dvs_ref[...].reshape(spans_all * seqs, D).astype(bf)
        far = dot(fk, wk_ref[...], 1, 1) + dot(fv, wv_ref[...], 1, 1)
        gain = aga[...] + jnp.sum((far * mean).reshape(spans_all * seqs // 8, 8, D), axis=0)
        gsum_ref[:, :rd, :] = aq[...].reshape(ndev, rd, D).astype(bf)
        gsum_ref[:, rd : 2 * rd, :] = (ak[...] + dot(mb, fk, 0, 0)).reshape(ndev, rd, D).astype(bf)
        gsum_ref[:, 2 * rd : 3 * rd, :] = (av[...] + dot(mb, fv, 0, 0)).reshape(ndev, rd, D).astype(bf)
        gsum_ref[:, 3 * rd :, :] = spread_gain(gain, ndev, rd).astype(bf)


def attend_backward_call(slots, block, ndev, x, q, k, v, da, lse, mean, ks, vs, wq, wk, wv, ga):
    n_tok, D = x.shape
    tok = pl.BlockSpec((block, D), lambda i: (i, 0))
    rows = D // ndev * 3 + 16
    return pl.pallas_call(
        partial(attend_backward_kernel, slots, ndev),
        grid=(n_tok // block,),
        in_specs=[tok] * 5
        + [pl.BlockSpec((H, block), lambda i: (0, i)), full(mean.shape), full(ks.shape), full(vs.shape)]
        + [full((D, D))] * 3
        + [full((1, D))],
        out_specs=[tok, full((ndev, rows, D)), full(mean.shape), full(mean.shape)],
        out_shape=[sds((n_tok, D), bf), sds((ndev, rows, D), bf), sds(mean.shape, f32), sds(mean.shape, f32)],
        scratch_shapes=[pltpu.VMEM((D, D), f32)] * 3 + [pltpu.VMEM((8, D), f32)],
        compiler_params=pltpu.CompilerParams(
            vmem_limit_bytes=VMEM_LIMIT, dimension_semantics=("arbitrary",)
        ),
    )(x, q, k, v, da, lse, mean, ks, vs, wq, wk, wv, ga)


def grad_input_kernel(slots, x_ref, dxn_ref, dmid_ref, own_k_ref, own_v_ref, wk_ref, wv_ref, ga_ref, out_ref, far_ref):
    T, D = x_ref.shape
    spt, seqs, _ = own_k_ref.shape
    i = pl.program_id(0)
    nseq = T // slots

    @pl.when(i == 0)
    def _():
        fk = own_k_ref[...].reshape(spt * seqs, D)
        fv = own_v_ref[...].reshape(spt * seqs, D)
        far = (dot(fk, wk_ref[...], 1, 1) + dot(fv, wv_ref[...], 1, 1)) * (1.0 / SPAN)
        far_ref[...] = far.reshape(spt, seqs, D)

    ga = ga_ref[...]
    x = x_ref[...].astype(f32)
    r = lax.rsqrt(jnp.mean(x * x, axis=1, keepdims=True) + EPS)
    xr = x * r
    dxn = dxn_ref[...].astype(f32)
    parts = []
    for s in range(T // SPAN):
        far = far_ref[s % spt, pl.ds(i * nseq + s // spt, 1), :]
        parts.append(dxn[s * SPAN : (s + 1) * SPAN] + far)
    gd = jnp.concatenate(parts, axis=0) * ga
    coef = jnp.mean(gd * xr, axis=1, keepdims=True)
    out_ref[...] = dmid_ref[...].astype(f32) + r * (gd - xr * coef)


def grad_input_call(slots, block, x, dxn, dmid, own_k, own_v, wk, wv, ga):
    n_tok, D = x.shape
    tok = pl.BlockSpec((block, D), lambda i: (i, 0))
    return pl.pallas_call(
        partial(grad_input_kernel, slots),
        grid=(n_tok // block,),
        in_specs=[tok] * 3 + [full(own_k.shape)] * 2 + [full((D, D))] * 2 + [full((1, D))],
        out_specs=tok,
        out_shape=sds((n_tok, D), f32),
        scratch_shapes=[pltpu.VMEM(own_k.shape, f32)],
        compiler_params=pltpu.CompilerParams(
            vmem_limit_bytes=VMEM_LIMIT, dimension_semantics=("arbitrary",)
        ),
    )(x, dxn, dmid, own_k, own_v, wk, wv, ga)


def gains_kernel(rows, ndev, tiles_ref, ga_ref, gm_ref):
    tiles = tiles_ref[:, :128]
    ga_ref[...] = gain_row(tiles, 0, ndev, rows)
    gm_ref[...] = gain_row(tiles, 1, ndev, rows)


def body(dims, inputs, lengths, cotangent, w_query, w_key, w_value, w_out, w_up, w_down, gain_attn, gain_mlp):
    seqs, slots, D = inputs.shape
    nz, nx, ny, nc = dims
    ndev = nz * nx * ny * nc
    FF = w_up.shape[1]
    rd, rf = w_query.shape[0], w_down.shape[0]
    n_tok = seqs * slots
    block = 512
    x = inputs.reshape(n_tok, D)
    cot = cotangent.reshape(n_tok, D)
    weights = (w_query, w_key, w_value, w_out, w_up, w_down)
    gains = jnp.zeros((8, 256), f32)
    gains = gains.at[0, :rd].set(gain_attn.astype(f32)).at[1, :rd].set(gain_mlp.astype(f32))
    everyone = ("dp", "seq")
    near = rd % 16 == 0
    if near:
        *wholes, tiles, mean = gather_call(dims, slots, block, x, weights + (gains,))
    else:
        *wholes, tiles, mean = gather_call(dims, slots, block, x, (gains,))
        wholes = [lax.all_gather(w, everyone, axis=0, tiled=True) for w in weights]
    wq, wk, wv, wo, wu, wd = (w.reshape(-1, w.shape[-1]) for w in wholes)
    ga, gm = pl.pallas_call(
        partial(gains_kernel, rd, ndev), out_shape=[sds((1, D), f32)] * 2
    )(tiles.reshape(ndev * 8, 256))
    q, k, v, att, lse, ks, vs = attend_forward_call(slots, block, x, mean, wq, wk, wv, ga)
    pack = ndev if near else 32
    output, datt, dmid, sums_m = mlp_call(512, slots, block, pack, lengths, x, att, cot, wo, wu, wd, gm)
    dxn, sums_a, dks, dvs = attend_backward_call(slots, block, pack, x, q, k, v, datt, lse, mean, ks, vs, wq, wk, wv, ga)
    device = lax.axis_index("dp") * (ny * nc) + lax.axis_index("seq")
    if near:
        sums, own_k, own_v = scatter_call(dims, slots, jnp.concatenate([sums_m, sums_a], axis=1), dks, dvs)
        last = rd * (FF // D + 1) + rf
        g_out = sums[:rd]
        g_up = jnp.concatenate([sums[rd * (j + 1) : rd * (j + 2)] for j in range(FF // D)], axis=1)
        g_down = sums[rd * (FF // D + 1) : last]
        g_gm = lax.dynamic_slice(sums[last], (device * rd,), (rd,))
        rest = sums[last + 16 :]
        g_q, g_k, g_v = rest[:rd], rest[rd : 2 * rd], rest[2 * rd : 3 * rd]
        g_ga = lax.dynamic_slice(rest[3 * rd], (device * rd,), (rd,))
    else:
        pd, pf = D // pack, FF // pack
        last = pd * (FF // D + 1) + pf

        def scattered(a):
            return lax.psum_scatter(a.astype(f32), everyone, scatter_dimension=0, tiled=True)

        g_out = scattered(sums_m[:, :pd].reshape(D, D))
        g_up = scattered(
            jnp.concatenate([sums_m[:, pd * (j + 1) : pd * (j + 2)].reshape(D, D) for j in range(FF // D)], axis=1)
        )
        g_down = scattered(sums_m[:, pd * (FF // D + 1) : last].reshape(FF, D))
        g_gm = scattered(jnp.sum(sums_m[:, last].astype(f32), axis=0))
        g_q, g_k, g_v = (scattered(sums_a[:, j * pd : (j + 1) * pd].reshape(D, D)) for j in range(3))
        g_ga = scattered(jnp.sum(sums_a[:, 3 * pd].astype(f32), axis=0))
        own_k, own_v = (
            lax.psum_scatter(d.astype(bf), "seq", scatter_dimension=0, tiled=True) for d in (dks, dvs)
        )
    grad_input = grad_input_call(slots, block, x, dxn, dmid, own_k, own_v, wk, wv, ga)
    return (
        output.reshape(inputs.shape), grad_input.reshape(inputs.shape),
        g_q, g_k, g_v, g_out, g_up, g_down, g_ga, g_gm,
    )


def solution(mesh):
    dp, seq = mesh.shape["dp"], mesh.shape["seq"]
    nx = max(d for d in range(1, dp + 1) if dp % d == 0 and d * d <= dp)
    nc = 2 if seq % 2 == 0 else 1
    dims = (dp // nx, nx, seq // nc, nc)
    rows, vec = P(("dp", "seq"), None), P(("dp", "seq"))
    tokens = P("dp", "seq", None)
    return jax.shard_map(
        partial(body, dims),
        mesh=mesh,
        in_specs=(tokens, P("dp"), tokens) + (rows,) * 6 + (vec,) * 2,
        out_specs=(tokens, tokens) + (rows,) * 6 + (vec,) * 2,
        check_vma=False,
    )
```

```python
from functools import partial

import jax
import jax.numpy as jnp
from jax import lax
from jax.experimental import pallas as pl
from jax.experimental.pallas import tpu as pltpu
from jax.sharding import PartitionSpec as P

H = 8
HD = 64
SPAN = 128
EPS = 1e-06
K0 = 0.7978845608028654
K1 = 0.044715
FARP = 16
f32 = jnp.float32
bf = jnp.bfloat16
MESH = pl.DeviceIdType.MESH
VMEM_LIMIT = 62 << 20


def dot(a, b, ca=1, cb=0):
    return lax.dot_general(a, b, (((ca,), (cb,)), ((), ())), preferred_element_type=f32)


def sds(shape, dtype):
    return jax.ShapeDtypeStruct(shape, dtype)


def full(shape):
    return pl.BlockSpec(shape, lambda i: (0,) * len(shape), pipeline_mode=pl.Buffered(1))


def pair_diag(a):
    lane = lax.broadcasted_iota(jnp.int32, a.shape, 1)
    zero = jnp.zeros_like(a)
    return jnp.concatenate([jnp.where(lane < HD, a, zero), jnp.where(lane >= HD, a, zero)], axis=0)


def causal_mask():
    j = lax.broadcasted_iota(jnp.int32, (SPAN, 2 * SPAN), 0)
    i = lax.broadcasted_iota(jnp.int32, (SPAN, 2 * SPAN), 1)
    return j <= jnp.where(i >= SPAN, i - SPAN, i)


def gain_row(tiles, which, ndev, rows):
    width = ndev * rows
    r = lax.broadcasted_iota(jnp.int32, (ndev * 8, 128), 0)
    l = lax.broadcasted_iota(jnp.int32, (ndev * 8, 128), 1)
    keep = jnp.where((r % 8 == which) & (l < rows), tiles, 0.0).astype(bf)
    a = lax.broadcasted_iota(jnp.int32, (128, width), 0)
    b = lax.broadcasted_iota(jnp.int32, (128, width), 1)
    spread = dot(keep, jnp.where(b % rows == a, 1.0, 0.0).astype(bf))
    d = lax.broadcasted_iota(jnp.int32, (ndev * 8, width), 0)
    c = lax.broadcasted_iota(jnp.int32, (ndev * 8, width), 1)
    return jnp.sum(jnp.where(d // 8 == c // rows, spread, 0.0), axis=0, keepdims=True)


class Place:
    def __init__(self, dims):
        self.nz, self.nx, self.ny, self.nc = dims
        dp, seq = lax.axis_index("dp"), lax.axis_index("seq")
        self.z, self.x = dp // self.nx, dp % self.nx
        self.y, self.c = seq // self.nc, seq % self.nc

    def at(self, z=None, x=None, y=None, c=None):
        z = self.z if z is None else z
        x = self.x if x is None else x
        y = self.y if y is None else y
        c = self.c if c is None else c
        return (z * self.nx + x, y * self.nc + c)

    def line(self, axis):
        return getattr(self, axis), getattr(self, "n" + axis)

    def partners(self, axis):
        me, n = self.line(axis)
        return [(o, (me + o) % n, (me + n - o) % n) for o in range(1, n)]

    def greet(self, others):
        barrier = pltpu.get_barrier_semaphore()
        for other in others:
            pl.semaphore_signal(barrier, inc=1, device_id=other, device_id_type=MESH)
        pl.semaphore_wait(barrier, len(others))

    def others(self):
        return [self.at(**{a: to}) for a in ("z", "x", "y", "c") for _, to, _ in self.partners(a)]


class Copies:
    def __init__(self, send_sem, recv_sem):
        self.send_sem, self.recv_sem, self.used = send_sem, recv_sem, 0

    def make(self, src, dst, landed, device):
        k = self.used
        self.used += 1
        out = pltpu.make_async_remote_copy(
            src_ref=src, dst_ref=dst, send_sem=self.send_sem.at[k], recv_sem=self.recv_sem.at[k],
            device_id=device, device_id_type=MESH,
        )
        into = pltpu.make_async_remote_copy(
            src_ref=src, dst_ref=landed, send_sem=self.send_sem.at[k], recv_sem=self.recv_sem.at[k],
            device_id=device, device_id_type=MESH,
        )
        return out, into


def start(copies):
    for out, _ in copies:
        out.start()


def finish(copies):
    for out, into in copies:
        out.wait_send()
        into.wait_recv()


def halves(ref):
    n = ref.shape[-1] // 2
    return pl.ds(0, n), pl.ds(n, n)


def gather_phases(pc, cp, pieces, wholes):
    z, x, y, c = pc.z, pc.x, pc.y, pc.c
    first, second, third, last = [], [], [], []
    for piece, whole in zip(pieces, wholes):
        for _, to, fr in pc.partners("z"):
            first.append(cp.make(piece, whole.at[z, x, y, c], whole.at[fr, x, y, c], pc.at(z=to)))
    for whole in wholes:
        a, b = halves(whole)
        for _, to, fr in pc.partners("x"):
            v = whole.at[:, x, y, c, :, a]
            second.append(cp.make(v, v, whole.at[:, fr, y, c, :, a], pc.at(x=to)))
        for _, to, fr in pc.partners("y"):
            v = whole.at[:, x, y, c, :, b]
            second.append(cp.make(v, v, whole.at[:, x, fr, c, :, b], pc.at(y=to)))
    for whole in wholes:
        a, b = halves(whole)
        for _, to, fr in pc.partners("y"):
            v = whole.at[:, :, y, c, :, a]
            third.append(cp.make(v, v, whole.at[:, :, fr, c, :, a], pc.at(y=to)))
        for _, to, fr in pc.partners("x"):
            v = whole.at[:, x, :, c, :, b]
            third.append(cp.make(v, v, whole.at[:, fr, :, c, :, b], pc.at(x=to)))
    for whole in wholes:
        for _, to, fr in pc.partners("c"):
            v = whole.at[:, :, :, c]
            last.append(cp.make(v, v, whole.at[:, :, :, fr], pc.at(c=to)))
    return first, second, third, last


def front_kernel(dims, slots, n_first, n_later, *refs):
    near = n_first > 0
    refs = list(refs)

    def take(n):
        out = refs[:n]
        del refs[:n]
        return out

    (x_ref,) = take(1)
    pieces = take(n_first + n_later + 1 if near else 1)
    w_in = [] if near else take(3)
    q_ref, k_ref, v_ref, att_ref, lse_ref, ks_ref, vs_ref, mean_ref, ga_ref, gm_ref = take(10)
    first_out = take(n_first)
    later = take(n_later)
    w_refs = take(3) if near else w_in
    tiles_ref, own_mean, all_mean, tmp_ref, local_sem, send_sem, recv_sem = take(7)
    T, D = x_ref.shape
    spt, nseq = slots // SPAN, T // slots
    pc = Place(dims)
    cp = Copies(send_sem, recv_sem)
    seq, dp = lax.axis_index("seq"), lax.axis_index("dp")
    seqn = pc.ny * pc.nc
    spans_all, seqs = spt * seqn, all_mean.shape[1]
    ndev = pc.nz * pc.nx * seqn
    rd = D // ndev
    chunks = []
    own = []
    if near:
        wholes = w_refs + [tiles_ref]
        firsts = pieces[:n_first] + pieces[-1:]
        groups = [(firsts, wholes)] + [([p], [w]) for p, w in zip(pieces[n_first:-1], later)]
    else:
        groups = [(pieces, [tiles_ref])]
    for sources, targets in groups:
        chunks.append(gather_phases(pc, cp, sources, targets))
        mine = []
        for source, target in zip(sources, targets):
            mine.append(
                pltpu.make_async_copy(
                    source, target.at[pc.z, pc.x, pc.y, pc.c], local_sem.at[sum(map(len, own)) + len(mine)]
                )
            )
        own.append(mine)
    means = []
    for o in range(1, seqn):
        to, fr = (seq + o) % seqn, (seq + seqn - o) % seqn
        v = all_mean.at[pl.ds(seq * spt, spt)]
        means.append(cp.make(v, v, all_mean.at[pl.ds(fr * spt, spt)], (dp, to)))
    i, n = pl.program_id(0), pl.num_programs(0) // 2

    @pl.when(i == 0)
    def _():
        seq_peers = [(dp, (seq + o) % seqn) for o in range(1, seqn)]
        zx = [pc.at(**{a: to}) for a in ("z", "x") for _, to, _ in pc.partners(a)]
        pc.greet(zx + seq_peers)
        start(chunks[0][0])
        for mine in own:
            for copy in mine:
                copy.start()

    x = x_ref[...].astype(f32)
    r = lax.rsqrt(jnp.mean(x * x, axis=1, keepdims=True) + EPS)
    xr = x * r

    @pl.when(i < n)
    def _():
        for s in range(T // SPAN):
            row = jnp.sum(xr[s * SPAN : (s + 1) * SPAN], axis=0, keepdims=True) * (1.0 / SPAN)
            own_mean[s % spt, pl.ds(i * nseq + s // spt, 1), :] = row

    @pl.when(i == n - 1)
    def _():
        for mine in own:
            for copy in mine:
                copy.wait()
        c0 = chunks[0]
        finish(c0[0])
        start(c0[1])
        all_mean[pl.ds(seq * spt, spt)] = own_mean[...].astype(bf)
        start(means)
        if near:
            start(chunks[1][0])
        finish(c0[1])
        start(c0[2])
        finish(means)
        mean_ref[...] = all_mean[...]
        finish(c0[2])
        start(c0[3])
        finish(c0[3])
        for w_ref, out in zip(w_refs, first_out):
            out[...] = w_ref[...]
        tiles = tiles_ref[...].reshape(ndev * 8, tiles_ref.shape[-1])[:, :128]
        ga_ref[...] = gain_row(tiles, 0, ndev, rd)
        gm_ref[...] = gain_row(tiles, 1, ndev, rd)
        mb = (all_mean[...].astype(f32).reshape(spans_all * seqs, D) * ga_ref[...]).astype(bf)
        for w_ref, out in ((w_refs[1], ks_ref), (w_refs[2], vs_ref)):
            sums = dot(mb, w_ref[...].reshape(D, D))
            tmp_ref[...] = jnp.zeros_like(tmp_ref)
            for t in range(spans_all):
                tmp_ref[:, t, :] = sums[t * seqs : (t + 1) * seqs]
            out[...] = tmp_ref[...].astype(bf)

    if near:
        up, down, last = chunks[1], chunks[2], chunks[3]
        plan = [
            (0, [up[0]], [up[1], down[0], last[0]]),
            (2, [up[1]], [up[2]]),
            (4, [up[2], down[0], last[0]], [up[3], down[1]]),
            (6, [up[3], down[1]], [down[2]]),
            (8, [down[2]], [down[3], last[1]]),
            (9, [last[1]], [last[2]]),
            (10, [last[2]], [last[3]]),
        ]
        for at, ends, begins in plan:

            @pl.when(i == n + at)
            def _(ends=ends, begins=begins):
                for c in ends:
                    finish(c)
                for c in begins:
                    start(c)

    @pl.when(i >= n)
    def _():
        j = i - n
        xn = (xr * ga_ref[...]).astype(bf)
        q_ref[...] = (dot(xn, w_refs[0][...].reshape(D, D)).astype(bf) * (HD**-0.5)).astype(bf)
        k_ref[...] = dot(xn, w_refs[1][...].reshape(D, D)).astype(bf)
        v_ref[...] = dot(xn, w_refs[2][...].reshape(D, D)).astype(bf)
        attend_forward(slots, j, seq, q_ref, k_ref, v_ref, ks_ref, vs_ref, att_ref, lse_ref)

    if near:

        @pl.when(i == 2 * n - 1)
        def _():
            finish(chunks[2][3])
            finish(chunks[3][3])


def attend_forward(slots, j, seq, q_ref, k_ref, v_ref, ks_ref, vs_ref, att_ref, lse_ref):
    T, D = q_ref.shape
    spt, nseq = slots // SPAN, T // slots
    causal = causal_mask()
    t_row = lax.broadcasted_iota(jnp.int32, (FARP, 2 * SPAN), 0)

    def where(u):
        s, p = u
        return slice(s * SPAN, (s + 1) * SPAN), slice(p * 128, (p + 1) * 128), j * nseq + s // spt

    def scores(u):
        rows, ln, sq = where(u)
        ke = jnp.concatenate([k_ref[rows, ln], ks_ref[sq, :, ln]], axis=0)
        return dot(ke, pair_diag(q_ref[rows, ln]), 1, 1)

    def weigh(u, sc):
        far = t_row < (seq * spt + u[0] % spt)
        sn = jnp.where(causal, sc[:SPAN], -1e30)
        sf = jnp.where(far, sc[SPAN:], -1e30)
        m = jnp.maximum(jnp.max(sn, axis=0, keepdims=True), jnp.max(sf, axis=0, keepdims=True))
        en = jnp.exp(sn - m)
        ef = jnp.exp(sf - m)
        l = jnp.sum(en, axis=0, keepdims=True) + jnp.sum(ef, axis=0, keepdims=True)
        return en.astype(bf), ef.astype(bf), m, l

    def combine(u, en, ef, m, l):
        rows, ln, sq = where(u)
        p = u[1]
        at = (dot(v_ref[rows, ln], en, 0, 0) + dot(vs_ref[sq, :, ln], ef, 0, 0)) * (1.0 / l)
        att_ref[rows, ln] = jnp.concatenate([at[:HD, :SPAN], at[HD:, SPAN:]], axis=0).astype(bf).T
        total = m + jnp.log(l)
        lse_ref[2 * p : 2 * p + 1, rows] = total[:, :SPAN]
        lse_ref[2 * p + 1 : 2 * p + 2, rows] = total[:, SPAN:]

    units = [(s, p) for s in range(T // SPAN) for p in range(D // 128)]
    staged(units, scores, weigh, combine)


def staged(units, first, second, third):
    a, b = {}, {}
    for t in range(len(units) + 2):
        if t < len(units):
            a[t] = first(units[t])
        if 0 <= t - 1 < len(units):
            b[t - 1] = second(units[t - 1], a.pop(t - 1))
        if 0 <= t - 2:
            third(units[t - 2], *b.pop(t - 2))


def front_call(dims, slots, block, x, w_first, w_later, gains, near):
    n_tok, D = x.shape
    seqs, spt = n_tok // slots, slots // SPAN
    nz, nx, ny, nc = dims
    n = n_tok // block
    spans_all = spt * ny * nc
    hbm = pl.BlockSpec(memory_space=pl.ANY)
    summ = (seqs, FARP, D)
    per_piece = (nz - 1) + 2 * (nx - 1) + 2 * (ny - 1) + (nc - 1)
    n_pieces = len(w_first) + len(w_later) + 1 if near else 1
    copies = n_pieces * per_piece + ny * nc - 1
    tok = pl.BlockSpec((block, D), lambda i: (jnp.maximum(i - n, 0), 0))
    args = [x] + (list(w_first) + list(w_later) if near else []) + [gains] + ([] if near else list(w_first))
    in_specs = [pl.BlockSpec((block, D), lambda i: (i % n, 0))] + [hbm] * n_pieces
    if not near:
        in_specs += [full(w.shape) for w in w_first]
    row = sds((1, D), f32)
    return pl.pallas_call(
        partial(front_kernel, dims, slots, len(w_first) if near else 0, len(w_later) if near else 0),
        grid=(2 * n,),
        in_specs=in_specs,
        out_specs=[tok] * 4
        + [pl.BlockSpec((H, block), lambda i: (0, jnp.maximum(i - n, 0))), full(summ), full(summ)]
        + [full((spans_all, seqs, D)), full((1, D)), full((1, D))]
        + ([full(dims + w.shape) for w in w_first] + [hbm] * len(w_later) if near else []),
        out_shape=[sds((n_tok, D), bf)] * 4
        + [sds((H, n_tok), f32), sds(summ, bf), sds(summ, bf), sds((spans_all, seqs, D), bf), row, row]
        + ([sds(dims + w.shape, w.dtype) for w in (*w_first, *w_later)] if near else []),
        scratch_shapes=([pltpu.VMEM(dims + w.shape, w.dtype) for w in w_first] if near else [])
        + [
            pltpu.VMEM(dims + gains.shape, f32),
            pltpu.VMEM((spt, seqs, D), f32),
            pltpu.VMEM((spans_all, seqs, D), bf),
            pltpu.VMEM(summ, f32),
            pltpu.SemaphoreType.DMA((n_pieces,)),
            pltpu.SemaphoreType.DMA((copies,)),
            pltpu.SemaphoreType.DMA((copies,)),
        ],
        compiler_params=pltpu.CompilerParams(
            vmem_limit_bytes=VMEM_LIMIT, collective_id=0, has_side_effects=True,
            dimension_semantics=("arbitrary",),
        ),
    )(*args)


def mlp_kernel(chunk, slots, ndev, len_ref, x_ref, att_ref, cot_ref, wo_ref, wu_ref, wd_ref, gm_ref,
               out_ref, datt_ref, dmid_ref, gsum_ref, adown, aup, aout):
    T, D = x_ref.shape
    FF = wu_ref.shape[1]
    i, n = pl.program_id(0), pl.num_programs(0)

    @pl.when(i == 0)
    def _():
        for acc in (adown, aup, aout):
            acc[...] = jnp.zeros_like(acc)

    att = att_ref[...]
    mid = x_ref[...].astype(f32) + dot(att, wo_ref[...])
    r = lax.rsqrt(jnp.mean(mid * mid, axis=1, keepdims=True) + EPS)
    gm = gm_ref[...]
    hn = (mid * r * gm).astype(bf)
    nseq = T // slots
    row = lax.broadcasted_iota(jnp.int32, (slots, 1), 0) + lax.axis_index("seq") * slots
    valid = jnp.concatenate(
        [jnp.where(row < len_ref[i * nseq + s], 1.0, 0.0) for s in range(nseq)], axis=0
    )
    g = cot_ref[...].astype(f32) * valid
    gb = g.astype(bf)
    gbt = gb.T
    hnt = hn.T
    y = jnp.zeros((T, D), f32)
    dhn = jnp.zeros((T, D), f32)
    cols = [slice(j * chunk, (j + 1) * chunk) for j in range(FF // chunk)]

    def products(sl):
        return dot(hn, wu_ref[:, sl]), dot(gb, wd_ref[sl, :], 1, 1)

    ready = products(cols[0])
    for j, sl in enumerate(cols):
        u, da = ready
        if j + 1 < len(cols):
            ready = products(cols[j + 1])
        h = 0.5 + 0.5 * jnp.tanh(u * (K0 + (K0 * K1) * (u * u)))
        act = (u * h).astype(bf)
        ub, hb = u.astype(bf), h.astype(bf)
        slope = hb + (ub * (bf(K0) + bf(3 * K0 * K1) * (ub * ub))) * ((hb + hb) * (bf(1.0) - hb))
        du = da.astype(bf) * slope
        y = y + dot(act, wd_ref[sl, :])
        dhn = dhn + dot(du, wu_ref[:, sl], 1, 1)
        adown[:, sl] += dot(gbt, act)
        aup[:, sl] += dot(hnt, du)
    out_ref[...] = ((mid + y) * valid).astype(bf)
    mr = mid * r
    gd = dhn * gm
    coef = jnp.mean(gd * mr, axis=1, keepdims=True)
    db = (g + r * (gd - mr * coef)).astype(bf)
    dmid_ref[...] = db
    aout[...] += dot(att, db, 0, 0)
    datt_ref[...] = dot(db, wo_ref[...], 1, 1).astype(bf)

    @pl.when(i == n - 1)
    def _():
        rd, rf = D // ndev, FF // ndev
        gsum_ref[:, :rd, :] = aout[...].reshape(ndev, rd, D).astype(bf)
        for j in range(FF // D):
            gsum_ref[:, rd * (j + 1) : rd * (j + 2), :] = (
                aup[:, j * D : (j + 1) * D].reshape(ndev, rd, D).astype(bf)
            )
            part = adown[:, j * D : (j + 1) * D].T.astype(bf)
            nd = D // rf
            gsum_ref[j * nd : (j + 1) * nd, rd * (FF // D + 1) : rd * (FF // D + 1) + rf, :] = part.reshape(
                nd, rf, D
            )


def mlp_call(chunk, slots, block, ndev, lens, x, att, cot, wo, wu, wd, gm):
    n_tok, D = x.shape
    FF = wu.shape[1]
    tok = pl.BlockSpec((block, D), lambda i: (i, 0))
    rows = D // ndev * (FF // D + 1) + FF // ndev
    return pl.pallas_call(
        partial(mlp_kernel, chunk, slots, ndev),
        grid=(n_tok // block,),
        in_specs=[pl.BlockSpec(memory_space=pltpu.SMEM), tok, tok, tok]
        + [full((D, D)), full((D, FF)), full((FF, D)), full((1, D))],
        out_specs=[tok, tok, tok, full((ndev, rows, D))],
        out_shape=[sds((n_tok, D), bf)] * 3 + [sds((ndev, rows, D), bf)],
        scratch_shapes=[pltpu.VMEM((D, FF), f32), pltpu.VMEM((D, FF), f32), pltpu.VMEM((D, D), f32)],
        compiler_params=pltpu.CompilerParams(
            vmem_limit_bytes=VMEM_LIMIT, dimension_semantics=("arbitrary",)
        ),
    )(lens, x, att, cot, wo, wu, wd, gm)


class Scatter:
    @staticmethod
    def scratch(dims, rows, width):
        nz, nx, ny, nc = dims
        half, most = width // 2, max(nx, ny)
        return [
            pltpu.VMEM((nc - 1, nz, nx, ny, rows, width), bf),
            pltpu.VMEM((nz, nx, ny, rows, width), bf),
            pltpu.VMEM((nx - 1, nz, ny, rows, half), bf),
            pltpu.VMEM((ny - 1, nz, nx, rows, half), bf),
            pltpu.VMEM((2, nz, most, rows, half), bf),
            pltpu.VMEM((ny - 1, nz, rows, half), bf),
            pltpu.VMEM((nx - 1, nz, rows, half), bf),
            pltpu.VMEM((nz, rows, width), bf),
            pltpu.VMEM((nz - 1, rows, width), bf),
        ]

    @staticmethod
    def copies(dims):
        nz, nx, ny, nc = dims
        return (nc - 1) + 2 * (nx - 1) + 2 * (ny - 1) + (nz - 1)

    def __init__(self, pc, cp, g, mine, out, scratch):
        self.pc, self.mine, self.out, self.bufs = pc, mine, out, scratch
        got1, held1, got2a, got2b, held2, got3a, got3b, held3, got4 = scratch
        a, b = halves(g)
        self.one = [
            cp.make(g.at[:, :, :, to], got1.at[o - 1], got1.at[o - 1], pc.at(c=to))
            for o, to, _ in pc.partners("c")
        ]
        self.two = [
            cp.make(held1.at[:, to, :, :, a], got2a.at[o - 1], got2a.at[o - 1], pc.at(x=to))
            for o, to, _ in pc.partners("x")
        ] + [
            cp.make(held1.at[:, :, to, :, b], got2b.at[o - 1], got2b.at[o - 1], pc.at(y=to))
            for o, to, _ in pc.partners("y")
        ]
        self.three = [
            cp.make(held2.at[0, :, to], got3a.at[o - 1], got3a.at[o - 1], pc.at(y=to))
            for o, to, _ in pc.partners("y")
        ] + [
            cp.make(held2.at[1, :, to], got3b.at[o - 1], got3b.at[o - 1], pc.at(x=to))
            for o, to, _ in pc.partners("x")
        ]
        self.four = [
            cp.make(held3.at[to], got4.at[o - 1], got4.at[o - 1], pc.at(z=to)) for o, to, _ in pc.partners("z")
        ]

    @staticmethod
    def total(acc, got, n):
        acc = acc.astype(f32)
        for o in range(n - 1):
            acc = acc + got[o].astype(f32)
        return acc

    def step(self, k):
        pc = self.pc
        got1, held1, got2a, got2b, held2, got3a, got3b, held3, got4 = self.bufs
        half = held1.shape[-1] // 2
        if k == 0:
            start(self.one)
        elif k == 1:
            finish(self.one)
            for z in range(pc.nz):
                for x in range(pc.nx):
                    acc = self.mine(z, x).astype(f32)
                    for o in range(pc.nc - 1):
                        acc = acc + got1[o, z, x].astype(f32)
                    held1[z, x] = acc.astype(bf)
            start(self.two)
        elif k == 2:
            finish(self.two)
            held2[0, :, : pc.ny] = self.total(held1[:, pc.x, :, :, :half], got2a, pc.nx).astype(bf)
            held2[1, :, : pc.nx] = self.total(held1[:, :, pc.y, :, half:], got2b, pc.ny).astype(bf)
            start(self.three)
        elif k == 3:
            finish(self.three)
            held3[:, :, :half] = self.total(held2[0, :, pc.y], got3a, pc.ny).astype(bf)
            held3[:, :, half:] = self.total(held2[1, :, pc.x], got3b, pc.nx).astype(bf)
            start(self.four)
        else:
            finish(self.four)
            self.out[...] = self.total(held3[pc.z], got4, pc.nz)


def back_kernel(dims, slots, pack, near, *refs):
    refs = list(refs)

    def take(n):
        out = refs[:n]
        del refs[:n]
        return out

    x_ref, q_ref, k_ref, v_ref, da_ref, lse_ref, dmid_ref, mean_ref, ks_ref, vs_ref = take(10)
    wq_ref, wk_ref, wv_ref, ga_ref = take(4)
    (g1_ref,) = take(1) if near else (None,)
    (din_ref,) = take(1)
    outs = take(2 if near else 1)
    aq, ak, av, dq_ref, dk_ref, dv_ref, dks_ref, dvs_ref, far_send, far_got, far_ref = take(11)
    if near:
        (g2_ref, own1) = take(2)
        bufs1, bufs2 = take(9), take(9)
        (own_sem,) = take(1)
    send_sem, recv_sem = take(2)
    T, D = x_ref.shape
    spt, nseq = slots // SPAN, T // slots
    pc = Place(dims)
    cp = Copies(send_sem, recv_sem)
    seq, dp = lax.axis_index("seq"), lax.axis_index("dp")
    seqn = pc.ny * pc.nc
    spans_all, seqs, _ = mean_ref.shape
    i, n = pl.program_id(0), pl.num_programs(0) // 2
    far = []
    for o in range(1, seqn):
        to = (seq + o) % seqn
        far.append(
            cp.make(far_send.at[:, pl.ds(to * spt, spt)], far_got.at[o - 1], far_got.at[o - 1], (dp, to))
        )
    if near:
        own_copy = pltpu.make_async_copy(g1_ref.at[:, :, :, pc.c], own1, own_sem.at[0])
        big = Scatter(pc, cp, g1_ref, lambda z, x: own1[z, x], outs[0], bufs1)
        small = Scatter(pc, cp, g2_ref, lambda z, x: g2_ref[z, x, :, pc.c], outs[1], bufs2)

    @pl.when(i == 0)
    def _():
        seq_peers = [(dp, (seq + o) % seqn) for o in range(1, seqn)]
        zx = [pc.at(**{a: to}) for a in ("z", "x") for _, to, _ in pc.partners(a)]
        pc.greet(zx + seq_peers)
        if near:
            own_copy.start()
            big.step(0)
        for acc in (aq, ak, av):
            acc[...] = jnp.zeros_like(acc)

    if near:

        @pl.when(i == 2)
        def _():
            own_copy.wait()
            big.step(1)

        for k, at in ((2, 6), (3, 8), (4, 11)):

            @pl.when(i == at)
            def _(k=k):
                big.step(k)

    x = x_ref[...].astype(f32)
    r = lax.rsqrt(jnp.mean(x * x, axis=1, keepdims=True) + EPS)
    xr = x * r
    ga = ga_ref[...]

    @pl.when(i < n)
    def _():
        tok = pl.ds(pl.multiple_of(i * T, T), T)
        attend_backward(slots, i, seq, spans_all, q_ref, k_ref, v_ref, da_ref, ks_ref, vs_ref, lse_ref,
                        dq_ref.at[tok], dk_ref.at[tok], dv_ref.at[tok], dks_ref, dvs_ref)
        xt = (xr * ga).astype(bf).T
        aq[...] += dot(xt, dq_ref[tok, :])
        ak[...] += dot(xt, dk_ref[tok, :])
        av[...] += dot(xt, dv_ref[tok, :])

    @pl.when(i == n - 1)
    def _():
        for t in range(spans_all):
            far_send[0, t] = dks_ref[:, t, :].astype(bf)
            far_send[1, t] = dvs_ref[:, t, :].astype(bf)
        start(far)
        mb = (mean_ref[...].astype(f32).reshape(spans_all * seqs, D) * ga).astype(bf)
        fk = far_send[0].reshape(spans_all * seqs, D)
        fv = far_send[1].reshape(spans_all * seqs, D)
        rows = D // pack
        parts = (aq[...], ak[...] + dot(mb, fk, 0, 0), av[...] + dot(mb, fv, 0, 0))
        for j, part in enumerate(parts):
            if near:
                g2_ref[:, :, :, :, j * rows : (j + 1) * rows, :] = part.astype(bf).reshape(dims + (rows, D))
            else:
                outs[0][j] = part
        if near:
            small.step(0)

    @pl.when(i == n)
    def _():
        finish(far)
        tot = []
        for h in range(2):
            acc = far_send[h, pl.ds(seq * spt, spt)].astype(f32)
            for o in range(seqn - 1):
                acc = acc + far_got[o, h].astype(f32)
            tot.append(acc.astype(bf).reshape(spt * seqs, D))
        rows = dot(tot[0], wk_ref[...], 1, 1) + dot(tot[1], wv_ref[...], 1, 1)
        far_ref[...] = (rows * (1.0 / SPAN)).reshape(spt, seqs, D)

    if near:
        for k, at in ((1, 1), (2, 5), (3, 8)):

            @pl.when(i == n + at)
            def _(k=k):
                small.step(k)

    @pl.when(i >= n)
    def _():
        j = i - n
        tok = pl.ds(pl.multiple_of(j * T, T), T)
        dxn = dot(dq_ref[tok, :], wq_ref[...], 1, 1)
        dxn = dxn + dot(dk_ref[tok, :], wk_ref[...], 1, 1)
        dxn = dxn + dot(dv_ref[tok, :], wv_ref[...], 1, 1)
        parts = []
        for s in range(T // SPAN):
            row = far_ref[s % spt, pl.ds(j * nseq + s // spt, 1), :]
            parts.append(dxn[s * SPAN : (s + 1) * SPAN] + row)
        gd = jnp.concatenate(parts, axis=0) * ga
        coef = jnp.mean(gd * xr, axis=1, keepdims=True)
        din_ref[...] = (dmid_ref[...].astype(f32) + r * (gd - xr * coef)).astype(bf)

    if near:

        @pl.when(i == 2 * n - 1)
        def _():
            small.step(4)


def attend_backward(slots, i, seq, spans_all, q_ref, k_ref, v_ref, da_ref, ks_ref, vs_ref, lse_ref,
                    dq_ref, dk_ref, dv_ref, dks_ref, dvs_ref):
    T, D = q_ref.shape
    spt, nseq = slots // SPAN, T // slots
    causal = causal_mask()
    t_row = lax.broadcasted_iota(jnp.int32, (FARP, 2 * SPAN), 0)

    def where(u):
        s, p = u
        return slice(s * SPAN, (s + 1) * SPAN), slice(p * 128, (p + 1) * 128), i * nseq + s // spt

    def scores(u):
        rows, ln, sq = where(u)
        ke = jnp.concatenate([k_ref[rows, ln], ks_ref[sq, :, ln]], axis=0)
        ve = jnp.concatenate([v_ref[rows, ln], vs_ref[sq, :, ln]], axis=0)
        qbd, dbd = pair_diag(q_ref[rows, ln]), pair_diag(da_ref[rows, ln])
        return dot(ke, qbd, 1, 1), dot(ve, dbd, 1, 1)

    def weigh(u, got):
        sc, dp = got
        rows, p = where(u)[0], u[1]
        far = t_row < (seq * spt + u[0] % spt)
        lse = jnp.concatenate([lse_ref[2 * p : 2 * p + 1, rows], lse_ref[2 * p + 1 : 2 * p + 2, rows]], axis=1)
        pn = jnp.where(causal, jnp.exp(sc[:SPAN] - lse), 0.0)
        pf = jnp.where(far, jnp.exp(sc[SPAN:] - lse), 0.0)
        dpn, dpf = dp[:SPAN], dp[SPAN:]
        delta = jnp.sum(pn * dpn, axis=0, keepdims=True) + jnp.sum(pf * dpf, axis=0, keepdims=True)
        dsn, dsf = (pn * (dpn - delta)).astype(bf), (pf * (dpf - delta)).astype(bf)
        return pn.astype(bf), pf.astype(bf), dsn, dsf

    def combine(u, pn, pf, dsn, dsf):
        rows, ln, sq = where(u)
        qbd, dbd = pair_diag(q_ref[rows, ln]), pair_diag(da_ref[rows, ln])
        dv = dot(jnp.concatenate([pn, pf], axis=0), dbd)
        dk = dot(jnp.concatenate([dsn, dsf], axis=0), qbd)
        dq = dot(k_ref[rows, ln], dsn, 0, 0) + dot(ks_ref[sq, :, ln], dsf, 0, 0)
        dq = jnp.concatenate([dq[:HD, :SPAN], dq[HD:, SPAN:]], axis=0) * (HD**-0.5)
        dq_ref[rows, ln] = dq.astype(bf).T
        dk_ref[rows, ln] = dk[:SPAN].astype(bf)
        dv_ref[rows, ln] = dv[:SPAN].astype(bf)
        fk, fv = dk[SPAN : SPAN + spans_all], dv[SPAN : SPAN + spans_all]
        if u[0] % spt == 0:
            dks_ref[sq, :, ln] = fk
            dvs_ref[sq, :, ln] = fv
        else:
            dks_ref[sq, :, ln] += fk
            dvs_ref[sq, :, ln] += fv

    units = [(s, p) for s in range(T // SPAN) for p in range(D // 128)]
    staged(units, scores, weigh, combine)


def back_call(dims, slots, block, pack, near, x, q, k, v, da, lse, dmid, mean, ks, vs, wq, wk, wv, ga, g1):
    n_tok, D = x.shape
    nz, nx, ny, nc = dims
    n = n_tok // block
    spt = slots // SPAN
    spans_all, seqs, _ = mean.shape
    seqn = ny * nc
    vm = pltpu.VMEM
    early = pl.BlockSpec((block, D), lambda i: (jnp.minimum(i, n - 1), 0))
    late = pl.BlockSpec((block, D), lambda i: (jnp.maximum(i - n, 0), 0))
    rows2 = D // pack * 3
    in_specs = (
        [pl.BlockSpec((block, D), lambda i: (i % n, 0))]
        + [early] * 4
        + [pl.BlockSpec((H, block), lambda i: (0, jnp.minimum(i, n - 1))), late]
        + [full(mean.shape), full(ks.shape), full(vs.shape)]
        + [full((D, D))] * 3
        + [full((1, D))]
    )
    args = [x, q, k, v, da, lse, dmid, mean, ks, vs, wq, wk, wv, ga]
    out_specs, out_shape = [late], [sds((n_tok, D), bf)]
    scratch = [vm((D, D), f32)] * 3 + [vm((n_tok, D), bf)] * 3 + [vm((seqs, spans_all, D), f32)] * 2
    scratch += [
        vm((2, spans_all, seqs, D), bf),
        vm((seqn - 1, 2, spt, seqs, D), bf),
        vm((spt, seqs, D), f32),
    ]
    copies = seqn - 1
    if near:
        rows1 = g1.shape[1]
        args.append(g1.reshape(dims + g1.shape[1:]))
        in_specs.append(pl.BlockSpec(memory_space=pl.ANY))
        out_specs += [full((rows1, D)), full((rows2, D))]
        out_shape += [sds((rows1, D), f32), sds((rows2, D), f32)]
        scratch += [vm(dims + (rows2, D), bf), vm((nz, nx, ny, rows1, D), bf)]
        scratch += Scatter.scratch(dims, rows1, D) + Scatter.scratch(dims, rows2, D)
        scratch.append(pltpu.SemaphoreType.DMA((1,)))
        copies += 2 * Scatter.copies(dims)
    else:
        out_specs.append(full((3, D, D)))
        out_shape.append(sds((3, D, D), f32))
    scratch += [pltpu.SemaphoreType.DMA((copies,))] * 2
    return pl.pallas_call(
        partial(back_kernel, dims, slots, pack, near),
        grid=(2 * n,),
        in_specs=in_specs,
        out_specs=out_specs,
        out_shape=out_shape,
        scratch_shapes=scratch,
        compiler_params=pltpu.CompilerParams(
            vmem_limit_bytes=VMEM_LIMIT, collective_id=1, has_side_effects=True,
            dimension_semantics=("arbitrary",),
        ),
    )(*args)


def body(dims, inputs, lengths, cotangent, w_query, w_key, w_value, w_out, w_up, w_down, gain_attn, gain_mlp):
    seqs, slots, D = inputs.shape
    nz, nx, ny, nc = dims
    ndev = nz * nx * ny * nc
    FF = w_up.shape[1]
    rd, rf = w_query.shape[0], w_down.shape[0]
    n_tok = seqs * slots
    block = 512
    x = inputs.reshape(n_tok, D)
    cot = cotangent.reshape(n_tok, D)
    gains = jnp.zeros((8, 256), f32)
    gains = gains.at[0, :rd].set(gain_attn.astype(f32)).at[1, :rd].set(gain_mlp.astype(f32))
    everyone = ("dp", "seq")
    near = rd % 16 == 0 and n_tok // block >= 12
    if near:
        w_first, w_later = (w_query, w_key, w_value), (w_up, w_down, w_out)
    else:
        wq, wk, wv, wu, wd, wo = (
            lax.all_gather(w, everyone, axis=0, tiled=True)
            for w in (w_query, w_key, w_value, w_up, w_down, w_out)
        )
        w_first, w_later = (wq, wk, wv), ()
    q, k, v, att, lse, ks, vs, mean, ga, gm, *later = front_call(dims, slots, block, x, w_first, w_later, gains, near)
    if near:
        *firsts, wu, wd, wo = (w.reshape(-1, w.shape[-1]) for w in later)
        wq, wk, wv = firsts
    pack = ndev if near else 32
    output, datt, dmid, sums_m = mlp_call(512, slots, 2 * block, pack, lengths, x, att, cot, wo, wu, wd, gm)
    grad_in, *sums = back_call(
        dims, slots, block, pack, near, x, q, k, v, datt, lse, dmid, mean, ks, vs, wq, wk, wv, ga, sums_m
    )
    pd, pf = D // pack, FF // pack
    last = pd * (FF // D + 1) + pf
    if near:
        sums_m, sums_a = sums
        g_out = sums_m[:pd]
        g_up = jnp.concatenate([sums_m[pd * (j + 1) : pd * (j + 2)] for j in range(FF // D)], axis=1)
        g_down = sums_m[pd * (FF // D + 1) : last]
        g_q, g_k, g_v = (sums_a[j * pd : (j + 1) * pd] for j in range(3))
    else:

        def scattered(a):
            return lax.psum_scatter(a.astype(f32), everyone, scatter_dimension=0, tiled=True)

        g_out = scattered(sums_m[:, :pd].reshape(D, D))
        g_up = scattered(
            jnp.concatenate([sums_m[:, pd * (j + 1) : pd * (j + 2)].reshape(D, D) for j in range(FF // D)], axis=1)
        )
        g_down = scattered(sums_m[:, pd * (FF // D + 1) : last].reshape(FF, D))
        g_q, g_k, g_v = (scattered(sums[0][j]) for j in range(3))
    g_ga = jnp.sum(
        w_query.astype(f32) * g_q + w_key.astype(f32) * g_k + w_value.astype(f32) * g_v, axis=1
    ) / gain_attn.astype(f32)
    g_gm = jnp.sum(w_up.astype(f32) * g_up, axis=1) / gain_mlp.astype(f32)
    return (
        output.reshape(inputs.shape), grad_in.astype(f32).reshape(inputs.shape),
        g_q, g_k, g_v, g_out, g_up, g_down, g_ga, g_gm,
    )


def solution(mesh):
    dp, seq = mesh.shape["dp"], mesh.shape["seq"]
    nx = max(d for d in range(1, dp + 1) if dp % d == 0 and d * d <= dp)
    nc = 2 if seq % 2 == 0 else 1
    dims = (dp // nx, nx, seq // nc, nc)
    rows, vec = P(("dp", "seq"), None), P(("dp", "seq"))
    tokens = P("dp", "seq", None)
    return jax.shard_map(
        partial(body, dims),
        mesh=mesh,
        in_specs=(tokens, P("dp"), tokens) + (rows,) * 6 + (vec,) * 2,
        out_specs=(tokens, tokens) + (rows,) * 6 + (vec,) * 2,
        check_vma=False,
    )
```

```python
from functools import partial

import jax
import jax.numpy as jnp
from jax import lax
from jax.experimental import pallas as pl
from jax.experimental.pallas import tpu as pltpu
from jax.sharding import PartitionSpec as P

H = 8
HD = 64
SPAN = 128
EPS = 1e-06
K0 = 0.7978845608028654
K1 = 0.044715
FARP = 16
f32 = jnp.float32
bf = jnp.bfloat16
MESH = pl.DeviceIdType.MESH
VMEM_LIMIT = 62 << 20


def dot(a, b, ca=1, cb=0):
    return lax.dot_general(a, b, (((ca,), (cb,)), ((), ())), preferred_element_type=f32)


def sds(shape, dtype):
    return jax.ShapeDtypeStruct(shape, dtype)


def full(shape):
    return pl.BlockSpec(shape, lambda i: (0,) * len(shape), pipeline_mode=pl.Buffered(1))


def pair_diag(a):
    lane = lax.broadcasted_iota(jnp.int32, a.shape, 1)
    zero = jnp.zeros_like(a)
    return jnp.concatenate([jnp.where(lane < HD, a, zero), jnp.where(lane >= HD, a, zero)], axis=0)


def causal_mask():
    j = lax.broadcasted_iota(jnp.int32, (SPAN, 2 * SPAN), 0)
    i = lax.broadcasted_iota(jnp.int32, (SPAN, 2 * SPAN), 1)
    return j <= jnp.where(i >= SPAN, i - SPAN, i)


def gain_row(slabs, which, ndev, rows):
    width = ndev * rows
    r = lax.broadcasted_iota(jnp.int32, slabs.shape, 0)
    l = lax.broadcasted_iota(jnp.int32, slabs.shape, 1)
    keep = jnp.where((r % 16 == which) & (l < rows), slabs.astype(f32), 0.0).astype(bf)
    a = lax.broadcasted_iota(jnp.int32, (128, width), 0)
    b = lax.broadcasted_iota(jnp.int32, (128, width), 1)
    spread = dot(keep, jnp.where(b % rows == a, 1.0, 0.0).astype(bf))
    d = lax.broadcasted_iota(jnp.int32, spread.shape, 0)
    c = lax.broadcasted_iota(jnp.int32, spread.shape, 1)
    return jnp.sum(jnp.where(d // 16 == c // rows, spread, 0.0), axis=0, keepdims=True)


class Place:
    def __init__(self, dims):
        self.nz, self.nx, self.ny, self.nc = dims
        dp, seq = lax.axis_index("dp"), lax.axis_index("seq")
        self.z, self.x = dp // self.nx, dp % self.nx
        self.y, self.c = seq // self.nc, seq % self.nc

    def at(self, z=None, x=None, y=None, c=None):
        z = self.z if z is None else z
        x = self.x if x is None else x
        y = self.y if y is None else y
        c = self.c if c is None else c
        return (z * self.nx + x, y * self.nc + c)

    def line(self, axis):
        return getattr(self, axis), getattr(self, "n" + axis)

    def partners(self, axis):
        me, n = self.line(axis)
        return [(o, (me + o) % n, (me + n - o) % n) for o in range(1, n)]

    def greet(self, others):
        for other in others:
            pl.semaphore_signal(pltpu.get_barrier_semaphore(), inc=1, device_id=other, device_id_type=MESH)

    def meet(self, others):
        pl.semaphore_wait(pltpu.get_barrier_semaphore(), len(others))

    def others(self):
        return [self.at(**{a: to}) for a in ("z", "x", "y", "c") for _, to, _ in self.partners(a)]


class Copies:
    def __init__(self, send_sem, recv_sem):
        self.send_sem, self.recv_sem, self.used = send_sem, recv_sem, 0

    def make(self, src, dst, landed, device):
        k = self.used
        self.used += 1
        out = pltpu.make_async_remote_copy(
            src_ref=src, dst_ref=dst, send_sem=self.send_sem.at[k], recv_sem=self.recv_sem.at[k],
            device_id=device, device_id_type=MESH,
        )
        into = pltpu.make_async_remote_copy(
            src_ref=src, dst_ref=landed, send_sem=self.send_sem.at[k], recv_sem=self.recv_sem.at[k],
            device_id=device, device_id_type=MESH,
        )
        return out, into


def start(copies):
    for out, _ in copies:
        out.start()


def finish(copies):
    for out, into in copies:
        out.wait_send()
        into.wait_recv()


def shares(rows, width):
    if rows % 32 == 0:
        return (pl.ds(0, rows // 2), slice(None)), (pl.ds(rows // 2, rows // 2), slice(None))
    return (slice(None), pl.ds(0, width // 2)), (slice(None), pl.ds(width // 2, width // 2))


def gather_phases(pc, cp, pieces, wholes, routes):
    z, x, y, c = pc.z, pc.x, pc.y, pc.c
    first, second, third, last = [], [], [], []
    for piece, whole, route in zip(pieces, wholes, routes):
        rows, width = whole.shape[-2:]
        everything = (slice(None), slice(None))
        one, two = shares(rows, width) if route == "both" else (everything, everything)
        for _, to, fr in pc.partners("z"):
            first.append(cp.make(piece, whole.at[z, x, y, c], whole.at[fr, x, y, c], pc.at(z=to)))
        for _, to, fr in pc.partners("x"):
            if route != "yx":
                v = whole.at[(slice(None), x, y, c) + one]
                second.append(cp.make(v, v, whole.at[(slice(None), fr, y, c) + one], pc.at(x=to)))
            if route != "xy":
                v = whole.at[(slice(None), x, slice(None), c) + two]
                third.append(cp.make(v, v, whole.at[(slice(None), fr, slice(None), c) + two], pc.at(x=to)))
        for _, to, fr in pc.partners("y"):
            if route != "xy":
                v = whole.at[(slice(None), x, y, c) + two]
                second.append(cp.make(v, v, whole.at[(slice(None), x, fr, c) + two], pc.at(y=to)))
            if route != "yx":
                v = whole.at[(slice(None), slice(None), y, c) + one]
                third.append(cp.make(v, v, whole.at[(slice(None), slice(None), fr, c) + one], pc.at(y=to)))
        for _, to, fr in pc.partners("c"):
            v = whole.at[:, :, :, c]
            last.append(cp.make(v, v, whole.at[:, :, :, fr], pc.at(c=to)))
    return first, second, third, last


def front_kernel(dims, slots, n_first, n_later, *refs):
    near = n_first > 0
    refs = list(refs)

    def take(n):
        out = refs[:n]
        del refs[:n]
        return out

    x_ref, ga_own, gm_own = take(3)
    pieces = take(n_first + n_later)
    w_in = [] if near else take(3)
    q_ref, k_ref, v_ref, att_ref, lse_ref, ks_ref, vs_ref, mean_ref, ga_ref, gm_ref = take(10)
    w_out = take(n_first)
    later = take(n_later)
    pack_ref, gain_ref, own_mean, all_mean, local_sem, send_sem, recv_sem = take(7)
    T, D = x_ref.shape
    spt, nseq = slots // SPAN, T // slots
    pc = Place(dims)
    cp = Copies(send_sem, recv_sem)
    seq, dp = lax.axis_index("seq"), lax.axis_index("dp")
    seqn = pc.ny * pc.nc
    spans_all, seqs = spt * seqn, all_mean.shape[1]
    ndev = pc.nz * pc.nx * seqn
    rd = D // ndev
    mine = (pc.z, pc.x, pc.y, pc.c)
    packs = [pack_ref, gain_ref] if near else [gain_ref]
    first = gather_phases(pc, cp, [p.at[mine] for p in packs], packs, ["both", "xy"][-len(packs) :])
    later_phases = gather_phases(pc, cp, pieces[n_first:], later, ["xy", "yx", "both"][:n_later])
    own_first = [
        pltpu.make_async_copy(p, pack_ref.at[mine + (pl.ds(k * rd, rd),)], local_sem.at[k])
        for k, p in enumerate(pieces[:n_first])
    ]
    own_later = [
        pltpu.make_async_copy(p, w.at[mine], local_sem.at[n_first + k])
        for k, (p, w) in enumerate(zip(pieces[n_first:], later))
    ]
    means = []
    for o in range(1, seqn):
        to, fr = (seq + o) % seqn, (seq + seqn - o) % seqn
        v = all_mean.at[pl.ds(seq * spt, spt)]
        means.append(cp.make(v, v, all_mean.at[pl.ds(fr * spt, spt)], (dp, to)))
    i, n = pl.program_id(0), pl.num_programs(0) // 2
    w_refs = w_out if near else w_in

    @pl.when(i == 0)
    def _():
        for copy in own_first + own_later:
            copy.start()
        slab = jnp.concatenate([ga_own[...], gm_own[...]], axis=0).astype(f32)
        gain_ref[mine] = jnp.concatenate(
            [jnp.concatenate([slab, jnp.zeros((2, max(128 - rd, 0)), f32)], axis=1)[:, :128], jnp.zeros((14, 128), f32)], axis=0
        ).astype(bf)
        seq_peers = [(dp, (seq + o) % seqn) for o in range(1, seqn)]
        zx = [pc.at(**{a: to}) for a in ("z", "x") for _, to, _ in pc.partners(a)]
        pc.greet(zx + seq_peers)
        pc.meet(zx + seq_peers)
        for copy in own_first:
            copy.wait()
        start(first[0])

    x = x_ref[...].astype(f32)
    r = lax.rsqrt(jnp.mean(x * x, axis=1, keepdims=True) + EPS)
    xr = x * r

    @pl.when(i < n)
    def _():
        for s in range(T // SPAN):
            row = jnp.sum(xr[s * SPAN : (s + 1) * SPAN], axis=0, keepdims=True) * (1.0 / SPAN)
            own_mean[s % spt, pl.ds(i * nseq + s // spt, 1), :] = row

    @pl.when(i == 1)
    def _():
        finish(first[0])
        start(first[1])
        for copy in own_later:
            copy.wait()
        if near:
            start(later_phases[0])

    @pl.when(i == n - 1)
    def _():
        finish(first[1])
        start(first[2])
        all_mean[pl.ds(seq * spt, spt)] = own_mean[...].astype(bf)
        start(means)
        finish(first[2])
        start(first[3])
        finish(means)
        mean_ref[...] = all_mean[...]
        to = lax.broadcasted_iota(jnp.int32, (seqs * FARP, spans_all * seqs), 0)
        fr = lax.broadcasted_iota(jnp.int32, (seqs * FARP, spans_all * seqs), 1)
        order = jnp.where((to % FARP == fr // seqs) & (to // FARP == fr % seqs), 1.0, 0.0).astype(bf)
        ordered = dot(order, all_mean[...].reshape(spans_all * seqs, D))
        finish(first[3])
        slabs = gain_ref[...].reshape(ndev * 16, 128)
        ga_ref[...] = gain_row(slabs, 0, ndev, rd)
        gm_ref[...] = gain_row(slabs, 1, ndev, rd)
        for k in range(n_first):
            w_out[k][...] = pack_ref[:, :, :, :, k * rd : (k + 1) * rd, :].reshape(D, D)
        mb = (ordered * ga_ref[...]).astype(bf)
        ks_ref[...] = dot(mb, w_refs[1][...]).astype(bf).reshape(seqs, FARP, D)
        vs_ref[...] = dot(mb, w_refs[2][...]).astype(bf).reshape(seqs, FARP, D)

    if near:
        for k, at in ((1, 0), (2, 2), (3, 5)):

            @pl.when(i == n + at)
            def _(k=k):
                finish(later_phases[k - 1])
                start(later_phases[k])

    @pl.when(i >= n)
    def _():
        j = i - n
        xn = (xr * ga_ref[...]).astype(bf)
        q_ref[...] = (dot(xn, w_refs[0][...]).astype(bf) * (HD**-0.5)).astype(bf)
        k_ref[...] = dot(xn, w_refs[1][...]).astype(bf)
        v_ref[...] = dot(xn, w_refs[2][...]).astype(bf)
        attend_forward(slots, j, seq, q_ref, k_ref, v_ref, ks_ref, vs_ref, att_ref, lse_ref)

    if near:

        @pl.when(i == 2 * n - 1)
        def _():
            finish(later_phases[3])


def attend_forward(slots, j, seq, q_ref, k_ref, v_ref, ks_ref, vs_ref, att_ref, lse_ref):
    T, D = q_ref.shape
    spt, nseq = slots // SPAN, T // slots
    causal = causal_mask()
    t_row = lax.broadcasted_iota(jnp.int32, (FARP, 2 * SPAN), 0)

    def where(u):
        s, p = u
        return slice(s * SPAN, (s + 1) * SPAN), slice(p * 128, (p + 1) * 128), j * nseq + s // spt

    def scores(u):
        rows, ln, sq = where(u)
        ke = jnp.concatenate([k_ref[rows, ln], ks_ref[sq, :, ln]], axis=0)
        return dot(ke, pair_diag(q_ref[rows, ln]), 1, 1)

    def weigh(u, sc):
        far = t_row < (seq * spt + u[0] % spt)
        sn = jnp.where(causal, sc[:SPAN], -1e30)
        sf = jnp.where(far, sc[SPAN:], -1e30)
        m = jnp.maximum(jnp.max(sn, axis=0, keepdims=True), jnp.max(sf, axis=0, keepdims=True))
        en = jnp.exp(sn - m)
        ef = jnp.exp(sf - m)
        l = jnp.sum(en, axis=0, keepdims=True) + jnp.sum(ef, axis=0, keepdims=True)
        return en.astype(bf), ef.astype(bf), m, l

    def combine(u, en, ef, m, l):
        rows, ln, sq = where(u)
        p = u[1]
        ve = jnp.concatenate([v_ref[rows, ln], vs_ref[sq, :, ln]], axis=0)
        at = dot(ve, jnp.concatenate([en, ef], axis=0), 0, 0) * (1.0 / l)
        att_ref[rows, ln] = jnp.concatenate([at[:HD, :SPAN], at[HD:, SPAN:]], axis=0).astype(bf).T
        total = m + jnp.log(l)
        lse_ref[2 * p : 2 * p + 1, rows] = total[:, :SPAN]
        lse_ref[2 * p + 1 : 2 * p + 2, rows] = total[:, SPAN:]

    units = [(s, p) for s in range(T // SPAN) for p in range(D // 128)]
    staged(units, scores, weigh, combine)


def staged(units, first, second, third):
    a, b = {}, {}
    for t in range(0, len(units) + 4, 2):
        for k in (t, t + 1):
            if k < len(units):
                a[k] = first(units[k])
        for k in (t - 2, t - 1):
            if 0 <= k < len(units):
                b[k] = second(units[k], a.pop(k))
        for k in (t - 4, t - 3):
            if 0 <= k < len(units):
                third(units[k], *b.pop(k))


def front_call(dims, slots, block, x, w_first, w_later, gains, near):
    n_tok, D = x.shape
    seqs, spt = n_tok // slots, slots // SPAN
    nz, nx, ny, nc = dims
    n = n_tok // block
    ndev = nz * nx * ny * nc
    spans_all = spt * ny * nc
    hbm = pl.BlockSpec(memory_space=pl.ANY)
    summ = (seqs, FARP, D)
    per_piece = (nz - 1) + 2 * (nx - 1) + 2 * (ny - 1) + (nc - 1)
    n_first, n_later = (len(w_first), len(w_later)) if near else (0, 0)
    rows = sum(w.shape[0] for w in w_first) if near else 16
    copies = (2 + n_later) * per_piece + ny * nc - 1
    late = lambda i: jnp.maximum(i - n, 0)
    tok = pl.BlockSpec((block, D), lambda i: (late(i), 0))
    in_specs = [pl.BlockSpec((block, D), lambda i: (i % n, 0)), full((1, D // ndev)), full((1, D // ndev))]
    in_specs += [hbm] * (n_first + n_later) if near else [full(w.shape) for w in w_first]
    row = sds((1, D), f32)
    return pl.pallas_call(
        partial(front_kernel, dims, slots, n_first, n_later),
        grid=(2 * n,),
        in_specs=in_specs,
        out_specs=[tok] * 4
        + [pl.BlockSpec((H, block), lambda i: (0, late(i))), full(summ), full(summ)]
        + [full((spans_all, seqs, D)), full((1, D)), full((1, D))]
        + [full((D, D))] * n_first
        + [hbm] * n_later,
        out_shape=[sds((n_tok, D), bf)] * 4
        + [sds((H, n_tok), f32), sds(summ, bf), sds(summ, bf), sds((spans_all, seqs, D), bf), row, row]
        + [sds((D, D), bf)] * n_first
        + [sds(dims + w.shape, w.dtype) for w in w_later[:n_later]],
        scratch_shapes=[
            pltpu.VMEM(dims + (rows, D), bf),
            pltpu.VMEM(dims + (16, 128), bf),
            pltpu.VMEM((spt, seqs, D), f32),
            pltpu.VMEM((spans_all, seqs, D), bf),
            pltpu.SemaphoreType.DMA((max(n_first + n_later, 1),)),
            pltpu.SemaphoreType.DMA((max(copies, 1),)),
            pltpu.SemaphoreType.DMA((max(copies, 1),)),
        ],
        compiler_params=pltpu.CompilerParams(
            vmem_limit_bytes=VMEM_LIMIT, collective_id=0, has_side_effects=True,
            dimension_semantics=("arbitrary",),
        ),
    )(x, *gains, *w_first, *w_later)


def mlp_kernel(chunk, slots, ndev, len_ref, x_ref, att_ref, cot_ref, wo_ref, wu_ref, wd_ref, gm_ref,
               out_ref, datt_ref, dmid_ref, gsum_ref, adown, aup, aout):
    T, D = x_ref.shape
    FF = wu_ref.shape[1]
    i, n = pl.program_id(0), pl.num_programs(0)

    @pl.when(i == 0)
    def _():
        for acc in (adown, aup, aout):
            acc[...] = jnp.zeros_like(acc)

    att = att_ref[...]
    mid = x_ref[...].astype(f32) + dot(att, wo_ref[...])
    r = lax.rsqrt(jnp.mean(mid * mid, axis=1, keepdims=True) + EPS)
    gm = gm_ref[...]
    hn = (mid * r * gm).astype(bf)
    nseq = T // slots
    row = lax.broadcasted_iota(jnp.int32, (slots, 1), 0) + lax.axis_index("seq") * slots
    valid = jnp.concatenate(
        [jnp.where(row < len_ref[i * nseq + s], 1.0, 0.0) for s in range(nseq)], axis=0
    )
    g = cot_ref[...].astype(f32) * valid
    gb = g.astype(bf)
    gbt = gb.T
    hnt = hn.T
    y = jnp.zeros((T, D), f32)
    dhn = jnp.zeros((T, D), f32)
    cols = [slice(j * chunk, (j + 1) * chunk) for j in range(FF // chunk)]

    def products(sl):
        return dot(hn, wu_ref[:, sl]), dot(gb, wd_ref[sl, :], 1, 1)

    ready = products(cols[0])
    for j, sl in enumerate(cols):
        u, da = ready
        if j + 1 < len(cols):
            ready = products(cols[j + 1])
        h = 0.5 + 0.5 * jnp.tanh(u * (K0 + (K0 * K1) * (u * u)))
        act = (u * h).astype(bf)
        ub, hb = u.astype(bf), h.astype(bf)
        slope = hb + (ub * (bf(K0) + bf(3 * K0 * K1) * (ub * ub))) * ((hb + hb) * (bf(1.0) - hb))
        du = da.astype(bf) * slope
        y = y + dot(act, wd_ref[sl, :])
        dhn = dhn + dot(du, wu_ref[:, sl], 1, 1)
        adown[:, sl] += dot(gbt, act)
        aup[:, sl] += dot(hnt, du)
    out_ref[...] = ((mid + y) * valid).astype(bf)
    mr = mid * r
    gd = dhn * gm
    coef = jnp.mean(gd * mr, axis=1, keepdims=True)
    db = (g + r * (gd - mr * coef)).astype(bf)
    dmid_ref[...] = db
    aout[...] += dot(att, db, 0, 0)
    datt_ref[...] = dot(db, wo_ref[...], 1, 1).astype(bf)

    @pl.when(i == n - 1)
    def _():
        rd, rf = D // ndev, FF // ndev
        gsum_ref[:, :rd, :] = aout[...].reshape(ndev, rd, D).astype(bf)
        for j in range(FF // D):
            gsum_ref[:, rd * (j + 1) : rd * (j + 2), :] = (
                aup[:, j * D : (j + 1) * D].reshape(ndev, rd, D).astype(bf)
            )
            part = adown[:, j * D : (j + 1) * D].T.astype(bf)
            nd = D // rf
            gsum_ref[j * nd : (j + 1) * nd, rd * (FF // D + 1) : rd * (FF // D + 1) + rf, :] = part.reshape(
                nd, rf, D
            )


def mlp_call(chunk, slots, block, ndev, lens, x, att, cot, wo, wu, wd, gm):
    n_tok, D = x.shape
    FF = wu.shape[1]
    tok = pl.BlockSpec((block, D), lambda i: (i, 0))
    rows = D // ndev * (FF // D + 1) + FF // ndev
    return pl.pallas_call(
        partial(mlp_kernel, chunk, slots, ndev),
        grid=(n_tok // block,),
        in_specs=[pl.BlockSpec(memory_space=pltpu.SMEM), tok, tok, tok]
        + [full((D, D)), full((D, FF)), full((FF, D)), full((1, D))],
        out_specs=[tok, tok, tok, full((ndev, rows, D))],
        out_shape=[sds((n_tok, D), bf)] * 3 + [sds((ndev, rows, D), bf)],
        scratch_shapes=[pltpu.VMEM((D, FF), f32), pltpu.VMEM((D, FF), f32), pltpu.VMEM((D, D), f32)],
        compiler_params=pltpu.CompilerParams(
            vmem_limit_bytes=VMEM_LIMIT, dimension_semantics=("arbitrary",)
        ),
    )(lens, x, att, cot, wo, wu, wd, gm)


class Scatter:
    @staticmethod
    def scratch(dims, rows, width):
        nz, nx, ny, nc = dims
        most = max(nx, ny)
        half = (rows // 2, width) if rows % 32 == 0 else (rows, width // 2)
        return [
            pltpu.VMEM((nc - 1, nz, nx, ny, rows, width), bf),
            pltpu.VMEM((nz, nx, ny, rows, width), bf),
            pltpu.VMEM((nx - 1, nz, ny) + half, bf),
            pltpu.VMEM((ny - 1, nz, nx) + half, bf),
            pltpu.VMEM((2, nz, most) + half, bf),
            pltpu.VMEM((ny - 1, nz) + half, bf),
            pltpu.VMEM((nx - 1, nz) + half, bf),
            pltpu.VMEM((nz, rows, width), bf),
            pltpu.VMEM((nz - 1, rows, width), bf),
        ]

    @staticmethod
    def copies(dims):
        nz, nx, ny, nc = dims
        return (nc - 1) + 2 * (nx - 1) + 2 * (ny - 1) + (nz - 1)

    def __init__(self, pc, cp, g, mine, out, scratch):
        self.pc, self.mine, self.out, self.bufs = pc, mine, out, scratch
        got1, held1, got2a, got2b, held2, got3a, got3b, held3, got4 = scratch
        a, b = self.a, self.b = shares(*g.shape[-2:])
        every = slice(None)
        self.one = [
            cp.make(g.at[:, :, :, to], got1.at[o - 1], got1.at[o - 1], pc.at(c=to))
            for o, to, _ in pc.partners("c")
        ]
        self.two = [
            cp.make(held1.at[(every, to, every) + a], got2a.at[o - 1], got2a.at[o - 1], pc.at(x=to))
            for o, to, _ in pc.partners("x")
        ] + [
            cp.make(held1.at[(every, every, to) + b], got2b.at[o - 1], got2b.at[o - 1], pc.at(y=to))
            for o, to, _ in pc.partners("y")
        ]
        self.three = [
            cp.make(held2.at[0, :, to], got3a.at[o - 1], got3a.at[o - 1], pc.at(y=to))
            for o, to, _ in pc.partners("y")
        ] + [
            cp.make(held2.at[1, :, to], got3b.at[o - 1], got3b.at[o - 1], pc.at(x=to))
            for o, to, _ in pc.partners("x")
        ]
        self.four = [
            cp.make(held3.at[to], got4.at[o - 1], got4.at[o - 1], pc.at(z=to)) for o, to, _ in pc.partners("z")
        ]

    @staticmethod
    def total(acc, got, n):
        if n == 2:
            return acc + got[0]
        acc = acc.astype(f32)
        for o in range(n - 1):
            acc = acc + got[o].astype(f32)
        return acc

    def step(self, k):
        pc = self.pc
        got1, held1, got2a, got2b, held2, got3a, got3b, held3, got4 = self.bufs
        every = slice(None)
        if k == 0:
            start(self.one)
        elif k == 1:
            finish(self.one)
            for z in range(pc.nz):
                for x in range(pc.nx):
                    acc = self.mine(z, x)
                    for o in range(pc.nc - 1):
                        acc = acc + got1[o, z, x]
                    held1[z, x] = acc
            start(self.two)
        elif k == 2:
            finish(self.two)
            held2[0, :, : pc.ny] = self.total(held1[(every, pc.x, every) + self.a], got2a, pc.nx).astype(bf)
            held2[1, :, : pc.nx] = self.total(held1[(every, every, pc.y) + self.b], got2b, pc.ny).astype(bf)
            start(self.three)
        elif k == 3:
            finish(self.three)
            held3[(every,) + self.a] = self.total(held2[0, :, pc.y], got3a, pc.ny).astype(bf)
            held3[(every,) + self.b] = self.total(held2[1, :, pc.x], got3b, pc.nx).astype(bf)
            start(self.four)
        else:
            finish(self.four)
            self.out[...] = self.total(held3[pc.z], got4, pc.nz).astype(f32)


def back_kernel(dims, slots, pack, near, *refs):
    refs = list(refs)

    def take(n):
        out = refs[:n]
        del refs[:n]
        return out

    x_ref, q_ref, k_ref, v_ref, da_ref, lse_ref, dmid_ref, mean_ref, ks_ref, vs_ref = take(10)
    wq_ref, wk_ref, wv_ref, ga_ref = take(4)
    (g1_ref,) = take(1) if near else (None,)
    (din_ref,) = take(1)
    outs = take(2 if near else 1)
    aq, ak, av, dq_ref, dk_ref, dv_ref, dks_ref, dvs_ref, far_send, far_got, far_ref = take(11)
    if near:
        (g2_ref, own1) = take(2)
        bufs1, bufs2 = take(9), take(9)
        (own_sem,) = take(1)
    send_sem, recv_sem = take(2)
    T, D = x_ref.shape
    spt, nseq = slots // SPAN, T // slots
    pc = Place(dims)
    cp = Copies(send_sem, recv_sem)
    seq, dp = lax.axis_index("seq"), lax.axis_index("dp")
    seqn = pc.ny * pc.nc
    spans_all, seqs, _ = mean_ref.shape
    i, n = pl.program_id(0), pl.num_programs(0) // 2
    far = []
    for o in range(1, seqn):
        to = (seq + o) % seqn
        far.append(
            cp.make(far_send.at[:, pl.ds(to * spt, spt)], far_got.at[o - 1], far_got.at[o - 1], (dp, to))
        )
    if near:
        own_copy = pltpu.make_async_copy(g1_ref.at[:, :, :, pc.c], own1, own_sem.at[0])
        big = Scatter(pc, cp, g1_ref, lambda z, x: own1[z, x], outs[0], bufs1)
        small = Scatter(pc, cp, g2_ref, lambda z, x: g2_ref[z, x, :, pc.c], outs[1], bufs2)

    seq_peers = [(dp, (seq + o) % seqn) for o in range(1, seqn)]
    zx = [pc.at(**{a: to}) for a in ("z", "x") for _, to, _ in pc.partners(a)]

    @pl.when(i == 0)
    def _():
        pc.greet(zx + seq_peers)
        if near:
            own_copy.start()
        for acc in (aq, ak, av):
            acc[...] = jnp.zeros_like(acc)

    @pl.when(i == 1)
    def _():
        pc.meet(zx + seq_peers)
        if near:
            own_copy.wait()
            big.step(0)

    if near:
        for k, at in ((1, n // 3), (2, 2 * n // 3), (3, n - 1), (4, n + 1)):

            @pl.when(i == at)
            def _(k=k):
                big.step(k)

    x = x_ref[...].astype(f32)
    r = lax.rsqrt(jnp.mean(x * x, axis=1, keepdims=True) + EPS)
    xr = x * r
    ga = ga_ref[...]

    @pl.when(i < n)
    def _():
        tok = pl.ds(pl.multiple_of(i * T, T), T)
        attend_backward(slots, i, seq, spans_all, q_ref, k_ref, v_ref, da_ref, ks_ref, vs_ref, lse_ref,
                        dq_ref.at[tok], dk_ref.at[tok], dv_ref.at[tok], dks_ref, dvs_ref)
        xt = (xr * ga).astype(bf).T
        aq[...] += dot(xt, dq_ref[tok, :])
        ak[...] += dot(xt, dk_ref[tok, :])
        av[...] += dot(xt, dv_ref[tok, :])

    @pl.when(i == n - 1)
    def _():
        for t in range(spans_all):
            far_send[0, t] = dks_ref[:, t, :].astype(bf)
            far_send[1, t] = dvs_ref[:, t, :].astype(bf)
        start(far)
        mb = (mean_ref[...].astype(f32).reshape(spans_all * seqs, D) * ga).astype(bf)
        fk = far_send[0].reshape(spans_all * seqs, D)
        fv = far_send[1].reshape(spans_all * seqs, D)
        rows = D // pack
        parts = (aq[...], ak[...] + dot(mb, fk, 0, 0), av[...] + dot(mb, fv, 0, 0))
        for j, part in enumerate(parts):
            if near:
                g2_ref[:, :, :, :, j * rows : (j + 1) * rows, :] = part.astype(bf).reshape(dims + (rows, D))
            else:
                outs[0][j] = part
        if near:
            small.step(0)

    def products(j):
        tok = pl.ds(pl.multiple_of(j * T, T), T)
        dxn = dot(dq_ref[tok, :], wq_ref[...], 1, 1)
        dxn = dxn + dot(dk_ref[tok, :], wk_ref[...], 1, 1)
        return dxn + dot(dv_ref[tok, :], wv_ref[...], 1, 1)

    def to_input(j, dxn):
        parts = []
        for s in range(T // SPAN):
            row = far_ref[s % spt, pl.ds(j * nseq + s // spt, 1), :]
            parts.append(dxn[s * SPAN : (s + 1) * SPAN] + row)
        gd = jnp.concatenate(parts, axis=0) * ga
        coef = jnp.mean(gd * xr, axis=1, keepdims=True)
        din_ref[...] = (dmid_ref[...].astype(f32) + r * (gd - xr * coef)).astype(bf)

    @pl.when(i == n)
    def _():
        dxn = products(0)
        finish(far)
        tot = []
        for h in range(2):
            acc = far_send[h, pl.ds(seq * spt, spt)].astype(f32)
            for o in range(seqn - 1):
                acc = acc + far_got[o, h].astype(f32)
            tot.append(acc.astype(bf).reshape(spt * seqs, D))
        rows = dot(tot[0], wk_ref[...], 1, 1) + dot(tot[1], wv_ref[...], 1, 1)
        far_ref[...] = (rows * (1.0 / SPAN)).reshape(spt, seqs, D)
        to_input(0, dxn)

    if near:
        for k, at in ((1, 1), (2, n // 2), (3, 2 * n // 3)):

            @pl.when(i == n + at)
            def _(k=k):
                small.step(k)

    @pl.when(i > n)
    def _():
        to_input(i - n, products(i - n))

    if near:

        @pl.when(i == 2 * n - 1)
        def _():
            small.step(4)


def attend_backward(slots, i, seq, spans_all, q_ref, k_ref, v_ref, da_ref, ks_ref, vs_ref, lse_ref,
                    dq_ref, dk_ref, dv_ref, dks_ref, dvs_ref):
    T, D = q_ref.shape
    spt, nseq = slots // SPAN, T // slots
    causal = causal_mask()
    t_row = lax.broadcasted_iota(jnp.int32, (FARP, 2 * SPAN), 0)

    def where(u):
        s, p = u
        return slice(s * SPAN, (s + 1) * SPAN), slice(p * 128, (p + 1) * 128), i * nseq + s // spt

    def scores(u):
        rows, ln, sq = where(u)
        ke = jnp.concatenate([k_ref[rows, ln], ks_ref[sq, :, ln]], axis=0)
        ve = jnp.concatenate([v_ref[rows, ln], vs_ref[sq, :, ln]], axis=0)
        qbd, dbd = pair_diag(q_ref[rows, ln]), pair_diag(da_ref[rows, ln])
        return dot(ke, qbd, 1, 1), dot(ve, dbd, 1, 1)

    def weigh(u, got):
        sc, dp = got
        rows, p = where(u)[0], u[1]
        far = t_row < (seq * spt + u[0] % spt)
        lse = jnp.concatenate([lse_ref[2 * p : 2 * p + 1, rows], lse_ref[2 * p + 1 : 2 * p + 2, rows]], axis=1)
        pn = jnp.where(causal, jnp.exp(sc[:SPAN] - lse), 0.0)
        pf = jnp.where(far, jnp.exp(sc[SPAN:] - lse), 0.0)
        dpn, dpf = dp[:SPAN], dp[SPAN:]
        delta = jnp.sum(pn * dpn, axis=0, keepdims=True) + jnp.sum(pf * dpf, axis=0, keepdims=True)
        dsn, dsf = (pn * (dpn - delta)).astype(bf), (pf * (dpf - delta)).astype(bf)
        return pn.astype(bf), pf.astype(bf), dsn, dsf

    def combine(u, pn, pf, dsn, dsf):
        rows, ln, sq = where(u)
        qbd, dbd = pair_diag(q_ref[rows, ln]), pair_diag(da_ref[rows, ln])
        dv = dot(jnp.concatenate([pn, pf], axis=0), dbd)
        ds = jnp.concatenate([dsn, dsf], axis=0)
        dk = dot(ds, qbd)
        ke = jnp.concatenate([k_ref[rows, ln], ks_ref[sq, :, ln]], axis=0)
        dq = dot(ke, ds, 0, 0)
        dq = jnp.concatenate([dq[:HD, :SPAN], dq[HD:, SPAN:]], axis=0) * (HD**-0.5)
        dq_ref[rows, ln] = dq.astype(bf).T
        dk_ref[rows, ln] = dk[:SPAN].astype(bf)
        dv_ref[rows, ln] = dv[:SPAN].astype(bf)
        fk, fv = dk[SPAN : SPAN + spans_all], dv[SPAN : SPAN + spans_all]
        if u[0] % spt == 0:
            dks_ref[sq, :, ln] = fk
            dvs_ref[sq, :, ln] = fv
        else:
            dks_ref[sq, :, ln] += fk
            dvs_ref[sq, :, ln] += fv

    units = [(s, p) for s in range(T // SPAN) for p in range(D // 128)]
    staged(units, scores, weigh, combine)


def back_call(dims, slots, block, pack, near, x, q, k, v, da, lse, dmid, mean, ks, vs, wq, wk, wv, ga, g1):
    n_tok, D = x.shape
    nz, nx, ny, nc = dims
    n = n_tok // block
    spt = slots // SPAN
    spans_all, seqs, _ = mean.shape
    seqn = ny * nc
    vm = pltpu.VMEM
    early = pl.BlockSpec((block, D), lambda i: (jnp.minimum(i, n - 1), 0))
    late = pl.BlockSpec((block, D), lambda i: (jnp.maximum(i - n, 0), 0))
    rows2 = D // pack * 3
    in_specs = (
        [pl.BlockSpec((block, D), lambda i: (i % n, 0))]
        + [early] * 4
        + [pl.BlockSpec((H, block), lambda i: (0, jnp.minimum(i, n - 1))), late]
        + [full(mean.shape), full(ks.shape), full(vs.shape)]
        + [full((D, D))] * 3
        + [full((1, D))]
    )
    args = [x, q, k, v, da, lse, dmid, mean, ks, vs, wq, wk, wv, ga]
    out_specs, out_shape = [late], [sds((n_tok, D), bf)]
    scratch = [vm((D, D), f32)] * 3 + [vm((n_tok, D), bf)] * 3 + [vm((seqs, spans_all, D), f32)] * 2
    scratch += [
        vm((2, spans_all, seqs, D), bf),
        vm((seqn - 1, 2, spt, seqs, D), bf),
        vm((spt, seqs, D), f32),
    ]
    copies = seqn - 1
    if near:
        rows1 = g1.shape[1]
        args.append(g1.reshape(dims + g1.shape[1:]))
        in_specs.append(pl.BlockSpec(memory_space=pl.ANY))
        out_specs += [full((rows1, D)), full((rows2, D))]
        out_shape += [sds((rows1, D), f32), sds((rows2, D), f32)]
        scratch += [vm(dims + (rows2, D), bf), vm((nz, nx, ny, rows1, D), bf)]
        scratch += Scatter.scratch(dims, rows1, D) + Scatter.scratch(dims, rows2, D)
        scratch.append(pltpu.SemaphoreType.DMA((1,)))
        copies += 2 * Scatter.copies(dims)
    else:
        out_specs.append(full((3, D, D)))
        out_shape.append(sds((3, D, D), f32))
    scratch += [pltpu.SemaphoreType.DMA((max(copies, 1),))] * 2
    return pl.pallas_call(
        partial(back_kernel, dims, slots, pack, near),
        grid=(2 * n,),
        in_specs=in_specs,
        out_specs=out_specs,
        out_shape=out_shape,
        scratch_shapes=scratch,
        compiler_params=pltpu.CompilerParams(
            vmem_limit_bytes=VMEM_LIMIT, collective_id=1, has_side_effects=True,
            dimension_semantics=("arbitrary",),
        ),
    )(*args)


def last_kernel(rd, rf, din_ref, m_ref, a_ref, wq_ref, wk_ref, wv_ref, wu_ref, ga_ref, gm_ref,
                out_ref, gq_ref, gk_ref, gv_ref, go_ref, gu_ref, gd_ref, gga_ref, ggm_ref):
    out_ref[...] = din_ref[...].astype(f32)
    D = out_ref.shape[1]
    FF = gu_ref.shape[1]

    @pl.when(pl.program_id(0) == 0)
    def _():
        attn = jnp.zeros((rd, 1), f32)
        for j, (w_ref, g_ref) in enumerate(((wq_ref, gq_ref), (wk_ref, gk_ref), (wv_ref, gv_ref))):
            g = a_ref[j * rd : (j + 1) * rd, :]
            g_ref[...] = g
            attn = attn + jnp.sum(g * w_ref[...].astype(f32), axis=1, keepdims=True)
        go_ref[...] = m_ref[:rd, :]
        up = jnp.zeros((rd, 1), f32)
        for j in range(FF // D):
            g = m_ref[rd * (j + 1) : rd * (j + 2), :]
            gu_ref[:, j * D : (j + 1) * D] = g
            up = up + jnp.sum(g * wu_ref[:, j * D : (j + 1) * D].astype(f32), axis=1, keepdims=True)
        gd_ref[...] = m_ref[rd * (FF // D + 1) :, :]
        for total, gain, out in ((attn, ga_ref, gga_ref), (up, gm_ref, ggm_ref)):
            row = jnp.broadcast_to(total, (rd, 128)).T[:1, :]
            out[...] = row[:, :rd] / gain[...].astype(f32)


def last_call(block, din, sums_m, sums_a, wq, wk, wv, wu, ga, gm):
    n_tok, D = din.shape
    rd, FF = wu.shape
    rf = sums_m.shape[0] - rd * (FF // D + 1)
    tok = pl.BlockSpec((block, D), lambda i: (i, 0))
    args = [sums_m, sums_a, wq, wk, wv, wu, ga, gm]
    shapes = [(rd, D)] * 4 + [(rd, FF), (rf, D), (1, rd), (1, rd)]
    return pl.pallas_call(
        partial(last_kernel, rd, rf),
        grid=(n_tok // block,),
        in_specs=[tok] + [full(a.shape) for a in args],
        out_specs=[tok] + [full(s) for s in shapes],
        out_shape=[sds((n_tok, D), f32)] + [sds(s, f32) for s in shapes],
        compiler_params=pltpu.CompilerParams(
            vmem_limit_bytes=VMEM_LIMIT, dimension_semantics=("arbitrary",)
        ),
    )(din, *args)


def body(dims, inputs, lengths, cotangent, w_query, w_key, w_value, w_out, w_up, w_down, gain_attn, gain_mlp):
    seqs, slots, D = inputs.shape
    nz, nx, ny, nc = dims
    ndev = nz * nx * ny * nc
    FF = w_up.shape[1]
    rd, rf = w_query.shape[0], w_down.shape[0]
    n_tok = seqs * slots
    block = 1024
    x = inputs.reshape(n_tok, D)
    cot = cotangent.reshape(n_tok, D)
    gains = [g.reshape(1, rd) for g in (gain_attn, gain_mlp)]
    everyone = ("dp", "seq")
    near = rd % 16 == 0 and n_tok // block >= 6
    if near:
        w_first, w_later = (w_query, w_key, w_value), (w_up, w_down, w_out)
    else:
        wq, wk, wv, wu, wd, wo = (
            lax.all_gather(w, everyone, axis=0, tiled=True)
            for w in (w_query, w_key, w_value, w_up, w_down, w_out)
        )
        w_first, w_later = (wq, wk, wv), ()
    q, k, v, att, lse, ks, vs, mean, ga, gm, *later = front_call(dims, slots, block, x, w_first, w_later, gains, near)
    if near:
        wq, wk, wv, wu, wd, wo = (w.reshape(-1, w.shape[-1]) for w in later)
    pack = ndev if near else 32
    output, datt, dmid, sums_m = mlp_call(512, slots, block, pack, lengths, x, att, cot, wo, wu, wd, gm)
    grad_in, *sums = back_call(
        dims, slots, block, pack, near, x, q, k, v, datt, lse, dmid, mean, ks, vs, wq, wk, wv, ga, sums_m
    )
    if near:
        grad_in, g_q, g_k, g_v, g_out, g_up, g_down, g_ga, g_gm = last_call(
            n_tok // 3, grad_in, *sums, w_query, w_key, w_value, w_up, *gains
        )
        g_ga, g_gm = g_ga.reshape(rd), g_gm.reshape(rd)
    else:
        pd, pf = D // pack, FF // pack
        last = pd * (FF // D + 1) + pf

        def scattered(a):
            return lax.psum_scatter(a.astype(f32), everyone, scatter_dimension=0, tiled=True)

        g_out = scattered(sums_m[:, :pd].reshape(D, D))
        g_up = scattered(
            jnp.concatenate([sums_m[:, pd * (j + 1) : pd * (j + 2)].reshape(D, D) for j in range(FF // D)], axis=1)
        )
        g_down = scattered(sums_m[:, pd * (FF // D + 1) : last].reshape(FF, D))
        g_q, g_k, g_v = (scattered(sums[0][j]) for j in range(3))
        g_ga = jnp.sum(
            w_query.astype(f32) * g_q + w_key.astype(f32) * g_k + w_value.astype(f32) * g_v, axis=1
        ) / gain_attn.astype(f32)
        g_gm = jnp.sum(w_up.astype(f32) * g_up, axis=1) / gain_mlp.astype(f32)
        grad_in = grad_in.astype(f32)
    return (
        output.reshape(inputs.shape), grad_in.reshape(inputs.shape),
        g_q, g_k, g_v, g_out, g_up, g_down, g_ga, g_gm,
    )


def solution(mesh):
    dp, seq = mesh.shape["dp"], mesh.shape["seq"]
    nx = max(d for d in range(1, dp + 1) if dp % d == 0 and d * d <= dp)
    nc = 2 if seq % 2 == 0 else 1
    dims = (dp // nx, nx, seq // nc, nc)
    rows, vec = P(("dp", "seq"), None), P(("dp", "seq"))
    tokens = P("dp", "seq", None)
    return jax.shard_map(
        partial(body, dims),
        mesh=mesh,
        in_specs=(tokens, P("dp"), tokens) + (rows,) * 6 + (vec,) * 2,
        out_specs=(tokens, tokens) + (rows,) * 6 + (vec,) * 2,
        check_vma=False,
    )
```

```python
from functools import partial

import jax
import jax.numpy as jnp
from jax import lax
from jax.experimental import pallas as pl
from jax.experimental.pallas import tpu as pltpu
from jax.sharding import PartitionSpec as P

H = 8
HD = 64
SPAN = 128
EPS = 1e-06
K0 = 0.7978845608028654
K1 = 0.044715
FARP = 16
f32 = jnp.float32
bf = jnp.bfloat16
MESH = pl.DeviceIdType.MESH
VMEM_LIMIT = 62 << 20


def dot(a, b, ca=1, cb=0):
    return lax.dot_general(a, b, (((ca,), (cb,)), ((), ())), preferred_element_type=f32)


def sds(shape, dtype):
    return jax.ShapeDtypeStruct(shape, dtype)


def full(shape):
    return pl.BlockSpec(shape, lambda i: (0,) * len(shape), pipeline_mode=pl.Buffered(1))


def pair_diag(a):
    lane = lax.broadcasted_iota(jnp.int32, a.shape, 1)
    zero = jnp.zeros_like(a)
    return jnp.concatenate([jnp.where(lane < HD, a, zero), jnp.where(lane >= HD, a, zero)], axis=0)


def unit_rows(x_ref):
    x = x_ref[...].astype(f32)
    r = lax.rsqrt(jnp.mean(x * x, axis=1, keepdims=True) + EPS)
    return x * r, r


def causal_mask():
    j = lax.broadcasted_iota(jnp.int32, (SPAN, 2 * SPAN), 0)
    i = lax.broadcasted_iota(jnp.int32, (SPAN, 2 * SPAN), 1)
    return j <= jnp.where(i >= SPAN, i - SPAN, i)


def gain_row(slabs, which, ndev, rows):
    width = ndev * rows
    r = lax.broadcasted_iota(jnp.int32, slabs.shape, 0)
    l = lax.broadcasted_iota(jnp.int32, slabs.shape, 1)
    keep = jnp.where((r % 16 == which) & (l < rows), slabs.astype(f32), 0.0).astype(bf)
    a = lax.broadcasted_iota(jnp.int32, (128, width), 0)
    b = lax.broadcasted_iota(jnp.int32, (128, width), 1)
    spread = dot(keep, jnp.where(b % rows == a, 1.0, 0.0).astype(bf))
    d = lax.broadcasted_iota(jnp.int32, spread.shape, 0)
    c = lax.broadcasted_iota(jnp.int32, spread.shape, 1)
    return jnp.sum(jnp.where(d // 16 == c // rows, spread, 0.0), axis=0, keepdims=True)


class Place:
    def __init__(self, dims):
        self.nz, self.nx, self.ny, self.nc = dims
        dp, seq = lax.axis_index("dp"), lax.axis_index("seq")
        self.z, self.x = dp // self.nx, dp % self.nx
        self.y, self.c = seq // self.nc, seq % self.nc

    def at(self, z=None, x=None, y=None, c=None):
        z = self.z if z is None else z
        x = self.x if x is None else x
        y = self.y if y is None else y
        c = self.c if c is None else c
        return (z * self.nx + x, y * self.nc + c)

    def line(self, axis):
        return getattr(self, axis), getattr(self, "n" + axis)

    def partners(self, axis):
        me, n = self.line(axis)
        return [(o, (me + o) % n, (me + n - o) % n) for o in range(1, n)]

    def greet(self, others):
        for other in others:
            pl.semaphore_signal(pltpu.get_barrier_semaphore(), inc=1, device_id=other, device_id_type=MESH)

    def meet(self, others):
        pl.semaphore_wait(pltpu.get_barrier_semaphore(), len(others))

    def others(self):
        return [self.at(**{a: to}) for a in ("z", "x", "y", "c") for _, to, _ in self.partners(a)]


class Copies:
    def __init__(self, send_sem, recv_sem):
        self.send_sem, self.recv_sem, self.used = send_sem, recv_sem, 0

    def make(self, src, dst, landed, device):
        k = self.used
        self.used += 1
        out = pltpu.make_async_remote_copy(
            src_ref=src, dst_ref=dst, send_sem=self.send_sem.at[k], recv_sem=self.recv_sem.at[k],
            device_id=device, device_id_type=MESH,
        )
        into = pltpu.make_async_remote_copy(
            src_ref=src, dst_ref=landed, send_sem=self.send_sem.at[k], recv_sem=self.recv_sem.at[k],
            device_id=device, device_id_type=MESH,
        )
        return out, into


def start(copies):
    for out, _ in copies:
        out.start()


def finish(copies):
    for out, into in copies:
        out.wait_send()
        into.wait_recv()


def shares(rows, width):
    if rows % 32 == 0:
        return (pl.ds(0, rows // 2), slice(None)), (pl.ds(rows // 2, rows // 2), slice(None))
    return (slice(None), pl.ds(0, width // 2)), (slice(None), pl.ds(width // 2, width // 2))


def gather_phases(pc, cp, pieces, wholes, routes):
    z, x, y, c = pc.z, pc.x, pc.y, pc.c
    first, second, third, last = [], [], [], []
    for piece, whole, route in zip(pieces, wholes, routes):
        rows, width = whole.shape[-2:]
        everything = (slice(None), slice(None))
        one, two = shares(rows, width) if route == "both" else (everything, everything)
        for _, to, fr in pc.partners("z"):
            first.append(cp.make(piece, whole.at[z, x, y, c], whole.at[fr, x, y, c], pc.at(z=to)))
        for _, to, fr in pc.partners("x"):
            if route != "yx":
                v = whole.at[(slice(None), x, y, c) + one]
                second.append(cp.make(v, v, whole.at[(slice(None), fr, y, c) + one], pc.at(x=to)))
            if route != "xy":
                v = whole.at[(slice(None), x, slice(None), c) + two]
                third.append(cp.make(v, v, whole.at[(slice(None), fr, slice(None), c) + two], pc.at(x=to)))
        for _, to, fr in pc.partners("y"):
            if route != "xy":
                v = whole.at[(slice(None), x, y, c) + two]
                second.append(cp.make(v, v, whole.at[(slice(None), x, fr, c) + two], pc.at(y=to)))
            if route != "yx":
                v = whole.at[(slice(None), slice(None), y, c) + one]
                third.append(cp.make(v, v, whole.at[(slice(None), slice(None), fr, c) + one], pc.at(y=to)))
        for _, to, fr in pc.partners("c"):
            v = whole.at[:, :, :, c]
            last.append(cp.make(v, v, whole.at[:, :, :, fr], pc.at(c=to)))
    return first, second, third, last


def front_kernel(dims, slots, n_first, n_later, *refs):
    near = n_first > 0
    refs = list(refs)

    def take(n):
        out = refs[:n]
        del refs[:n]
        return out

    x_ref, ga_own, gm_own = take(3)
    pieces = take(n_first + n_later)
    w_in = [] if near else take(3)
    q_ref, k_ref, v_ref, att_ref, lse_ref, ks_ref, vs_ref, mean_ref, ga_ref, gm_ref = take(10)
    w_out = take(n_first)
    later = take(n_later)
    pack_ref, gain_ref, own_mean, all_mean, local_sem, send_sem, recv_sem = take(7)
    T, D = x_ref.shape
    spt, nseq = slots // SPAN, T // slots
    pc = Place(dims)
    cp = Copies(send_sem, recv_sem)
    seq, dp = lax.axis_index("seq"), lax.axis_index("dp")
    seqn = pc.ny * pc.nc
    spans_all, seqs = spt * seqn, all_mean.shape[1]
    ndev = pc.nz * pc.nx * seqn
    rd = D // ndev
    mine = (pc.z, pc.x, pc.y, pc.c)
    packs = [pack_ref, gain_ref] if near else [gain_ref]
    first = gather_phases(pc, cp, [p.at[mine] for p in packs], packs, ["both", "xy"][-len(packs) :])
    later_phases = gather_phases(pc, cp, pieces[n_first:], later, ["xy", "yx", "both"][:n_later])
    own_first = [
        pltpu.make_async_copy(p, pack_ref.at[mine + (pl.ds(k * rd, rd),)], local_sem.at[k])
        for k, p in enumerate(pieces[:n_first])
    ]
    own_later = [
        pltpu.make_async_copy(p, w.at[mine], local_sem.at[n_first + k])
        for k, (p, w) in enumerate(zip(pieces[n_first:], later))
    ]
    means = []
    for o in range(1, seqn):
        to, fr = (seq + o) % seqn, (seq + seqn - o) % seqn
        v = all_mean.at[pl.ds(seq * spt, spt)]
        means.append(cp.make(v, v, all_mean.at[pl.ds(fr * spt, spt)], (dp, to)))
    i, n = pl.program_id(0), pl.num_programs(0) // 2
    w_refs = w_out if near else w_in

    @pl.when(i == 0)
    def _():
        for copy in own_first + own_later:
            copy.start()
        slab = jnp.concatenate([ga_own[...], gm_own[...]], axis=0).astype(f32)[:, :128]
        if rd < 128:
            slab = jnp.concatenate([slab, jnp.zeros((2, 128 - rd), f32)], axis=1)
        gain_ref[mine] = jnp.concatenate([slab, jnp.zeros((14, 128), f32)], axis=0).astype(bf)
        seq_peers = [(dp, (seq + o) % seqn) for o in range(1, seqn)]
        zx = [pc.at(**{a: to}) for a in ("z", "x") for _, to, _ in pc.partners(a)]
        pc.greet(zx + seq_peers)
        pc.meet(zx + seq_peers)
        for copy in own_first:
            copy.wait()
        start(first[0])
        for copy in own_later:
            copy.wait()
        if near:
            start(later_phases[0])

    @pl.when(i < n)
    def _():
        xr, _ = unit_rows(x_ref)
        for s in range(T // SPAN):
            row = jnp.sum(xr[s * SPAN : (s + 1) * SPAN], axis=0, keepdims=True) * (1.0 / SPAN)
            own_mean[s % spt, pl.ds(i * nseq + s // spt, 1), :] = row

    @pl.when(i == 1)
    def _():
        finish(first[0])
        start(first[1])

    @pl.when(i == n - 1)
    def _():
        finish(first[1])
        start(first[2])
        all_mean[pl.ds(seq * spt, spt)] = own_mean[...].astype(bf)
        start(means)
        finish(first[2])
        start(first[3])
        if near:
            finish(later_phases[0])
            start(later_phases[1])
        finish(means)
        mean_ref[...] = all_mean[...]
        to = lax.broadcasted_iota(jnp.int32, (seqs * FARP, spans_all * seqs), 0)
        fr = lax.broadcasted_iota(jnp.int32, (seqs * FARP, spans_all * seqs), 1)
        order = jnp.where((to % FARP == fr // seqs) & (to // FARP == fr % seqs), 1.0, 0.0).astype(bf)
        ordered = dot(order, all_mean[...].reshape(spans_all * seqs, D))
        finish(first[3])
        slabs = gain_ref[...].reshape(ndev * 16, 128)
        ga_ref[...] = gain_row(slabs, 0, ndev, rd)
        gm_ref[...] = gain_row(slabs, 1, ndev, rd)
        for k in range(n_first):
            w_out[k][...] = pack_ref[:, :, :, :, k * rd : (k + 1) * rd, :].reshape(D, D)
        mb = (ordered * ga_ref[...]).astype(bf)
        ks_ref[...] = dot(mb, w_refs[1][...]).astype(bf).reshape(seqs, FARP, D)
        vs_ref[...] = dot(mb, w_refs[2][...]).astype(bf).reshape(seqs, FARP, D)

    if near:
        for k, at in ((2, 1), (3, 4)):

            @pl.when(i == n + at)
            def _(k=k):
                finish(later_phases[k - 1])
                start(later_phases[k])

    @pl.when(i >= n)
    def _():
        j = i - n
        xn = (unit_rows(x_ref)[0] * ga_ref[...]).astype(bf)
        sub = T // 4
        cuts = [(k, h) for k in range(3) for h in (slice(0, D // 2), slice(D // 2, D))]

        def project(b):
            rows = slice(b * sub, (b + 1) * sub)

            def part(k, h):
                y = dot(xn[rows], w_refs[k][:, h]).astype(bf)
                (q_ref, k_ref, v_ref)[k][rows, h] = (y * (HD**-0.5)).astype(bf) if k == 0 else y

            return [partial(part, k, h) for k, h in cuts]

        for work in project(0):
            work()
        each = sub // SPAN * (D // 128)
        beside = {}
        for b in range(1, 4):
            beside.update(spread_out(project(b), (b - 1) * each, b * each - 1))
        attend_forward(slots, j, seq, q_ref, k_ref, v_ref, ks_ref, vs_ref, att_ref, lse_ref, beside)

    if near:

        @pl.when(i == 2 * n - 1)
        def _():
            finish(later_phases[3])


def attend_forward(slots, j, seq, q_ref, k_ref, v_ref, ks_ref, vs_ref, att_ref, lse_ref, beside):
    T, D = q_ref.shape
    spt, nseq = slots // SPAN, T // slots
    causal = causal_mask()
    t_row = lax.broadcasted_iota(jnp.int32, (FARP, 2 * SPAN), 0)

    def where(u):
        s, p = u
        return slice(s * SPAN, (s + 1) * SPAN), slice(p * 128, (p + 1) * 128), j * nseq + s // spt

    def scores(u):
        rows, ln, sq = where(u)
        ke = jnp.concatenate([k_ref[rows, ln], ks_ref[sq, :, ln]], axis=0)
        return dot(ke, pair_diag(q_ref[rows, ln]), 1, 1)

    def weigh(u, sc):
        far = t_row < (seq * spt + u[0] % spt)
        sn = jnp.where(causal, sc[:SPAN], -1e30)
        sf = jnp.where(far, sc[SPAN:], -1e30)
        m = jnp.maximum(jnp.max(sn, axis=0, keepdims=True), jnp.max(sf, axis=0, keepdims=True))
        en = jnp.exp(sn - m)
        ef = jnp.exp(sf - m)
        l = jnp.sum(en, axis=0, keepdims=True) + jnp.sum(ef, axis=0, keepdims=True)
        return en.astype(bf), ef.astype(bf), m, l

    def combine(u, en, ef, m, l):
        rows, ln, sq = where(u)
        p = u[1]
        ve = jnp.concatenate([v_ref[rows, ln], vs_ref[sq, :, ln]], axis=0)
        at = dot(ve, jnp.concatenate([en, ef], axis=0), 0, 0) * (1.0 / l)
        att_ref[rows, ln] = jnp.concatenate([at[:HD, :SPAN], at[HD:, SPAN:]], axis=0).astype(bf).T
        total = m + jnp.log(l)
        lse_ref[2 * p : 2 * p + 1, rows] = total[:, :SPAN]
        lse_ref[2 * p + 1 : 2 * p + 2, rows] = total[:, SPAN:]

    units = [(s, p) for s in range(T // SPAN) for p in range(D // 128)]
    staged(units, scores, weigh, combine, beside)


def staged(units, first, second, third, beside=None):
    a, b = {}, {}
    for t in range(0, len(units) + 4, 2):
        for k in (t, t + 1):
            for work in (beside or {}).get(k, ()):
                work()
            if k < len(units):
                a[k] = first(units[k])
        for k in (t - 2, t - 1):
            if 0 <= k < len(units):
                b[k] = second(units[k], a.pop(k))
        for k in (t - 4, t - 3):
            if 0 <= k < len(units):
                third(units[k], *b.pop(k))


def spread_out(works, begin, end):
    out = {}
    for j, work in enumerate(works):
        out.setdefault(begin + j * (end - begin) // len(works), []).append(work)
    return out


def front_call(dims, slots, block, x, w_first, w_later, gains, near):
    n_tok, D = x.shape
    seqs, spt = n_tok // slots, slots // SPAN
    nz, nx, ny, nc = dims
    n = n_tok // block
    ndev = nz * nx * ny * nc
    spans_all = spt * ny * nc
    hbm = pl.BlockSpec(memory_space=pl.ANY)
    summ = (seqs, FARP, D)
    per_piece = (nz - 1) + 2 * (nx - 1) + 2 * (ny - 1) + (nc - 1)
    n_first, n_later = (len(w_first), len(w_later)) if near else (0, 0)
    rows = sum(w.shape[0] for w in w_first) if near else 16
    copies = (2 + n_later) * per_piece + ny * nc - 1
    late = lambda i: jnp.maximum(i - n, 0)
    tok = pl.BlockSpec((block, D), lambda i: (late(i), 0))
    in_specs = [pl.BlockSpec((block, D), lambda i: (i % n, 0)), full((1, D // ndev)), full((1, D // ndev))]
    in_specs += [hbm] * (n_first + n_later) if near else [full(w.shape) for w in w_first]
    row = sds((1, D), f32)
    return pl.pallas_call(
        partial(front_kernel, dims, slots, n_first, n_later),
        grid=(2 * n,),
        in_specs=in_specs,
        out_specs=[tok] * 4
        + [pl.BlockSpec((H, block), lambda i: (0, late(i))), full(summ), full(summ)]
        + [full((spans_all, seqs, D)), full((1, D)), full((1, D))]
        + [full((D, D))] * n_first
        + [hbm] * n_later,
        out_shape=[sds((n_tok, D), bf)] * 4
        + [sds((H, n_tok), f32), sds(summ, bf), sds(summ, bf), sds((spans_all, seqs, D), bf), row, row]
        + [sds((D, D), bf)] * n_first
        + [sds(dims + w.shape, w.dtype) for w in w_later[:n_later]],
        scratch_shapes=[
            pltpu.VMEM(dims + (rows, D), bf),
            pltpu.VMEM(dims + (16, 128), bf),
            pltpu.VMEM((spt, seqs, D), f32),
            pltpu.VMEM((spans_all, seqs, D), bf),
            pltpu.SemaphoreType.DMA((max(n_first + n_later, 1),)),
            pltpu.SemaphoreType.DMA((max(copies, 1),)),
            pltpu.SemaphoreType.DMA((max(copies, 1),)),
        ],
        compiler_params=pltpu.CompilerParams(
            vmem_limit_bytes=VMEM_LIMIT, collective_id=0, has_side_effects=True,
            dimension_semantics=("arbitrary",),
        ),
    )(x, *gains, *w_first, *w_later)


def mlp_kernel(chunk, slots, ndev, len_ref, x_ref, att_ref, cot_ref, wo_ref, wu_ref, wd_ref, gm_ref,
               out_ref, datt_ref, dmid_ref, gsum_ref, adown, aup, aout):
    T, D = x_ref.shape
    FF = wu_ref.shape[1]
    i, n = pl.program_id(0), pl.num_programs(0)

    @pl.when(i == 0)
    def _():
        for acc in (adown, aup, aout):
            acc[...] = jnp.zeros_like(acc)

    att = att_ref[...]
    mid = x_ref[...].astype(f32) + dot(att, wo_ref[...])
    r = lax.rsqrt(jnp.mean(mid * mid, axis=1, keepdims=True) + EPS)
    gm = gm_ref[...]
    hn = (mid * r * gm).astype(bf)
    nseq = T // slots
    row = lax.broadcasted_iota(jnp.int32, (slots, 1), 0) + lax.axis_index("seq") * slots
    valid = jnp.concatenate(
        [jnp.where(row < len_ref[i * nseq + s], 1.0, 0.0) for s in range(nseq)], axis=0
    )
    g = cot_ref[...].astype(f32) * valid
    gb = g.astype(bf)
    gbt = gb.T
    hnt = hn.T
    y = jnp.zeros((T, D), f32)
    dhn = jnp.zeros((T, D), f32)
    cols = [slice(j * chunk, (j + 1) * chunk) for j in range(FF // chunk)]

    def products(sl):
        return dot(hn, wu_ref[:, sl]), dot(gb, wd_ref[sl, :], 1, 1)

    ready = products(cols[0])
    for j, sl in enumerate(cols):
        u, da = ready
        if j + 1 < len(cols):
            ready = products(cols[j + 1])
        h = 0.5 + 0.5 * jnp.tanh(u * (K0 + (K0 * K1) * (u * u)))
        act = (u * h).astype(bf)
        ub, hb = u.astype(bf), h.astype(bf)
        slope = hb + (ub * (bf(K0) + bf(3 * K0 * K1) * (ub * ub))) * ((hb + hb) * (bf(1.0) - hb))
        du = da.astype(bf) * slope
        y = y + dot(act, wd_ref[sl, :])
        dhn = dhn + dot(du, wu_ref[:, sl], 1, 1)
        adown[:, sl] += dot(gbt, act)
        aup[:, sl] += dot(hnt, du)
    out_ref[...] = ((mid + y) * valid).astype(bf)
    mr = mid * r
    gd = dhn * gm
    coef = jnp.mean(gd * mr, axis=1, keepdims=True)
    db = (g + r * (gd - mr * coef)).astype(bf)
    dmid_ref[...] = db
    aout[...] += dot(att, db, 0, 0)
    datt_ref[...] = dot(db, wo_ref[...], 1, 1).astype(bf)

    @pl.when(i == n - 1)
    def _():
        rd, rf = D // ndev, FF // ndev
        gsum_ref[:, :rd, :] = aout[...].reshape(ndev, rd, D).astype(bf)
        for j in range(FF // D):
            gsum_ref[:, rd * (j + 1) : rd * (j + 2), :] = (
                aup[:, j * D : (j + 1) * D].reshape(ndev, rd, D).astype(bf)
            )
            part = adown[:, j * D : (j + 1) * D].T.astype(bf)
            nd = D // rf
            gsum_ref[j * nd : (j + 1) * nd, rd * (FF // D + 1) : rd * (FF // D + 1) + rf, :] = part.reshape(
                nd, rf, D
            )


def mlp_call(chunk, slots, block, ndev, lens, x, att, cot, wo, wu, wd, gm):
    n_tok, D = x.shape
    FF = wu.shape[1]
    tok = pl.BlockSpec((block, D), lambda i: (i, 0))
    rows = D // ndev * (FF // D + 1) + FF // ndev
    return pl.pallas_call(
        partial(mlp_kernel, chunk, slots, ndev),
        grid=(n_tok // block,),
        in_specs=[pl.BlockSpec(memory_space=pltpu.SMEM), tok, tok, tok]
        + [full((D, D)), full((D, FF)), full((FF, D)), full((1, D))],
        out_specs=[tok, tok, tok, full((ndev, rows, D))],
        out_shape=[sds((n_tok, D), bf)] * 3 + [sds((ndev, rows, D), bf)],
        scratch_shapes=[pltpu.VMEM((D, FF), f32), pltpu.VMEM((D, FF), f32), pltpu.VMEM((D, D), f32)],
        compiler_params=pltpu.CompilerParams(
            vmem_limit_bytes=VMEM_LIMIT, dimension_semantics=("arbitrary",)
        ),
    )(lens, x, att, cot, wo, wu, wd, gm)


class Scatter:
    @staticmethod
    def scratch(dims, rows, width):
        nz, nx, ny, nc = dims
        most = max(nx, ny)
        half = (rows // 2, width) if rows % 32 == 0 else (rows, width // 2)
        return [
            pltpu.VMEM((nc - 1, nz, nx, ny, rows, width), bf),
            pltpu.VMEM((nz, nx, ny, rows, width), bf),
            pltpu.VMEM((nx - 1, nz, ny) + half, bf),
            pltpu.VMEM((ny - 1, nz, nx) + half, bf),
            pltpu.VMEM((2, nz, most) + half, bf),
            pltpu.VMEM((ny - 1, nz) + half, bf),
            pltpu.VMEM((nx - 1, nz) + half, bf),
            pltpu.VMEM((nz, rows, width), bf),
            pltpu.VMEM((nz - 1, rows, width), bf),
        ]

    @staticmethod
    def copies(dims):
        nz, nx, ny, nc = dims
        return (nc - 1) + 2 * (nx - 1) + 2 * (ny - 1) + (nz - 1)

    def __init__(self, pc, cp, g, mine, out, scratch):
        self.pc, self.mine, self.out, self.bufs = pc, mine, out, scratch
        got1, held1, got2a, got2b, held2, got3a, got3b, held3, got4 = scratch
        a, b = self.a, self.b = shares(*g.shape[-2:])
        every = slice(None)
        self.one = [
            cp.make(g.at[:, :, :, to], got1.at[o - 1], got1.at[o - 1], pc.at(c=to))
            for o, to, _ in pc.partners("c")
        ]
        self.two = [
            cp.make(held1.at[(every, to, every) + a], got2a.at[o - 1], got2a.at[o - 1], pc.at(x=to))
            for o, to, _ in pc.partners("x")
        ] + [
            cp.make(held1.at[(every, every, to) + b], got2b.at[o - 1], got2b.at[o - 1], pc.at(y=to))
            for o, to, _ in pc.partners("y")
        ]
        self.three = [
            cp.make(held2.at[0, :, to], got3a.at[o - 1], got3a.at[o - 1], pc.at(y=to))
            for o, to, _ in pc.partners("y")
        ] + [
            cp.make(held2.at[1, :, to], got3b.at[o - 1], got3b.at[o - 1], pc.at(x=to))
            for o, to, _ in pc.partners("x")
        ]
        self.four = [
            cp.make(held3.at[to], got4.at[o - 1], got4.at[o - 1], pc.at(z=to)) for o, to, _ in pc.partners("z")
        ]

    @staticmethod
    def total(acc, got, n):
        if n == 2:
            return acc + got[0]
        acc = acc.astype(f32)
        for o in range(n - 1):
            acc = acc + got[o].astype(f32)
        return acc

    def step(self, k):
        pc = self.pc
        got1, held1, got2a, got2b, held2, got3a, got3b, held3, got4 = self.bufs
        every = slice(None)
        if k == 0:
            start(self.one)
        elif k == 1:
            finish(self.one)
            for z in range(pc.nz):
                for x in range(pc.nx):
                    acc = self.mine(z, x)
                    for o in range(pc.nc - 1):
                        acc = acc + got1[o, z, x]
                    held1[z, x] = acc
            start(self.two)
        elif k == 2:
            finish(self.two)
            held2[0, :, : pc.ny] = self.total(held1[(every, pc.x, every) + self.a], got2a, pc.nx).astype(bf)
            held2[1, :, : pc.nx] = self.total(held1[(every, every, pc.y) + self.b], got2b, pc.ny).astype(bf)
            start(self.three)
        elif k == 3:
            finish(self.three)
            held3[(every,) + self.a] = self.total(held2[0, :, pc.y], got3a, pc.ny).astype(bf)
            held3[(every,) + self.b] = self.total(held2[1, :, pc.x], got3b, pc.nx).astype(bf)
            start(self.four)
        else:
            finish(self.four)
            self.out[...] = self.total(held3[pc.z], got4, pc.nz).astype(f32)


def back_kernel(dims, slots, pack, near, *refs):
    refs = list(refs)

    def take(n):
        out = refs[:n]
        del refs[:n]
        return out

    x_ref, q_ref, k_ref, v_ref, da_ref, lse_ref, dmid_ref, mean_ref, ks_ref, vs_ref = take(10)
    wq_ref, wk_ref, wv_ref, ga_ref = take(4)
    (g1_ref,) = take(1) if near else (None,)
    (din_ref,) = take(1)
    outs = take(2 if near else 1)
    aq, ak, av, dq_ref, dk_ref, dv_ref, dks_ref, dvs_ref, far_ref = take(9)
    far_send, far_got = take(2), take(2)
    if near:
        (g2_ref, own1) = take(2)
        bufs1, bufs2 = take(9), take(9)
        (own_sem,) = take(1)
    send_sem, recv_sem = take(2)
    T, D = x_ref.shape
    spt, nseq = slots // SPAN, T // slots
    pc = Place(dims)
    cp = Copies(send_sem, recv_sem)
    seq, dp = lax.axis_index("seq"), lax.axis_index("dp")
    seqn = pc.ny * pc.nc
    spans_all, seqs, _ = mean_ref.shape
    i, n = pl.program_id(0), pl.num_programs(0) // 2
    far = []
    for send, got in zip(far_send, far_got):
        far.append([])
        for o in range(1, seqn):
            to = (seq + o) % seqn
            far[-1].append(cp.make(send.at[:, pl.ds(to * spt, spt)], got.at[o - 1], got.at[o - 1], (dp, to)))
    if near:
        own_copy = pltpu.make_async_copy(g1_ref.at[:, :, :, pc.c], own1, own_sem.at[0])
        big = Scatter(pc, cp, g1_ref, lambda z, x: own1[z, x], outs[0], bufs1)
        small = Scatter(pc, cp, g2_ref, lambda z, x: g2_ref[z, x, :, pc.c], outs[1], bufs2)

    seq_peers = [(dp, (seq + o) % seqn) for o in range(1, seqn)]
    zx = [pc.at(**{a: to}) for a in ("z", "x") for _, to, _ in pc.partners(a)]

    @pl.when(i == 0)
    def _():
        pc.greet(zx + seq_peers)
        if near:
            own_copy.start()
        for acc in (aq, ak, av):
            acc[...] = jnp.zeros_like(acc)
        pc.meet(zx + seq_peers)
        if near:
            big.step(0)
            own_copy.wait()

    if near:
        for k, at in ((1, 1), (2, n // 2), (3, n - 1), (4, n + n // 3)):

            @pl.when(i == at)
            def _(k=k):
                big.step(k)

    ga = ga_ref[...]

    groups = ((0, seqs - nseq), (seqs - nseq, seqs))

    def send_far(g):
        lo, hi = groups[g]
        for t in range(spans_all):
            far_send[g][0, t] = dks_ref[lo:hi, t, :].astype(bf)
            far_send[g][1, t] = dvs_ref[lo:hi, t, :].astype(bf)
        start(far[g])

    @pl.when(i == n - 1)
    def _():
        send_far(0)

    @pl.when(i < n)
    def _():
        tok = pl.ds(pl.multiple_of(i * T, T), T)
        sub = T // 1
        xt = (unit_rows(x_ref)[0] * ga).astype(bf).T
        cuts = [(k, h) for k in range(3) for h in (slice(0, D // 2), slice(D // 2, D))]

        def gather_terms(b):
            rows = pl.ds(pl.multiple_of(i * T + b * sub, sub), sub)

            def part(k, h):
                (aq, ak, av)[k][:, h] += dot(xt[:, b * sub : (b + 1) * sub], (dq_ref, dk_ref, dv_ref)[k][rows, h])

            return [partial(part, k, h) for k, h in cuts]

        each = sub // SPAN * (D // 128)
        beside = {}
        for b in range(1 - 1):
            beside.update(spread_out(gather_terms(b), (b + 1) * each + 4, (b + 2) * each + 4))
        attend_backward(slots, i, seq, spans_all, q_ref, k_ref, v_ref, da_ref, ks_ref, vs_ref, lse_ref,
                        dq_ref.at[tok], dk_ref.at[tok], dv_ref.at[tok], dks_ref, dvs_ref, beside)
        for work in gather_terms(1 - 1):
            work()

    @pl.when(i == n - 1)
    def _():
        send_far(1)
        mean = mean_ref[...].astype(f32)
        terms = [jnp.zeros((D, D), f32)] * 2
        for g, (lo, hi) in enumerate(groups):
            mb = (mean[:, lo:hi].reshape(spans_all * (hi - lo), D) * ga).astype(bf)
            for h in range(2):
                terms[h] = terms[h] + dot(mb, far_send[g][h].reshape(spans_all * (hi - lo), D), 0, 0)
        rows = D // pack
        parts = (aq[...], ak[...] + terms[0], av[...] + terms[1])
        for j, part in enumerate(parts):
            if near:
                g2_ref[:, :, :, :, j * rows : (j + 1) * rows, :] = part.astype(bf).reshape(dims + (rows, D))
            else:
                outs[0][j] = part
        if near:
            small.step(0)

    def products(j):
        tok = pl.ds(pl.multiple_of(j * T, T), T)
        dxn = dot(dq_ref[tok, :], wq_ref[...], 1, 1)
        dxn = dxn + dot(dk_ref[tok, :], wk_ref[...], 1, 1)
        return dxn + dot(dv_ref[tok, :], wv_ref[...], 1, 1)

    def to_input(j, dxn):
        parts = []
        for s in range(T // SPAN):
            row = far_ref[s % spt, pl.ds(j * nseq + s // spt, 1), :]
            parts.append(dxn[s * SPAN : (s + 1) * SPAN] + row)
        gd = jnp.concatenate(parts, axis=0) * ga
        xr, r = unit_rows(x_ref)
        coef = jnp.mean(gd * xr, axis=1, keepdims=True)
        din_ref[...] = (dmid_ref[...].astype(f32) + r * (gd - xr * coef)).astype(bf)

    @pl.when(i == n)
    def _():
        dxn = products(0)
        for g, (lo, hi) in enumerate(groups):
            finish(far[g])
            tot = []
            for h in range(2):
                acc = far_send[g][h, pl.ds(seq * spt, spt)].astype(f32)
                for o in range(seqn - 1):
                    acc = acc + far_got[g][o, h].astype(f32)
                tot.append(acc.astype(bf).reshape(spt * (hi - lo), D))
            rows = dot(tot[0], wk_ref[...], 1, 1) + dot(tot[1], wv_ref[...], 1, 1)
            far_ref[:, lo:hi, :] = (rows * (1.0 / SPAN)).reshape(spt, hi - lo, D)
        to_input(0, dxn)

    if near:
        for k, at in ((1, 1), (2, n // 2), (3, 2 * n // 3)):

            @pl.when(i == n + at)
            def _(k=k):
                small.step(k)

    @pl.when(i > n)
    def _():
        to_input(i - n, products(i - n))

    if near:

        @pl.when(i == 2 * n - 1)
        def _():
            small.step(4)


def attend_backward(slots, i, seq, spans_all, q_ref, k_ref, v_ref, da_ref, ks_ref, vs_ref, lse_ref,
                    dq_ref, dk_ref, dv_ref, dks_ref, dvs_ref, beside):
    T, D = q_ref.shape
    spt, nseq = slots // SPAN, T // slots
    causal = causal_mask()
    t_row = lax.broadcasted_iota(jnp.int32, (FARP, 2 * SPAN), 0)

    def where(u):
        s, p = u
        return slice(s * SPAN, (s + 1) * SPAN), slice(p * 128, (p + 1) * 128), i * nseq + s // spt

    def scores(u):
        rows, ln, sq = where(u)
        ke = jnp.concatenate([k_ref[rows, ln], ks_ref[sq, :, ln]], axis=0)
        ve = jnp.concatenate([v_ref[rows, ln], vs_ref[sq, :, ln]], axis=0)
        qbd, dbd = pair_diag(q_ref[rows, ln]), pair_diag(da_ref[rows, ln])
        return dot(ke, qbd, 1, 1), dot(ve, dbd, 1, 1)

    def weigh(u, got):
        sc, dp = got
        rows, p = where(u)[0], u[1]
        far = t_row < (seq * spt + u[0] % spt)
        lse = jnp.concatenate([lse_ref[2 * p : 2 * p + 1, rows], lse_ref[2 * p + 1 : 2 * p + 2, rows]], axis=1)
        pn = jnp.where(causal, jnp.exp(sc[:SPAN] - lse), 0.0)
        pf = jnp.where(far, jnp.exp(sc[SPAN:] - lse), 0.0)
        dpn, dpf = dp[:SPAN], dp[SPAN:]
        delta = jnp.sum(pn * dpn, axis=0, keepdims=True) + jnp.sum(pf * dpf, axis=0, keepdims=True)
        dsn, dsf = (pn * (dpn - delta)).astype(bf), (pf * (dpf - delta)).astype(bf)
        return pn.astype(bf), pf.astype(bf), dsn, dsf

    def combine(u, pn, pf, dsn, dsf):
        rows, ln, sq = where(u)
        qbd, dbd = pair_diag(q_ref[rows, ln]), pair_diag(da_ref[rows, ln])
        dv = dot(jnp.concatenate([pn, pf], axis=0), dbd)
        ds = jnp.concatenate([dsn, dsf], axis=0)
        dk = dot(ds, qbd)
        ke = jnp.concatenate([k_ref[rows, ln], ks_ref[sq, :, ln]], axis=0)
        dq = dot(ke, ds, 0, 0)
        dq = jnp.concatenate([dq[:HD, :SPAN], dq[HD:, SPAN:]], axis=0) * (HD**-0.5)
        dq_ref[rows, ln] = dq.astype(bf).T
        dk_ref[rows, ln] = dk[:SPAN].astype(bf)
        dv_ref[rows, ln] = dv[:SPAN].astype(bf)
        fk, fv = dk[SPAN : SPAN + spans_all], dv[SPAN : SPAN + spans_all]
        if u[0] % spt == 0:
            dks_ref[sq, :, ln] = fk
            dvs_ref[sq, :, ln] = fv
        else:
            dks_ref[sq, :, ln] += fk
            dvs_ref[sq, :, ln] += fv

    units = [(s, p) for s in range(T // SPAN) for p in range(D // 128)]
    staged(units, scores, weigh, combine, beside)


def back_call(dims, slots, block, pack, near, x, q, k, v, da, lse, dmid, mean, ks, vs, wq, wk, wv, ga, g1):
    n_tok, D = x.shape
    nz, nx, ny, nc = dims
    n = n_tok // block
    spt, nseq = slots // SPAN, block // slots
    spans_all, seqs, _ = mean.shape
    seqn = ny * nc
    vm = pltpu.VMEM
    early = pl.BlockSpec((block, D), lambda i: (jnp.minimum(i, n - 1), 0))
    late = pl.BlockSpec((block, D), lambda i: (jnp.maximum(i - n, 0), 0))
    rows2 = D // pack * 3
    in_specs = (
        [pl.BlockSpec((block, D), lambda i: (i % n, 0))]
        + [early] * 4
        + [pl.BlockSpec((H, block), lambda i: (0, jnp.minimum(i, n - 1))), late]
        + [full(mean.shape), full(ks.shape), full(vs.shape)]
        + [full((D, D))] * 3
        + [full((1, D))]
    )
    args = [x, q, k, v, da, lse, dmid, mean, ks, vs, wq, wk, wv, ga]
    out_specs, out_shape = [late], [sds((n_tok, D), bf)]
    scratch = [vm((D, D), f32)] * 3 + [vm((n_tok, D), bf)] * 3 + [vm((seqs, spans_all, D), f32)] * 2
    scratch += [
        vm((spt, seqs, D), f32),
        vm((2, spans_all, seqs - nseq, D), bf),
        vm((2, spans_all, nseq, D), bf),
        vm((max(seqn - 1, 1), 2, spt, seqs - nseq, D), bf),
        vm((max(seqn - 1, 1), 2, spt, nseq, D), bf),
    ]
    copies = 2 * (seqn - 1)
    if near:
        rows1 = g1.shape[1]
        args.append(g1.reshape(dims + g1.shape[1:]))
        in_specs.append(pl.BlockSpec(memory_space=pl.ANY))
        out_specs += [full((rows1, D)), full((rows2, D))]
        out_shape += [sds((rows1, D), f32), sds((rows2, D), f32)]
        scratch += [vm(dims + (rows2, D), bf), vm((nz, nx, ny, rows1, D), bf)]
        scratch += Scatter.scratch(dims, rows1, D) + Scatter.scratch(dims, rows2, D)
        scratch.append(pltpu.SemaphoreType.DMA((1,)))
        copies += 2 * Scatter.copies(dims)
    else:
        out_specs.append(full((3, D, D)))
        out_shape.append(sds((3, D, D), f32))
    scratch += [pltpu.SemaphoreType.DMA((max(copies, 1),))] * 2
    return pl.pallas_call(
        partial(back_kernel, dims, slots, pack, near),
        grid=(2 * n,),
        in_specs=in_specs,
        out_specs=out_specs,
        out_shape=out_shape,
        scratch_shapes=scratch,
        compiler_params=pltpu.CompilerParams(
            vmem_limit_bytes=VMEM_LIMIT, collective_id=1, has_side_effects=True,
            dimension_semantics=("arbitrary",),
        ),
    )(*args)


def last_kernel(rd, rf, din_ref, m_ref, a_ref, wq_ref, wk_ref, wv_ref, wu_ref, ga_ref, gm_ref,
                out_ref, gq_ref, gk_ref, gv_ref, go_ref, gu_ref, gd_ref, gga_ref, ggm_ref):
    out_ref[...] = din_ref[...].astype(f32)
    D = out_ref.shape[1]
    FF = gu_ref.shape[1]

    @pl.when(pl.program_id(0) == 0)
    def _():
        attn = jnp.zeros((rd, 1), f32)
        for j, (w_ref, g_ref) in enumerate(((wq_ref, gq_ref), (wk_ref, gk_ref), (wv_ref, gv_ref))):
            g = a_ref[j * rd : (j + 1) * rd, :]
            g_ref[...] = g
            attn = attn + jnp.sum(g * w_ref[...].astype(f32), axis=1, keepdims=True)
        go_ref[...] = m_ref[:rd, :]
        up = jnp.zeros((rd, 1), f32)
        for j in range(FF // D):
            g = m_ref[rd * (j + 1) : rd * (j + 2), :]
            gu_ref[:, j * D : (j + 1) * D] = g
            up = up + jnp.sum(g * wu_ref[:, j * D : (j + 1) * D].astype(f32), axis=1, keepdims=True)
        gd_ref[...] = m_ref[rd * (FF // D + 1) :, :]
        for total, gain, out in ((attn, ga_ref, gga_ref), (up, gm_ref, ggm_ref)):
            row = jnp.broadcast_to(total, (rd, 128)).T[:1, :]
            out[...] = row[:, :rd] / gain[...].astype(f32)


def last_call(block, din, sums_m, sums_a, wq, wk, wv, wu, ga, gm):
    n_tok, D = din.shape
    rd, FF = wu.shape
    rf = sums_m.shape[0] - rd * (FF // D + 1)
    tok = pl.BlockSpec((block, D), lambda i: (i, 0))
    args = [sums_m, sums_a, wq, wk, wv, wu, ga, gm]
    shapes = [(rd, D)] * 4 + [(rd, FF), (rf, D), (1, rd), (1, rd)]
    return pl.pallas_call(
        partial(last_kernel, rd, rf),
        grid=(n_tok // block,),
        in_specs=[tok] + [full(a.shape) for a in args],
        out_specs=[tok] + [full(s) for s in shapes],
        out_shape=[sds((n_tok, D), f32)] + [sds(s, f32) for s in shapes],
        compiler_params=pltpu.CompilerParams(
            vmem_limit_bytes=VMEM_LIMIT, dimension_semantics=("arbitrary",)
        ),
    )(din, *args)


def body(dims, inputs, lengths, cotangent, w_query, w_key, w_value, w_out, w_up, w_down, gain_attn, gain_mlp):
    seqs, slots, D = inputs.shape
    nz, nx, ny, nc = dims
    ndev = nz * nx * ny * nc
    FF = w_up.shape[1]
    rd, rf = w_query.shape[0], w_down.shape[0]
    n_tok = seqs * slots
    block = 1024
    x = inputs.reshape(n_tok, D)
    cot = cotangent.reshape(n_tok, D)
    gains = [g.reshape(1, rd) for g in (gain_attn, gain_mlp)]
    everyone = ("dp", "seq")
    near = rd % 16 == 0 and n_tok // block >= 6
    if near:
        w_first, w_later = (w_query, w_key, w_value), (w_up, w_down, w_out)
    else:
        wq, wk, wv, wu, wd, wo = (
            lax.all_gather(w, everyone, axis=0, tiled=True)
            for w in (w_query, w_key, w_value, w_up, w_down, w_out)
        )
        w_first, w_later = (wq, wk, wv), ()
    q, k, v, att, lse, ks, vs, mean, ga, gm, *later = front_call(dims, slots, block, x, w_first, w_later, gains, near)
    if near:
        wq, wk, wv, wu, wd, wo = (w.reshape(-1, w.shape[-1]) for w in later)
    pack = ndev if near else 32
    output, datt, dmid, sums_m = mlp_call(512, slots, block, pack, lengths, x, att, cot, wo, wu, wd, gm)
    grad_in, *sums = back_call(
        dims, slots, block, pack, near, x, q, k, v, datt, lse, dmid, mean, ks, vs, wq, wk, wv, ga, sums_m
    )
    if near:
        grad_in, g_q, g_k, g_v, g_out, g_up, g_down, g_ga, g_gm = last_call(
            n_tok // 3, grad_in, *sums, w_query, w_key, w_value, w_up, *gains
        )
        g_ga, g_gm = g_ga.reshape(rd), g_gm.reshape(rd)
    else:
        pd, pf = D // pack, FF // pack
        last = pd * (FF // D + 1) + pf

        def scattered(a):
            return lax.psum_scatter(a.astype(f32), everyone, scatter_dimension=0, tiled=True)

        g_out = scattered(sums_m[:, :pd].reshape(D, D))
        g_up = scattered(
            jnp.concatenate([sums_m[:, pd * (j + 1) : pd * (j + 2)].reshape(D, D) for j in range(FF // D)], axis=1)
        )
        g_down = scattered(sums_m[:, pd * (FF // D + 1) : last].reshape(FF, D))
        g_q, g_k, g_v = (scattered(sums[0][j]) for j in range(3))
        g_ga = jnp.sum(
            w_query.astype(f32) * g_q + w_key.astype(f32) * g_k + w_value.astype(f32) * g_v, axis=1
        ) / gain_attn.astype(f32)
        g_gm = jnp.sum(w_up.astype(f32) * g_up, axis=1) / gain_mlp.astype(f32)
        grad_in = grad_in.astype(f32)
    return (
        output.reshape(inputs.shape), grad_in.reshape(inputs.shape),
        g_q, g_k, g_v, g_out, g_up, g_down, g_ga, g_gm,
    )


def solution(mesh):
    dp, seq = mesh.shape["dp"], mesh.shape["seq"]
    nx = max(d for d in range(1, dp + 1) if dp % d == 0 and d * d <= dp)
    nc = 2 if seq % 2 == 0 else 1
    dims = (dp // nx, nx, seq // nc, nc)
    rows, vec = P(("dp", "seq"), None), P(("dp", "seq"))
    tokens = P("dp", "seq", None)
    return jax.shard_map(
        partial(body, dims),
        mesh=mesh,
        in_specs=(tokens, P("dp"), tokens) + (rows,) * 6 + (vec,) * 2,
        out_specs=(tokens, tokens) + (rows,) * 6 + (vec,) * 2,
        check_vma=False,
    )
```

```python
from functools import partial

import jax
import jax.numpy as jnp
from jax import lax
from jax.experimental import pallas as pl
from jax.experimental.pallas import tpu as pltpu
from jax.sharding import PartitionSpec as P

H = 8
HD = 64
SPAN = 128
EPS = 1e-06
K0 = 0.7978845608028654
K1 = 0.044715
FARP = 8
f32 = jnp.float32
bf = jnp.bfloat16
MESH = pl.DeviceIdType.MESH
VMEM_LIMIT = 62 << 20


def dot(a, b, ca=1, cb=0):
    return lax.dot_general(a, b, (((ca,), (cb,)), ((), ())), preferred_element_type=f32)


def sds(shape, dtype):
    return jax.ShapeDtypeStruct(shape, dtype)


def full(shape):
    return pl.BlockSpec(shape, lambda i: (0,) * len(shape), pipeline_mode=pl.Buffered(1))


def pair_diag(a):
    lane = lax.broadcasted_iota(jnp.int32, a.shape, 1)
    zero = jnp.zeros_like(a)
    return jnp.concatenate([jnp.where(lane < HD, a, zero), jnp.where(lane >= HD, a, zero)], axis=0)


def unit_rows(x_ref):
    x = x_ref[...].astype(f32)
    r = lax.rsqrt(jnp.mean(x * x, axis=1, keepdims=True) + EPS)
    return x * r, r


def causal_mask():
    j = lax.broadcasted_iota(jnp.int32, (SPAN, 2 * SPAN), 0)
    i = lax.broadcasted_iota(jnp.int32, (SPAN, 2 * SPAN), 1)
    return j <= jnp.where(i >= SPAN, i - SPAN, i)


def gain_row(slabs, which, ndev, rows):
    width = ndev * rows
    r = lax.broadcasted_iota(jnp.int32, slabs.shape, 0)
    l = lax.broadcasted_iota(jnp.int32, slabs.shape, 1)
    keep = jnp.where((r % 16 == which) & (l < rows), slabs.astype(f32), 0.0).astype(bf)
    a = lax.broadcasted_iota(jnp.int32, (128, width), 0)
    b = lax.broadcasted_iota(jnp.int32, (128, width), 1)
    spread = dot(keep, jnp.where(b % rows == a, 1.0, 0.0).astype(bf))
    d = lax.broadcasted_iota(jnp.int32, spread.shape, 0)
    c = lax.broadcasted_iota(jnp.int32, spread.shape, 1)
    return jnp.sum(jnp.where(d // 16 == c // rows, spread, 0.0), axis=0, keepdims=True)


class Place:
    def __init__(self, dims):
        self.nz, self.nx, self.ny, self.nc = dims
        dp, seq = lax.axis_index("dp"), lax.axis_index("seq")
        self.z, self.x = dp // self.nx, dp % self.nx
        self.y, self.c = seq // self.nc, seq % self.nc

    def at(self, z=None, x=None, y=None, c=None):
        z = self.z if z is None else z
        x = self.x if x is None else x
        y = self.y if y is None else y
        c = self.c if c is None else c
        return (z * self.nx + x, y * self.nc + c)

    def line(self, axis):
        return getattr(self, axis), getattr(self, "n" + axis)

    def partners(self, axis):
        me, n = self.line(axis)
        return [(o, (me + o) % n, (me + n - o) % n) for o in range(1, n)]

    def greet(self, others):
        for other in others:
            pl.semaphore_signal(pltpu.get_barrier_semaphore(), inc=1, device_id=other, device_id_type=MESH)

    def meet(self, others):
        pl.semaphore_wait(pltpu.get_barrier_semaphore(), len(others))

    def others(self):
        return [self.at(**{a: to}) for a in ("z", "x", "y", "c") for _, to, _ in self.partners(a)]


class Copies:
    def __init__(self, send_sem, recv_sem):
        self.send_sem, self.recv_sem, self.used = send_sem, recv_sem, 0

    def make(self, src, dst, landed, device):
        k = self.used
        self.used += 1
        out = pltpu.make_async_remote_copy(
            src_ref=src, dst_ref=dst, send_sem=self.send_sem.at[k], recv_sem=self.recv_sem.at[k],
            device_id=device, device_id_type=MESH,
        )
        into = pltpu.make_async_remote_copy(
            src_ref=src, dst_ref=landed, send_sem=self.send_sem.at[k], recv_sem=self.recv_sem.at[k],
            device_id=device, device_id_type=MESH,
        )
        return out, into


def start(copies):
    for out, _ in copies:
        out.start()


def finish(copies):
    for out, into in copies:
        out.wait_send()
        into.wait_recv()


def shares(rows, width):
    if rows % 32 == 0:
        return (pl.ds(0, rows // 2), slice(None)), (pl.ds(rows // 2, rows // 2), slice(None))
    return (slice(None), pl.ds(0, width // 2)), (slice(None), pl.ds(width // 2, width // 2))


def gather_phases(pc, cp, pieces, wholes, routes):
    z, x, y, c = pc.z, pc.x, pc.y, pc.c
    first, second, third, last = [], [], [], []
    for piece, whole, route in zip(pieces, wholes, routes):
        rows, width = whole.shape[-2:]
        everything = (slice(None), slice(None))
        one, two = shares(rows, width) if route == "both" else (everything, everything)
        for _, to, fr in pc.partners("z"):
            first.append(cp.make(piece, whole.at[z, x, y, c], whole.at[fr, x, y, c], pc.at(z=to)))
        for _, to, fr in pc.partners("x"):
            if route != "yx":
                v = whole.at[(slice(None), x, y, c) + one]
                second.append(cp.make(v, v, whole.at[(slice(None), fr, y, c) + one], pc.at(x=to)))
            if route != "xy":
                v = whole.at[(slice(None), x, slice(None), c) + two]
                third.append(cp.make(v, v, whole.at[(slice(None), fr, slice(None), c) + two], pc.at(x=to)))
        for _, to, fr in pc.partners("y"):
            if route != "xy":
                v = whole.at[(slice(None), x, y, c) + two]
                second.append(cp.make(v, v, whole.at[(slice(None), x, fr, c) + two], pc.at(y=to)))
            if route != "yx":
                v = whole.at[(slice(None), slice(None), y, c) + one]
                third.append(cp.make(v, v, whole.at[(slice(None), slice(None), fr, c) + one], pc.at(y=to)))
        for _, to, fr in pc.partners("c"):
            v = whole.at[:, :, :, c]
            last.append(cp.make(v, v, whole.at[:, :, :, fr], pc.at(c=to)))
    return first, second, third, last


def front_kernel(dims, slots, n_first, n_later, *refs):
    near = n_first > 0
    refs = list(refs)

    def take(n):
        out = refs[:n]
        del refs[:n]
        return out

    x_ref, ga_own, gm_own = take(3)
    pieces = take(n_first + n_later)
    w_in = [] if near else take(3)
    q_ref, k_ref, v_ref, att_ref, lse_ref, ks_ref, vs_ref, mean_ref, ga_ref, gm_ref = take(10)
    w_out = take(n_first)
    later = take(n_later)
    pack_ref, gain_ref, own_mean, all_mean, local_sem, send_sem, recv_sem = take(7)
    T, D = x_ref.shape
    spt, nseq = slots // SPAN, T // slots
    pc = Place(dims)
    cp = Copies(send_sem, recv_sem)
    seq, dp = lax.axis_index("seq"), lax.axis_index("dp")
    seqn = pc.ny * pc.nc
    spans_all, seqs = spt * seqn, all_mean.shape[1]
    ndev = pc.nz * pc.nx * seqn
    rd = D // ndev
    mine = (pc.z, pc.x, pc.y, pc.c)
    packs = [pack_ref, gain_ref] if near else [gain_ref]
    first = gather_phases(pc, cp, [p.at[mine] for p in packs], packs, ["both", "xy"][-len(packs) :])
    later_phases = gather_phases(pc, cp, pieces[n_first:], later, ["xy", "yx", "both"][:n_later])
    own_first = [
        pltpu.make_async_copy(p, pack_ref.at[mine + (pl.ds(k * rd, rd),)], local_sem.at[k])
        for k, p in enumerate(pieces[:n_first])
    ]
    own_later = [
        pltpu.make_async_copy(p, w.at[mine], local_sem.at[n_first + k])
        for k, (p, w) in enumerate(zip(pieces[n_first:], later))
    ]
    means = []
    for o in range(1, seqn):
        to, fr = (seq + o) % seqn, (seq + seqn - o) % seqn
        v = all_mean.at[pl.ds(seq * spt, spt)]
        means.append(cp.make(v, v, all_mean.at[pl.ds(fr * spt, spt)], (dp, to)))
    i, n = pl.program_id(0), pl.num_programs(0) // 2
    w_refs = w_out if near else w_in

    @pl.when(i == 0)
    def _():
        for copy in own_first + own_later:
            copy.start()
        slab = jnp.concatenate([ga_own[...], gm_own[...]], axis=0).astype(f32)[:, :128]
        if rd < 128:
            slab = jnp.concatenate([slab, jnp.zeros((2, 128 - rd), f32)], axis=1)
        gain_ref[mine] = jnp.concatenate([slab, jnp.zeros((14, 128), f32)], axis=0).astype(bf)
        seq_peers = [(dp, (seq + o) % seqn) for o in range(1, seqn)]
        zx = [pc.at(**{a: to}) for a in ("z", "x") for _, to, _ in pc.partners(a)]
        pc.greet(zx + seq_peers)
        pc.meet(zx + seq_peers)
        for copy in own_first:
            copy.wait()
        start(first[0])
        for copy in own_later:
            copy.wait()
        if near:
            start(later_phases[0])

    @pl.when(i < n)
    def _():
        xr, _ = unit_rows(x_ref)
        for s in range(T // SPAN):
            row = jnp.sum(xr[s * SPAN : (s + 1) * SPAN], axis=0, keepdims=True) * (1.0 / SPAN)
            own_mean[s % spt, pl.ds(i * nseq + s // spt, 1), :] = row

    @pl.when(i == 1)
    def _():
        finish(first[0])
        start(first[1])

    @pl.when(i == n - 1)
    def _():
        finish(first[1])
        start(first[2])
        all_mean[pl.ds(seq * spt, spt)] = own_mean[...].astype(bf)
        start(means)
        finish(first[2])
        start(first[3])
        if near:
            finish(later_phases[0])
            start(later_phases[1])
        finish(means)
        mean_ref[...] = all_mean[...]
        to = lax.broadcasted_iota(jnp.int32, (seqs * FARP, spans_all * seqs), 0)
        fr = lax.broadcasted_iota(jnp.int32, (seqs * FARP, spans_all * seqs), 1)
        order = jnp.where((to % FARP == fr // seqs) & (to // FARP == fr % seqs), 1.0, 0.0).astype(bf)
        ordered = dot(order, all_mean[...].reshape(spans_all * seqs, D))
        finish(first[3])
        slabs = gain_ref[...].reshape(ndev * 16, 128)
        ga_ref[...] = gain_row(slabs, 0, ndev, rd)
        gm_ref[...] = gain_row(slabs, 1, ndev, rd)
        for k in range(n_first):
            w_out[k][...] = pack_ref[:, :, :, :, k * rd : (k + 1) * rd, :].reshape(D, D)
        mb = (ordered * ga_ref[...]).astype(bf)
        ks_ref[...] = dot(mb, w_refs[1][...]).astype(bf).reshape(seqs, FARP, D)
        vs_ref[...] = dot(mb, w_refs[2][...]).astype(bf).reshape(seqs, FARP, D)

    if near:
        for k, at in ((2, 1), (3, 4)):

            @pl.when(i == n + at)
            def _(k=k):
                finish(later_phases[k - 1])
                start(later_phases[k])

    @pl.when(i >= n)
    def _():
        j = i - n
        xn = (unit_rows(x_ref)[0] * ga_ref[...]).astype(bf)
        sub = T // 4
        cuts = [(k, h) for k in range(3) for h in (slice(0, D // 2), slice(D // 2, D))]

        def project(b):
            rows = slice(b * sub, (b + 1) * sub)

            def part(k, h):
                y = dot(xn[rows], w_refs[k][:, h]).astype(bf)
                (q_ref, k_ref, v_ref)[k][rows, h] = (y * (HD**-0.5)).astype(bf) if k == 0 else y

            return [partial(part, k, h) for k, h in cuts]

        for work in project(0):
            work()
        each = sub // SPAN * (D // 128)
        beside = {}
        for b in range(1, 4):
            beside.update(spread_out(project(b), (b - 1) * each, b * each - 1))
        attend_forward(slots, j, seq, q_ref, k_ref, v_ref, ks_ref, vs_ref, att_ref, lse_ref, beside)

    if near:

        @pl.when(i == 2 * n - 1)
        def _():
            finish(later_phases[3])


def attend_forward(slots, j, seq, q_ref, k_ref, v_ref, ks_ref, vs_ref, att_ref, lse_ref, beside):
    T, D = q_ref.shape
    spt, nseq = slots // SPAN, T // slots
    causal = causal_mask()
    t_row = lax.broadcasted_iota(jnp.int32, (FARP, 2 * SPAN), 0)

    def where(u):
        s, p = u
        return slice(s * SPAN, (s + 1) * SPAN), slice(p * 128, (p + 1) * 128), j * nseq + s // spt

    def scores(u):
        rows, ln, sq = where(u)
        ke = jnp.concatenate([k_ref[rows, ln], ks_ref[sq, :, ln]], axis=0)
        return dot(ke, pair_diag(q_ref[rows, ln]), 1, 1)

    def weigh(u, sc):
        far = t_row < (seq * spt + u[0] % spt)
        sn = jnp.where(causal, sc[:SPAN], -1e30)
        sf = jnp.where(far, sc[SPAN:], -1e30)
        m = jnp.maximum(jnp.max(sn, axis=0, keepdims=True), jnp.max(sf, axis=0, keepdims=True))
        en = jnp.exp(sn - m)
        ef = jnp.exp(sf - m)
        l = jnp.sum(en, axis=0, keepdims=True) + jnp.sum(ef, axis=0, keepdims=True)
        return en.astype(bf), ef.astype(bf), m, l

    def combine(u, en, ef, m, l):
        rows, ln, sq = where(u)
        p = u[1]
        ve = jnp.concatenate([v_ref[rows, ln], vs_ref[sq, :, ln]], axis=0)
        at = dot(ve, jnp.concatenate([en, ef], axis=0), 0, 0) * (1.0 / l)
        att_ref[rows, ln] = jnp.concatenate([at[:HD, :SPAN], at[HD:, SPAN:]], axis=0).astype(bf).T
        total = m + jnp.log(l)
        lse_ref[2 * p : 2 * p + 1, rows] = total[:, :SPAN]
        lse_ref[2 * p + 1 : 2 * p + 2, rows] = total[:, SPAN:]

    units = [(s, p) for s in range(T // SPAN) for p in range(D // 128)]
    staged(units, scores, weigh, combine, beside)


def staged(units, first, second, third, beside=None):
    a, b = {}, {}
    for t in range(0, len(units) + 4, 2):
        for k in (t, t + 1):
            for work in (beside or {}).get(k, ()):
                work()
            if k < len(units):
                a[k] = first(units[k])
        for k in (t - 2, t - 1):
            if 0 <= k < len(units):
                b[k] = second(units[k], a.pop(k))
        for k in (t - 4, t - 3):
            if 0 <= k < len(units):
                third(units[k], *b.pop(k))


def spread_out(works, begin, end):
    out = {}
    for j, work in enumerate(works):
        out.setdefault(begin + j * (end - begin) // len(works), []).append(work)
    return out


def front_call(dims, slots, block, x, w_first, w_later, gains, near):
    n_tok, D = x.shape
    seqs, spt = n_tok // slots, slots // SPAN
    nz, nx, ny, nc = dims
    n = n_tok // block
    ndev = nz * nx * ny * nc
    spans_all = spt * ny * nc
    hbm = pl.BlockSpec(memory_space=pl.ANY)
    summ = (seqs, FARP, D)
    per_piece = (nz - 1) + 2 * (nx - 1) + 2 * (ny - 1) + (nc - 1)
    n_first, n_later = (len(w_first), len(w_later)) if near else (0, 0)
    rows = sum(w.shape[0] for w in w_first) if near else 16
    copies = (2 + n_later) * per_piece + ny * nc - 1
    late = lambda i: jnp.maximum(i - n, 0)
    tok = pl.BlockSpec((block, D), lambda i: (late(i), 0))
    in_specs = [pl.BlockSpec((block, D), lambda i: (i % n, 0)), full((1, D // ndev)), full((1, D // ndev))]
    in_specs += [hbm] * (n_first + n_later) if near else [full(w.shape) for w in w_first]
    row = sds((1, D), f32)
    return pl.pallas_call(
        partial(front_kernel, dims, slots, n_first, n_later),
        grid=(2 * n,),
        in_specs=in_specs,
        out_specs=[tok] * 4
        + [pl.BlockSpec((H, block), lambda i: (0, late(i))), full(summ), full(summ)]
        + [full((spans_all, seqs, D)), full((1, D)), full((1, D))]
        + [full((D, D))] * n_first
        + [hbm] * n_later,
        out_shape=[sds((n_tok, D), bf)] * 4
        + [sds((H, n_tok), f32), sds(summ, bf), sds(summ, bf), sds((spans_all, seqs, D), bf), row, row]
        + [sds((D, D), bf)] * n_first
        + [sds(dims + w.shape, w.dtype) for w in w_later[:n_later]],
        scratch_shapes=[
            pltpu.VMEM(dims + (rows, D), bf),
            pltpu.VMEM(dims + (16, 128), bf),
            pltpu.VMEM((spt, seqs, D), f32),
            pltpu.VMEM((spans_all, seqs, D), bf),
            pltpu.SemaphoreType.DMA((max(n_first + n_later, 1),)),
            pltpu.SemaphoreType.DMA((max(copies, 1),)),
            pltpu.SemaphoreType.DMA((max(copies, 1),)),
        ],
        compiler_params=pltpu.CompilerParams(
            vmem_limit_bytes=VMEM_LIMIT, collective_id=0, has_side_effects=True,
            dimension_semantics=("arbitrary",),
        ),
    )(x, *gains, *w_first, *w_later)


def mlp_kernel(chunk, slots, ndev, len_ref, x_ref, att_ref, cot_ref, wo_ref, wu_ref, wd_ref, gm_ref,
               out_ref, datt_ref, dmid_ref, gsum_ref, adown, aup, aout):
    T, D = x_ref.shape
    FF = wu_ref.shape[1]
    i, n = pl.program_id(0), pl.num_programs(0)

    @pl.when(i == 0)
    def _():
        for acc in (adown, aup, aout):
            acc[...] = jnp.zeros_like(acc)

    att = att_ref[...]
    mid = x_ref[...].astype(f32) + dot(att, wo_ref[...])
    r = lax.rsqrt(jnp.mean(mid * mid, axis=1, keepdims=True) + EPS)
    gm = gm_ref[...]
    hn = (mid * r * gm).astype(bf)
    nseq = T // slots
    row = lax.broadcasted_iota(jnp.int32, (slots, 1), 0) + lax.axis_index("seq") * slots
    valid = jnp.concatenate(
        [jnp.where(row < len_ref[i * nseq + s], 1.0, 0.0) for s in range(nseq)], axis=0
    )
    g = cot_ref[...].astype(f32) * valid
    gb = g.astype(bf)
    gbt = gb.T
    hnt = hn.T
    y = jnp.zeros((T, D), f32)
    dhn = jnp.zeros((T, D), f32)
    cols = [slice(j * chunk, (j + 1) * chunk) for j in range(FF // chunk)]

    def products(sl):
        return dot(hn, wu_ref[:, sl]), dot(gb, wd_ref[sl, :], 1, 1)

    ready = products(cols[0])
    for j, sl in enumerate(cols):
        u, da = ready
        if j + 1 < len(cols):
            ready = products(cols[j + 1])
        h = 0.5 + 0.5 * jnp.tanh(u * (K0 + (K0 * K1) * (u * u)))
        act = (u * h).astype(bf)
        ub, hb = u.astype(bf), h.astype(bf)
        slope = hb + (ub * (bf(K0) + bf(3 * K0 * K1) * (ub * ub))) * ((hb + hb) * (bf(1.0) - hb))
        du = da.astype(bf) * slope
        y = y + dot(act, wd_ref[sl, :])
        dhn = dhn + dot(du, wu_ref[:, sl], 1, 1)
        adown[:, sl] += dot(gbt, act)
        aup[:, sl] += dot(hnt, du)
    out_ref[...] = ((mid + y) * valid).astype(bf)
    mr = mid * r
    gd = dhn * gm
    coef = jnp.mean(gd * mr, axis=1, keepdims=True)
    db = (g + r * (gd - mr * coef)).astype(bf)
    dmid_ref[...] = db
    aout[...] += dot(att, db, 0, 0)
    datt_ref[...] = dot(db, wo_ref[...], 1, 1).astype(bf)

    @pl.when(i == n - 1)
    def _():
        rd, rf = D // ndev, FF // ndev
        gsum_ref[:, :rd, :] = aout[...].reshape(ndev, rd, D).astype(bf)
        for j in range(FF // D):
            gsum_ref[:, rd * (j + 1) : rd * (j + 2), :] = (
                aup[:, j * D : (j + 1) * D].reshape(ndev, rd, D).astype(bf)
            )
            part = adown[:, j * D : (j + 1) * D].T.astype(bf)
            nd = D // rf
            gsum_ref[j * nd : (j + 1) * nd, rd * (FF // D + 1) : rd * (FF // D + 1) + rf, :] = part.reshape(
                nd, rf, D
            )


def mlp_call(chunk, slots, block, ndev, lens, x, att, cot, wo, wu, wd, gm):
    n_tok, D = x.shape
    FF = wu.shape[1]
    tok = pl.BlockSpec((block, D), lambda i: (i, 0))
    rows = D // ndev * (FF // D + 1) + FF // ndev
    return pl.pallas_call(
        partial(mlp_kernel, chunk, slots, ndev),
        grid=(n_tok // block,),
        in_specs=[pl.BlockSpec(memory_space=pltpu.SMEM), tok, tok, tok]
        + [full((D, D)), full((D, FF)), full((FF, D)), full((1, D))],
        out_specs=[tok, tok, tok, full((ndev, rows, D))],
        out_shape=[sds((n_tok, D), bf)] * 3 + [sds((ndev, rows, D), bf)],
        scratch_shapes=[pltpu.VMEM((D, FF), f32), pltpu.VMEM((D, FF), f32), pltpu.VMEM((D, D), f32)],
        compiler_params=pltpu.CompilerParams(
            vmem_limit_bytes=VMEM_LIMIT, dimension_semantics=("arbitrary",)
        ),
    )(lens, x, att, cot, wo, wu, wd, gm)


class Scatter:
    @staticmethod
    def scratch(dims, rows, width):
        nz, nx, ny, nc = dims
        most = max(nx, ny)
        half = (rows // 2, width) if rows % 32 == 0 else (rows, width // 2)
        return [
            pltpu.VMEM((nc - 1, nz, nx, ny, rows, width), bf),
            pltpu.VMEM((nz, nx, ny, rows, width), bf),
            pltpu.VMEM((nx - 1, nz, ny) + half, bf),
            pltpu.VMEM((ny - 1, nz, nx) + half, bf),
            pltpu.VMEM((2, nz, most) + half, bf),
            pltpu.VMEM((ny - 1, nz) + half, bf),
            pltpu.VMEM((nx - 1, nz) + half, bf),
            pltpu.VMEM((nz, rows, width), bf),
            pltpu.VMEM((nz - 1, rows, width), bf),
        ]

    @staticmethod
    def copies(dims):
        nz, nx, ny, nc = dims
        return (nc - 1) + 2 * (nx - 1) + 2 * (ny - 1) + (nz - 1)

    def __init__(self, pc, cp, g, mine, out, scratch):
        self.pc, self.mine, self.out, self.bufs = pc, mine, out, scratch
        got1, held1, got2a, got2b, held2, got3a, got3b, held3, got4 = scratch
        a, b = self.a, self.b = shares(*g.shape[-2:])
        every = slice(None)
        self.one = [
            cp.make(g.at[:, :, :, to], got1.at[o - 1], got1.at[o - 1], pc.at(c=to))
            for o, to, _ in pc.partners("c")
        ]
        self.two = [
            cp.make(held1.at[(every, to, every) + a], got2a.at[o - 1], got2a.at[o - 1], pc.at(x=to))
            for o, to, _ in pc.partners("x")
        ] + [
            cp.make(held1.at[(every, every, to) + b], got2b.at[o - 1], got2b.at[o - 1], pc.at(y=to))
            for o, to, _ in pc.partners("y")
        ]
        self.three = [
            cp.make(held2.at[0, :, to], got3a.at[o - 1], got3a.at[o - 1], pc.at(y=to))
            for o, to, _ in pc.partners("y")
        ] + [
            cp.make(held2.at[1, :, to], got3b.at[o - 1], got3b.at[o - 1], pc.at(x=to))
            for o, to, _ in pc.partners("x")
        ]
        self.four = [
            cp.make(held3.at[to], got4.at[o - 1], got4.at[o - 1], pc.at(z=to)) for o, to, _ in pc.partners("z")
        ]

    @staticmethod
    def total(acc, got, n):
        if n == 2:
            return acc + got[0]
        acc = acc.astype(f32)
        for o in range(n - 1):
            acc = acc + got[o].astype(f32)
        return acc

    def step(self, k):
        pc = self.pc
        got1, held1, got2a, got2b, held2, got3a, got3b, held3, got4 = self.bufs
        every = slice(None)
        if k == 0:
            start(self.one)
        elif k == 1:
            finish(self.one)
            for z in range(pc.nz):
                for x in range(pc.nx):
                    acc = self.mine(z, x)
                    for o in range(pc.nc - 1):
                        acc = acc + got1[o, z, x]
                    held1[z, x] = acc
            start(self.two)
        elif k == 2:
            finish(self.two)
            held2[0, :, : pc.ny] = self.total(held1[(every, pc.x, every) + self.a], got2a, pc.nx).astype(bf)
            held2[1, :, : pc.nx] = self.total(held1[(every, every, pc.y) + self.b], got2b, pc.ny).astype(bf)
            start(self.three)
        elif k == 3:
            finish(self.three)
            held3[(every,) + self.a] = self.total(held2[0, :, pc.y], got3a, pc.ny).astype(bf)
            held3[(every,) + self.b] = self.total(held2[1, :, pc.x], got3b, pc.nx).astype(bf)
            start(self.four)
        else:
            finish(self.four)
            self.out[...] = self.total(held3[pc.z], got4, pc.nz).astype(f32)


def back_kernel(dims, slots, pack, near, *refs):
    refs = list(refs)

    def take(n):
        out = refs[:n]
        del refs[:n]
        return out

    x_ref, q_ref, k_ref, v_ref, da_ref, lse_ref, dmid_ref, mean_ref, ks_ref, vs_ref = take(10)
    wq_ref, wk_ref, wv_ref, ga_ref = take(4)
    (g1_ref,) = take(1) if near else (None,)
    (din_ref,) = take(1)
    outs = take(2 if near else 1)
    aq, ak, av, dq_ref, dk_ref, dv_ref, dks_ref, dvs_ref, far_ref = take(9)
    far_send, far_got = take(2), take(2)
    if near:
        (g2_ref, own1) = take(2)
        bufs1, bufs2 = take(9), take(9)
        (own_sem,) = take(1)
    send_sem, recv_sem = take(2)
    T, D = x_ref.shape
    spt, nseq = slots // SPAN, T // slots
    pc = Place(dims)
    cp = Copies(send_sem, recv_sem)
    seq, dp = lax.axis_index("seq"), lax.axis_index("dp")
    seqn = pc.ny * pc.nc
    spans_all, seqs, _ = mean_ref.shape
    i, n = pl.program_id(0), pl.num_programs(0) // 2
    far = []
    for send, got in zip(far_send, far_got):
        far.append([])
        for o in range(1, seqn):
            to = (seq + o) % seqn
            far[-1].append(cp.make(send.at[:, pl.ds(to * spt, spt)], got.at[o - 1], got.at[o - 1], (dp, to)))
    if near:
        own_copy = pltpu.make_async_copy(g1_ref.at[:, :, :, pc.c], own1, own_sem.at[0])
        big = Scatter(pc, cp, g1_ref, lambda z, x: own1[z, x], outs[0], bufs1)
        small = Scatter(pc, cp, g2_ref, lambda z, x: g2_ref[z, x, :, pc.c], outs[1], bufs2)

    seq_peers = [(dp, (seq + o) % seqn) for o in range(1, seqn)]
    zx = [pc.at(**{a: to}) for a in ("z", "x") for _, to, _ in pc.partners(a)]

    @pl.when(i == 0)
    def _():
        pc.greet(zx + seq_peers)
        if near:
            own_copy.start()
        for acc in (aq, ak, av):
            acc[...] = jnp.zeros_like(acc)
        pc.meet(zx + seq_peers)
        if near:
            big.step(0)

    if near:
        for k, at in ((1, 1), (2, n // 2), (3, n - 1), (4, n + n // 3)):

            @pl.when(i == at)
            def _(k=k):
                if k == 1:
                    own_copy.wait()
                big.step(k)

    ga = ga_ref[...]

    groups = ((0, seqs - nseq), (seqs - nseq, seqs))

    def send_far(g):
        lo, hi = groups[g]
        for t in range(spans_all):
            far_send[g][0, t] = dks_ref[lo:hi, t, :].astype(bf)
            far_send[g][1, t] = dvs_ref[lo:hi, t, :].astype(bf)
        start(far[g])

    @pl.when(i == n - 1)
    def _():
        send_far(0)

    @pl.when(i < n)
    def _():
        tok = pl.ds(pl.multiple_of(i * T, T), T)
        sub = T // 1
        xt = (unit_rows(x_ref)[0] * ga).astype(bf).T
        cuts = [(k, h) for k in range(3) for h in (slice(0, D // 2), slice(D // 2, D))]

        def gather_terms(b):
            rows = pl.ds(pl.multiple_of(i * T + b * sub, sub), sub)

            def part(k, h):
                (aq, ak, av)[k][:, h] += dot(xt[:, b * sub : (b + 1) * sub], (dq_ref, dk_ref, dv_ref)[k][rows, h])

            return [partial(part, k, h) for k, h in cuts]

        each = sub // SPAN * (D // 128)
        beside = {}
        for b in range(1 - 1):
            beside.update(spread_out(gather_terms(b), (b + 1) * each + 4, (b + 2) * each + 4))
        attend_backward(slots, i, seq, spans_all, q_ref, k_ref, v_ref, da_ref, ks_ref, vs_ref, lse_ref,
                        dq_ref.at[tok], dk_ref.at[tok], dv_ref.at[tok], dks_ref, dvs_ref, beside)
        for work in gather_terms(1 - 1):
            work()

    @pl.when(i == n - 1)
    def _():
        send_far(1)
        mean = mean_ref[...].astype(f32)
        terms = [jnp.zeros((D, D), f32)] * 2
        for g, (lo, hi) in enumerate(groups):
            mb = (mean[:, lo:hi].reshape(spans_all * (hi - lo), D) * ga).astype(bf)
            for h in range(2):
                terms[h] = terms[h] + dot(mb, far_send[g][h].reshape(spans_all * (hi - lo), D), 0, 0)
        rows = D // pack
        parts = (aq[...], ak[...] + terms[0], av[...] + terms[1])
        for j, part in enumerate(parts):
            if near:
                g2_ref[:, :, :, :, j * rows : (j + 1) * rows, :] = part.astype(bf).reshape(dims + (rows, D))
            else:
                outs[0][j] = part
        if near:
            small.step(0)

    def products(j):
        tok = pl.ds(pl.multiple_of(j * T, T), T)
        dxn = dot(dq_ref[tok, :], wq_ref[...], 1, 1)
        dxn = dxn + dot(dk_ref[tok, :], wk_ref[...], 1, 1)
        return dxn + dot(dv_ref[tok, :], wv_ref[...], 1, 1)

    def to_input(j, dxn):
        parts = []
        for s in range(T // SPAN):
            row = far_ref[s % spt, pl.ds(j * nseq + s // spt, 1), :]
            parts.append(dxn[s * SPAN : (s + 1) * SPAN] + row)
        gd = jnp.concatenate(parts, axis=0) * ga
        xr, r = unit_rows(x_ref)
        coef = jnp.mean(gd * xr, axis=1, keepdims=True)
        din_ref[...] = (dmid_ref[...].astype(f32) + r * (gd - xr * coef)).astype(bf)

    @pl.when(i == n)
    def _():
        dxn = products(0)
        for g, (lo, hi) in enumerate(groups):
            finish(far[g])
            tot = []
            for h in range(2):
                acc = far_send[g][h, pl.ds(seq * spt, spt)].astype(f32)
                for o in range(seqn - 1):
                    acc = acc + far_got[g][o, h].astype(f32)
                tot.append(acc.astype(bf).reshape(spt * (hi - lo), D))
            rows = dot(tot[0], wk_ref[...], 1, 1) + dot(tot[1], wv_ref[...], 1, 1)
            far_ref[:, lo:hi, :] = (rows * (1.0 / SPAN)).reshape(spt, hi - lo, D)
        to_input(0, dxn)

    if near:
        for k, at in ((1, 1), (2, n // 2), (3, 2 * n // 3)):

            @pl.when(i == n + at)
            def _(k=k):
                small.step(k)

    @pl.when(i > n)
    def _():
        to_input(i - n, products(i - n))

    if near:

        @pl.when(i == 2 * n - 1)
        def _():
            small.step(4)


def attend_backward(slots, i, seq, spans_all, q_ref, k_ref, v_ref, da_ref, ks_ref, vs_ref, lse_ref,
                    dq_ref, dk_ref, dv_ref, dks_ref, dvs_ref, beside):
    T, D = q_ref.shape
    spt, nseq = slots // SPAN, T // slots
    causal = causal_mask()
    t_row = lax.broadcasted_iota(jnp.int32, (FARP, 2 * SPAN), 0)

    def where(u):
        s, p = u
        return slice(s * SPAN, (s + 1) * SPAN), slice(p * 128, (p + 1) * 128), i * nseq + s // spt

    def scores(u):
        rows, ln, sq = where(u)
        ke = jnp.concatenate([k_ref[rows, ln], ks_ref[sq, :, ln]], axis=0)
        ve = jnp.concatenate([v_ref[rows, ln], vs_ref[sq, :, ln]], axis=0)
        qbd, dbd = pair_diag(q_ref[rows, ln]), pair_diag(da_ref[rows, ln])
        return dot(ke, qbd, 1, 1), dot(ve, dbd, 1, 1)

    def weigh(u, got):
        sc, dp = got
        rows, p = where(u)[0], u[1]
        far = t_row < (seq * spt + u[0] % spt)
        lse = jnp.concatenate([lse_ref[2 * p : 2 * p + 1, rows], lse_ref[2 * p + 1 : 2 * p + 2, rows]], axis=1)
        pn = jnp.where(causal, jnp.exp(sc[:SPAN] - lse), 0.0)
        pf = jnp.where(far, jnp.exp(sc[SPAN:] - lse), 0.0)
        dpn, dpf = dp[:SPAN], dp[SPAN:]
        delta = jnp.sum(pn * dpn, axis=0, keepdims=True) + jnp.sum(pf * dpf, axis=0, keepdims=True)
        dsn, dsf = (pn * (dpn - delta)).astype(bf), (pf * (dpf - delta)).astype(bf)
        return pn.astype(bf), pf.astype(bf), dsn, dsf

    def combine(u, pn, pf, dsn, dsf):
        rows, ln, sq = where(u)
        qbd, dbd = pair_diag(q_ref[rows, ln]), pair_diag(da_ref[rows, ln])
        dv = dot(jnp.concatenate([pn, pf], axis=0), dbd)
        ds = jnp.concatenate([dsn, dsf], axis=0)
        dk = dot(ds, qbd)
        ke = jnp.concatenate([k_ref[rows, ln], ks_ref[sq, :, ln]], axis=0)
        dq = dot(ke, ds, 0, 0)
        dq = jnp.concatenate([dq[:HD, :SPAN], dq[HD:, SPAN:]], axis=0) * (HD**-0.5)
        dq_ref[rows, ln] = dq.astype(bf).T
        dk_ref[rows, ln] = dk[:SPAN].astype(bf)
        dv_ref[rows, ln] = dv[:SPAN].astype(bf)
        fk, fv = dk[SPAN : SPAN + spans_all], dv[SPAN : SPAN + spans_all]
        if u[0] % spt == 0:
            dks_ref[sq, :, ln] = fk
            dvs_ref[sq, :, ln] = fv
        else:
            dks_ref[sq, :, ln] += fk
            dvs_ref[sq, :, ln] += fv

    units = [(s, p) for s in range(T // SPAN) for p in range(D // 128)]
    staged(units, scores, weigh, combine, beside)


def back_call(dims, slots, block, pack, near, x, q, k, v, da, lse, dmid, mean, ks, vs, wq, wk, wv, ga, g1):
    n_tok, D = x.shape
    nz, nx, ny, nc = dims
    n = n_tok // block
    spt, nseq = slots // SPAN, block // slots
    spans_all, seqs, _ = mean.shape
    seqn = ny * nc
    vm = pltpu.VMEM
    early = pl.BlockSpec((block, D), lambda i: (jnp.minimum(i, n - 1), 0))
    late = pl.BlockSpec((block, D), lambda i: (jnp.maximum(i - n, 0), 0))
    rows2 = D // pack * 3
    in_specs = (
        [pl.BlockSpec((block, D), lambda i: (i % n, 0))]
        + [early] * 4
        + [pl.BlockSpec((H, block), lambda i: (0, jnp.minimum(i, n - 1))), late]
        + [full(mean.shape), full(ks.shape), full(vs.shape)]
        + [full((D, D))] * 3
        + [full((1, D))]
    )
    args = [x, q, k, v, da, lse, dmid, mean, ks, vs, wq, wk, wv, ga]
    out_specs, out_shape = [late], [sds((n_tok, D), bf)]
    scratch = [vm((D, D), f32)] * 3 + [vm((n_tok, D), bf)] * 3 + [vm((seqs, spans_all, D), f32)] * 2
    scratch += [
        vm((spt, seqs, D), f32),
        vm((2, spans_all, seqs - nseq, D), bf),
        vm((2, spans_all, nseq, D), bf),
        vm((max(seqn - 1, 1), 2, spt, seqs - nseq, D), bf),
        vm((max(seqn - 1, 1), 2, spt, nseq, D), bf),
    ]
    copies = 2 * (seqn - 1)
    if near:
        rows1 = g1.shape[1]
        args.append(g1.reshape(dims + g1.shape[1:]))
        in_specs.append(pl.BlockSpec(memory_space=pl.ANY))
        out_specs += [full((rows1, D)), full((rows2, D))]
        out_shape += [sds((rows1, D), f32), sds((rows2, D), f32)]
        scratch += [vm(dims + (rows2, D), bf), vm((nz, nx, ny, rows1, D), bf)]
        scratch += Scatter.scratch(dims, rows1, D) + Scatter.scratch(dims, rows2, D)
        scratch.append(pltpu.SemaphoreType.DMA((1,)))
        copies += 2 * Scatter.copies(dims)
    else:
        out_specs.append(full((3, D, D)))
        out_shape.append(sds((3, D, D), f32))
    scratch += [pltpu.SemaphoreType.DMA((max(copies, 1),))] * 2
    return pl.pallas_call(
        partial(back_kernel, dims, slots, pack, near),
        grid=(2 * n,),
        in_specs=in_specs,
        out_specs=out_specs,
        out_shape=out_shape,
        scratch_shapes=scratch,
        compiler_params=pltpu.CompilerParams(
            vmem_limit_bytes=VMEM_LIMIT, collective_id=1, has_side_effects=True,
            dimension_semantics=("arbitrary",),
        ),
    )(*args)


def last_kernel(rd, rf, din_ref, m_ref, a_ref, wq_ref, wk_ref, wv_ref, wu_ref, ga_ref, gm_ref,
                out_ref, gq_ref, gk_ref, gv_ref, go_ref, gu_ref, gd_ref, gga_ref, ggm_ref):
    out_ref[...] = din_ref[...].astype(f32)
    D = out_ref.shape[1]
    FF = gu_ref.shape[1]

    @pl.when(pl.program_id(0) == 0)
    def _():
        attn = jnp.zeros((rd, 1), f32)
        for j, (w_ref, g_ref) in enumerate(((wq_ref, gq_ref), (wk_ref, gk_ref), (wv_ref, gv_ref))):
            g = a_ref[j * rd : (j + 1) * rd, :]
            g_ref[...] = g
            attn = attn + jnp.sum(g * w_ref[...].astype(f32), axis=1, keepdims=True)
        go_ref[...] = m_ref[:rd, :]
        up = jnp.zeros((rd, 1), f32)
        for j in range(FF // D):
            g = m_ref[rd * (j + 1) : rd * (j + 2), :]
            gu_ref[:, j * D : (j + 1) * D] = g
            up = up + jnp.sum(g * wu_ref[:, j * D : (j + 1) * D].astype(f32), axis=1, keepdims=True)
        gd_ref[...] = m_ref[rd * (FF // D + 1) :, :]
        for total, gain, out in ((attn, ga_ref, gga_ref), (up, gm_ref, ggm_ref)):
            row = jnp.broadcast_to(total, (rd, 128)).T[:1, :]
            out[...] = row[:, :rd] / gain[...].astype(f32)


def last_call(block, din, sums_m, sums_a, wq, wk, wv, wu, ga, gm):
    n_tok, D = din.shape
    rd, FF = wu.shape
    rf = sums_m.shape[0] - rd * (FF // D + 1)
    tok = pl.BlockSpec((block, D), lambda i: (i, 0))
    args = [sums_m, sums_a, wq, wk, wv, wu, ga, gm]
    shapes = [(rd, D)] * 4 + [(rd, FF), (rf, D), (1, rd), (1, rd)]
    return pl.pallas_call(
        partial(last_kernel, rd, rf),
        grid=(n_tok // block,),
        in_specs=[tok] + [full(a.shape) for a in args],
        out_specs=[tok] + [full(s) for s in shapes],
        out_shape=[sds((n_tok, D), f32)] + [sds(s, f32) for s in shapes],
        compiler_params=pltpu.CompilerParams(
            vmem_limit_bytes=VMEM_LIMIT, dimension_semantics=("arbitrary",)
        ),
    )(din, *args)


def body(dims, inputs, lengths, cotangent, w_query, w_key, w_value, w_out, w_up, w_down, gain_attn, gain_mlp):
    seqs, slots, D = inputs.shape
    nz, nx, ny, nc = dims
    ndev = nz * nx * ny * nc
    FF = w_up.shape[1]
    rd, rf = w_query.shape[0], w_down.shape[0]
    n_tok = seqs * slots
    block = 1024
    x = inputs.reshape(n_tok, D)
    cot = cotangent.reshape(n_tok, D)
    gains = [g.reshape(1, rd) for g in (gain_attn, gain_mlp)]
    everyone = ("dp", "seq")
    near = rd % 16 == 0 and n_tok // block >= 6
    if near:
        w_first, w_later = (w_query, w_key, w_value), (w_up, w_down, w_out)
    else:
        wq, wk, wv, wu, wd, wo = (
            lax.all_gather(w, everyone, axis=0, tiled=True)
            for w in (w_query, w_key, w_value, w_up, w_down, w_out)
        )
        w_first, w_later = (wq, wk, wv), ()
    q, k, v, att, lse, ks, vs, mean, ga, gm, *later = front_call(dims, slots, block, x, w_first, w_later, gains, near)
    if near:
        wq, wk, wv, wu, wd, wo = (w.reshape(-1, w.shape[-1]) for w in later)
    pack = ndev if near else 32
    output, datt, dmid, sums_m = mlp_call(512, slots, block, pack, lengths, x, att, cot, wo, wu, wd, gm)
    grad_in, *sums = back_call(
        dims, slots, block, pack, near, x, q, k, v, datt, lse, dmid, mean, ks, vs, wq, wk, wv, ga, sums_m
    )
    if near:
        grad_in, g_q, g_k, g_v, g_out, g_up, g_down, g_ga, g_gm = last_call(
            n_tok // 3, grad_in, *sums, w_query, w_key, w_value, w_up, *gains
        )
        g_ga, g_gm = g_ga.reshape(rd), g_gm.reshape(rd)
    else:
        pd, pf = D // pack, FF // pack
        last = pd * (FF // D + 1) + pf

        def scattered(a):
            return lax.psum_scatter(a.astype(f32), everyone, scatter_dimension=0, tiled=True)

        g_out = scattered(sums_m[:, :pd].reshape(D, D))
        g_up = scattered(
            jnp.concatenate([sums_m[:, pd * (j + 1) : pd * (j + 2)].reshape(D, D) for j in range(FF // D)], axis=1)
        )
        g_down = scattered(sums_m[:, pd * (FF // D + 1) : last].reshape(FF, D))
        g_q, g_k, g_v = (scattered(sums[0][j]) for j in range(3))
        g_ga = jnp.sum(
            w_query.astype(f32) * g_q + w_key.astype(f32) * g_k + w_value.astype(f32) * g_v, axis=1
        ) / gain_attn.astype(f32)
        g_gm = jnp.sum(w_up.astype(f32) * g_up, axis=1) / gain_mlp.astype(f32)
        grad_in = grad_in.astype(f32)
    return (
        output.reshape(inputs.shape), grad_in.reshape(inputs.shape),
        g_q, g_k, g_v, g_out, g_up, g_down, g_ga, g_gm,
    )


def solution(mesh):
    dp, seq = mesh.shape["dp"], mesh.shape["seq"]
    nx = max(d for d in range(1, dp + 1) if dp % d == 0 and d * d <= dp)
    nc = 2 if seq % 2 == 0 else 1
    dims = (dp // nx, nx, seq // nc, nc)
    rows, vec = P(("dp", "seq"), None), P(("dp", "seq"))
    tokens = P("dp", "seq", None)
    return jax.shard_map(
        partial(body, dims),
        mesh=mesh,
        in_specs=(tokens, P("dp"), tokens) + (rows,) * 6 + (vec,) * 2,
        out_specs=(tokens, tokens) + (rows,) * 6 + (vec,) * 2,
        check_vma=False,
    )
```

```python
from functools import partial

import jax
import jax.numpy as jnp
from jax import lax
from jax.experimental import pallas as pl
from jax.experimental.pallas import tpu as pltpu
from jax.sharding import PartitionSpec as P

H = 8
HD = 64
SPAN = 128
EPS = 1e-06
K0 = 0.7978845608028654
K1 = 0.044715
FARP = 16
f32 = jnp.float32
bf = jnp.bfloat16
MESH = pl.DeviceIdType.MESH
VMEM_LIMIT = 62 << 20


def dot(a, b, ca=1, cb=0):
    return lax.dot_general(a, b, (((ca,), (cb,)), ((), ())), preferred_element_type=f32)


def sds(shape, dtype):
    return jax.ShapeDtypeStruct(shape, dtype)


def full(shape):
    return pl.BlockSpec(shape, lambda i: (0,) * len(shape), pipeline_mode=pl.Buffered(1))


def pair_diag(a):
    lane = lax.broadcasted_iota(jnp.int32, a.shape, 1)
    zero = jnp.zeros_like(a)
    return jnp.concatenate([jnp.where(lane < HD, a, zero), jnp.where(lane >= HD, a, zero)], axis=0)


def unit_rows(x_ref):
    x = x_ref[...].astype(f32)
    r = lax.rsqrt(jnp.mean(x * x, axis=1, keepdims=True) + EPS)
    return x * r, r


def causal_mask():
    j = lax.broadcasted_iota(jnp.int32, (SPAN, 2 * SPAN), 0)
    i = lax.broadcasted_iota(jnp.int32, (SPAN, 2 * SPAN), 1)
    return j <= jnp.where(i >= SPAN, i - SPAN, i)


def gain_row(slabs, which, ndev, rows):
    width = ndev * rows
    r = lax.broadcasted_iota(jnp.int32, slabs.shape, 0)
    l = lax.broadcasted_iota(jnp.int32, slabs.shape, 1)
    keep = jnp.where((r % 16 == which) & (l < rows), slabs.astype(f32), 0.0).astype(bf)
    a = lax.broadcasted_iota(jnp.int32, (128, width), 0)
    b = lax.broadcasted_iota(jnp.int32, (128, width), 1)
    spread = dot(keep, jnp.where(b % rows == a, 1.0, 0.0).astype(bf))
    d = lax.broadcasted_iota(jnp.int32, spread.shape, 0)
    c = lax.broadcasted_iota(jnp.int32, spread.shape, 1)
    return jnp.sum(jnp.where(d // 16 == c // rows, spread, 0.0), axis=0, keepdims=True)


class Place:
    def __init__(self, dims):
        self.nz, self.nx, self.ny, self.nc = dims
        dp, seq = lax.axis_index("dp"), lax.axis_index("seq")
        self.z, self.x = dp // self.nx, dp % self.nx
        self.y, self.c = seq // self.nc, seq % self.nc

    def at(self, z=None, x=None, y=None, c=None):
        z = self.z if z is None else z
        x = self.x if x is None else x
        y = self.y if y is None else y
        c = self.c if c is None else c
        return (z * self.nx + x, y * self.nc + c)

    def line(self, axis):
        return getattr(self, axis), getattr(self, "n" + axis)

    def partners(self, axis):
        me, n = self.line(axis)
        order = sorted(range(1, n), key=lambda o: abs(2 * o - n))
        return [(o, (me + o) % n, (me + n - o) % n) for o in order]

    def greet(self, others):
        for other in others:
            pl.semaphore_signal(pltpu.get_barrier_semaphore(), inc=1, device_id=other, device_id_type=MESH)

    def meet(self, others):
        pl.semaphore_wait(pltpu.get_barrier_semaphore(), len(others))

    def others(self):
        return [self.at(**{a: to}) for a in ("z", "x", "y", "c") for _, to, _ in self.partners(a)]


class Copies:
    def __init__(self, send_sem, recv_sem):
        self.send_sem, self.recv_sem, self.used = send_sem, recv_sem, 0

    def make(self, src, dst, landed, device):
        k = self.used
        self.used += 1
        out = pltpu.make_async_remote_copy(
            src_ref=src, dst_ref=dst, send_sem=self.send_sem.at[k], recv_sem=self.recv_sem.at[k],
            device_id=device, device_id_type=MESH,
        )
        into = pltpu.make_async_remote_copy(
            src_ref=src, dst_ref=landed, send_sem=self.send_sem.at[k], recv_sem=self.recv_sem.at[k],
            device_id=device, device_id_type=MESH,
        )
        return out, into


def start(copies):
    for out, _ in copies:
        out.start()


def finish(copies):
    for out, into in copies:
        out.wait_send()
        into.wait_recv()


def shares(rows, width):
    if rows % 32 == 0:
        return (pl.ds(0, rows // 2), slice(None)), (pl.ds(rows // 2, rows // 2), slice(None))
    return (slice(None), pl.ds(0, width // 2)), (slice(None), pl.ds(width // 2, width // 2))


def gather_phases(pc, cp, pieces, wholes, routes):
    z, x, y, c = pc.z, pc.x, pc.y, pc.c
    first, second, third, last = [], [], [], []
    for piece, whole, route in zip(pieces, wholes, routes):
        rows, width = whole.shape[-2:]
        everything = (slice(None), slice(None))
        one, two = shares(rows, width) if route == "both" else (everything, everything)
        for _, to, fr in pc.partners("z"):
            first.append(cp.make(piece, whole.at[z, x, y, c], whole.at[fr, x, y, c], pc.at(z=to)))
        for _, to, fr in pc.partners("x"):
            if route != "yx":
                v = whole.at[(slice(None), x, y, c) + one]
                second.append(cp.make(v, v, whole.at[(slice(None), fr, y, c) + one], pc.at(x=to)))
            if route != "xy":
                v = whole.at[(slice(None), x, slice(None), c) + two]
                third.append(cp.make(v, v, whole.at[(slice(None), fr, slice(None), c) + two], pc.at(x=to)))
        for _, to, fr in pc.partners("y"):
            if route != "xy":
                v = whole.at[(slice(None), x, y, c) + two]
                second.append(cp.make(v, v, whole.at[(slice(None), x, fr, c) + two], pc.at(y=to)))
            if route != "yx":
                v = whole.at[(slice(None), slice(None), y, c) + one]
                third.append(cp.make(v, v, whole.at[(slice(None), slice(None), fr, c) + one], pc.at(y=to)))
        for _, to, fr in pc.partners("c"):
            v = whole.at[:, :, :, c]
            last.append(cp.make(v, v, whole.at[:, :, :, fr], pc.at(c=to)))
    return first, second, third, last


def front_kernel(dims, slots, n_first, n_later, *refs):
    near = n_first > 0
    refs = list(refs)

    def take(n):
        out = refs[:n]
        del refs[:n]
        return out

    x_ref, ga_own, gm_own = take(3)
    pieces = take(n_first + n_later)
    w_in = [] if near else take(3)
    q_ref, k_ref, v_ref, att_ref, lse_ref, ks_ref, vs_ref, mean_ref, ga_ref, gm_ref = take(10)
    w_out = take(n_first)
    later = take(n_later)
    pack_ref, gain_ref, own_mean, all_mean, local_sem, send_sem, recv_sem = take(7)
    T, D = x_ref.shape
    spt, nseq = slots // SPAN, T // slots
    pc = Place(dims)
    cp = Copies(send_sem, recv_sem)
    seq, dp = lax.axis_index("seq"), lax.axis_index("dp")
    seqn = pc.ny * pc.nc
    spans_all, seqs = spt * seqn, all_mean.shape[1]
    ndev = pc.nz * pc.nx * seqn
    rd = D // ndev
    mine = (pc.z, pc.x, pc.y, pc.c)
    packs = [pack_ref, gain_ref] if near else [gain_ref]
    first = gather_phases(pc, cp, [p.at[mine] for p in packs], packs, ["both", "xy"][-len(packs) :])
    later_phases = gather_phases(pc, cp, pieces[n_first:], later, ["xy", "yx", "both"][:n_later])
    own_first = [
        pltpu.make_async_copy(p, pack_ref.at[mine + (pl.ds(k * rd, rd),)], local_sem.at[k])
        for k, p in enumerate(pieces[:n_first])
    ]
    own_later = [
        pltpu.make_async_copy(p, w.at[mine], local_sem.at[n_first + k])
        for k, (p, w) in enumerate(zip(pieces[n_first:], later))
    ]
    means = []
    for o in range(1, seqn):
        to, fr = (seq + o) % seqn, (seq + seqn - o) % seqn
        v = all_mean.at[pl.ds(seq * spt, spt)]
        means.append(cp.make(v, v, all_mean.at[pl.ds(fr * spt, spt)], (dp, to)))
    i, n = pl.program_id(0), pl.num_programs(0) // 2
    w_refs = w_out if near else w_in

    @pl.when(i == 0)
    def _():
        for copy in own_first + own_later:
            copy.start()
        slab = jnp.concatenate([ga_own[...], gm_own[...]], axis=0).astype(f32)[:, :128]
        if rd < 128:
            slab = jnp.concatenate([slab, jnp.zeros((2, 128 - rd), f32)], axis=1)
        gain_ref[mine] = jnp.concatenate([slab, jnp.zeros((14, 128), f32)], axis=0).astype(bf)
        seq_peers = [(dp, (seq + o) % seqn) for o in range(1, seqn)]
        zx = [pc.at(**{a: to}) for a in ("z", "x") for _, to, _ in pc.partners(a)]
        pc.greet(zx + seq_peers)
        pc.meet(zx + seq_peers)
        for copy in own_first:
            copy.wait()
        start(first[0])
        for copy in own_later:
            copy.wait()
        if near:
            start(later_phases[0])

    @pl.when(i < n)
    def _():
        xr, _ = unit_rows(x_ref)
        for s in range(T // SPAN):
            row = jnp.sum(xr[s * SPAN : (s + 1) * SPAN], axis=0, keepdims=True) * (1.0 / SPAN)
            own_mean[s % spt, pl.ds(i * nseq + s // spt, 1), :] = row

    @pl.when(i == 1)
    def _():
        finish(first[0])
        start(first[1])

    @pl.when(i == n - 1)
    def _():
        finish(first[1])
        start(first[2])
        all_mean[pl.ds(seq * spt, spt)] = own_mean[...].astype(bf)
        start(means)
        finish(first[2])
        start(first[3])
        if near:
            finish(later_phases[0])
            start(later_phases[1])
        finish(means)
        mean_ref[...] = all_mean[...]
        to = lax.broadcasted_iota(jnp.int32, (seqs * FARP, spans_all * seqs), 0)
        fr = lax.broadcasted_iota(jnp.int32, (seqs * FARP, spans_all * seqs), 1)
        order = jnp.where((to % FARP == fr // seqs) & (to // FARP == fr % seqs), 1.0, 0.0).astype(bf)
        ordered = dot(order, all_mean[...].reshape(spans_all * seqs, D))
        finish(first[3])
        slabs = gain_ref[...].reshape(ndev * 16, 128)
        ga_ref[...] = gain_row(slabs, 0, ndev, rd)
        gm_ref[...] = gain_row(slabs, 1, ndev, rd)
        for k in range(n_first):
            w_out[k][...] = pack_ref[:, :, :, :, k * rd : (k + 1) * rd, :].reshape(D, D)
        mb = (ordered * ga_ref[...]).astype(bf)
        ks_ref[...] = dot(mb, w_refs[1][...]).astype(bf).reshape(seqs, FARP, D)
        vs_ref[...] = dot(mb, w_refs[2][...]).astype(bf).reshape(seqs, FARP, D)

    if near:
        for k, at in ((2, 1), (3, 4)):

            @pl.when(i == n + at)
            def _(k=k):
                finish(later_phases[k - 1])
                start(later_phases[k])

    @pl.when(i >= n)
    def _():
        j = i - n
        xn = (unit_rows(x_ref)[0] * ga_ref[...]).astype(bf)
        sub = T // 4
        cuts = [(k, h) for k in range(3) for h in (slice(0, D // 2), slice(D // 2, D))]

        def project(b):
            rows = slice(b * sub, (b + 1) * sub)

            def part(k, h):
                y = dot(xn[rows], w_refs[k][:, h]).astype(bf)
                (q_ref, k_ref, v_ref)[k][rows, h] = (y * (HD**-0.5)).astype(bf) if k == 0 else y

            return [partial(part, k, h) for k, h in cuts]

        for work in project(0):
            work()
        each = sub // SPAN * (D // 128)
        beside = {}
        for b in range(1, 4):
            beside.update(spread_out(project(b), (b - 1) * each, b * each - 1))
        attend_forward(slots, j, seq, q_ref, k_ref, v_ref, ks_ref, vs_ref, att_ref, lse_ref, beside)

    if near:

        @pl.when(i == 2 * n - 1)
        def _():
            finish(later_phases[3])


def attend_forward(slots, j, seq, q_ref, k_ref, v_ref, ks_ref, vs_ref, att_ref, lse_ref, beside):
    T, D = q_ref.shape
    spt, nseq = slots // SPAN, T // slots
    causal = causal_mask()
    t_row = lax.broadcasted_iota(jnp.int32, (FARP, 2 * SPAN), 0)

    def where(u):
        s, p = u
        return slice(s * SPAN, (s + 1) * SPAN), slice(p * 128, (p + 1) * 128), j * nseq + s // spt

    def scores(u):
        rows, ln, sq = where(u)
        ke = jnp.concatenate([k_ref[rows, ln], ks_ref[sq, :, ln]], axis=0)
        return dot(ke, pair_diag(q_ref[rows, ln]), 1, 1)

    def weigh(u, sc):
        far = t_row < (seq * spt + u[0] % spt)
        sn = jnp.where(causal, sc[:SPAN], -1e30)
        sf = jnp.where(far, sc[SPAN:], -1e30)
        m = jnp.maximum(jnp.max(sn, axis=0, keepdims=True), jnp.max(sf, axis=0, keepdims=True))
        en = jnp.exp(sn - m)
        ef = jnp.exp(sf - m)
        l = jnp.sum(en, axis=0, keepdims=True) + jnp.sum(ef, axis=0, keepdims=True)
        return en.astype(bf), ef.astype(bf), m, l

    def combine(u, en, ef, m, l):
        rows, ln, sq = where(u)
        p = u[1]
        ve = jnp.concatenate([v_ref[rows, ln], vs_ref[sq, :, ln]], axis=0)
        at = dot(ve, jnp.concatenate([en, ef], axis=0), 0, 0) * (1.0 / l)
        att_ref[rows, ln] = jnp.concatenate([at[:HD, :SPAN], at[HD:, SPAN:]], axis=0).astype(bf).T
        total = m + jnp.log(l)
        lse_ref[2 * p : 2 * p + 1, rows] = total[:, :SPAN]
        lse_ref[2 * p + 1 : 2 * p + 2, rows] = total[:, SPAN:]

    units = [(s, p) for s in range(T // SPAN) for p in range(D // 128)]
    staged(units, scores, weigh, combine, beside)


def staged(units, first, second, third, beside=None):
    a, b = {}, {}
    for t in range(0, len(units) + 4, 2):
        for k in (t, t + 1):
            for work in (beside or {}).get(k, ()):
                work()
            if k < len(units):
                a[k] = first(units[k])
        for k in (t - 2, t - 1):
            if 0 <= k < len(units):
                b[k] = second(units[k], a.pop(k))
        for k in (t - 4, t - 3):
            if 0 <= k < len(units):
                third(units[k], *b.pop(k))


def spread_out(works, begin, end):
    out = {}
    for j, work in enumerate(works):
        out.setdefault(begin + j * (end - begin) // len(works), []).append(work)
    return out


def front_call(dims, slots, block, x, w_first, w_later, gains, near):
    n_tok, D = x.shape
    seqs, spt = n_tok // slots, slots // SPAN
    nz, nx, ny, nc = dims
    n = n_tok // block
    ndev = nz * nx * ny * nc
    spans_all = spt * ny * nc
    hbm = pl.BlockSpec(memory_space=pl.ANY)
    summ = (seqs, FARP, D)
    per_piece = (nz - 1) + 2 * (nx - 1) + 2 * (ny - 1) + (nc - 1)
    n_first, n_later = (len(w_first), len(w_later)) if near else (0, 0)
    rows = sum(w.shape[0] for w in w_first) if near else 16
    copies = (2 + n_later) * per_piece + ny * nc - 1
    late = lambda i: jnp.maximum(i - n, 0)
    tok = pl.BlockSpec((block, D), lambda i: (late(i), 0))
    in_specs = [pl.BlockSpec((block, D), lambda i: (i % n, 0)), full((1, D // ndev)), full((1, D // ndev))]
    in_specs += [hbm] * (n_first + n_later) if near else [full(w.shape) for w in w_first]
    row = sds((1, D), f32)
    return pl.pallas_call(
        partial(front_kernel, dims, slots, n_first, n_later),
        grid=(2 * n,),
        in_specs=in_specs,
        out_specs=[tok] * 4
        + [pl.BlockSpec((H, block), lambda i: (0, late(i))), full(summ), full(summ)]
        + [full((spans_all, seqs, D)), full((1, D)), full((1, D))]
        + [full((D, D))] * n_first
        + [hbm] * n_later,
        out_shape=[sds((n_tok, D), bf)] * 4
        + [sds((H, n_tok), f32), sds(summ, bf), sds(summ, bf), sds((spans_all, seqs, D), bf), row, row]
        + [sds((D, D), bf)] * n_first
        + [sds(dims + w.shape, w.dtype) for w in w_later[:n_later]],
        scratch_shapes=[
            pltpu.VMEM(dims + (rows, D), bf),
            pltpu.VMEM(dims + (16, 128), bf),
            pltpu.VMEM((spt, seqs, D), f32),
            pltpu.VMEM((spans_all, seqs, D), bf),
            pltpu.SemaphoreType.DMA((max(n_first + n_later, 1),)),
            pltpu.SemaphoreType.DMA((max(copies, 1),)),
            pltpu.SemaphoreType.DMA((max(copies, 1),)),
        ],
        compiler_params=pltpu.CompilerParams(
            vmem_limit_bytes=VMEM_LIMIT, collective_id=0, has_side_effects=True,
            dimension_semantics=("arbitrary",),
        ),
    )(x, *gains, *w_first, *w_later)


def mlp_kernel(chunk, slots, ndev, len_ref, x_ref, att_ref, cot_ref, wo_ref, wu_ref, wd_ref, gm_ref,
               out_ref, datt_ref, dmid_ref, gsum_ref, adown, aup, aout):
    T, D = x_ref.shape
    FF = wu_ref.shape[1]
    i, n = pl.program_id(0), pl.num_programs(0)

    @pl.when(i == 0)
    def _():
        for acc in (adown, aup, aout):
            acc[...] = jnp.zeros_like(acc)

    att = att_ref[...]
    mid = x_ref[...].astype(f32) + dot(att, wo_ref[...])
    r = lax.rsqrt(jnp.mean(mid * mid, axis=1, keepdims=True) + EPS)
    gm = gm_ref[...]
    hn = (mid * r * gm).astype(bf)
    nseq = T // slots
    row = lax.broadcasted_iota(jnp.int32, (slots, 1), 0) + lax.axis_index("seq") * slots
    valid = jnp.concatenate(
        [jnp.where(row < len_ref[i * nseq + s], 1.0, 0.0) for s in range(nseq)], axis=0
    )
    g = cot_ref[...].astype(f32) * valid
    gb = g.astype(bf)
    gbt = gb.T
    hnt = hn.T
    y = jnp.zeros((T, D), f32)
    dhn = jnp.zeros((T, D), f32)
    cols = [slice(j * chunk, (j + 1) * chunk) for j in range(FF // chunk)]

    def products(sl):
        return dot(hn, wu_ref[:, sl]), dot(gb, wd_ref[sl, :], 1, 1)

    ready = products(cols[0])
    for j, sl in enumerate(cols):
        u, da = ready
        if j + 1 < len(cols):
            ready = products(cols[j + 1])
        h = 0.5 + 0.5 * jnp.tanh(u * (K0 + (K0 * K1) * (u * u)))
        act = (u * h).astype(bf)
        ub, hb = u.astype(bf), h.astype(bf)
        slope = hb + (ub * (bf(K0) + bf(3 * K0 * K1) * (ub * ub))) * ((hb + hb) * (bf(1.0) - hb))
        du = da.astype(bf) * slope
        y = y + dot(act, wd_ref[sl, :])
        dhn = dhn + dot(du, wu_ref[:, sl], 1, 1)
        adown[:, sl] += dot(gbt, act)
        aup[:, sl] += dot(hnt, du)
    out_ref[...] = ((mid + y) * valid).astype(bf)
    mr = mid * r
    gd = dhn * gm
    coef = jnp.mean(gd * mr, axis=1, keepdims=True)
    db = (g + r * (gd - mr * coef)).astype(bf)
    dmid_ref[...] = db
    aout[...] += dot(att, db, 0, 0)
    datt_ref[...] = dot(db, wo_ref[...], 1, 1).astype(bf)

    @pl.when(i == n - 1)
    def _():
        rd, rf = D // ndev, FF // ndev
        gsum_ref[:, :rd, :] = aout[...].reshape(ndev, rd, D).astype(bf)
        for j in range(FF // D):
            gsum_ref[:, rd * (j + 1) : rd * (j + 2), :] = (
                aup[:, j * D : (j + 1) * D].reshape(ndev, rd, D).astype(bf)
            )
            part = adown[:, j * D : (j + 1) * D].T.astype(bf)
            nd = D // rf
            gsum_ref[j * nd : (j + 1) * nd, rd * (FF // D + 1) : rd * (FF // D + 1) + rf, :] = part.reshape(
                nd, rf, D
            )


def mlp_call(chunk, slots, block, ndev, lens, x, att, cot, wo, wu, wd, gm):
    n_tok, D = x.shape
    FF = wu.shape[1]
    tok = pl.BlockSpec((block, D), lambda i: (i, 0))
    rows = D // ndev * (FF // D + 1) + FF // ndev
    return pl.pallas_call(
        partial(mlp_kernel, chunk, slots, ndev),
        grid=(n_tok // block,),
        in_specs=[pl.BlockSpec(memory_space=pltpu.SMEM), tok, tok, tok]
        + [full((D, D)), full((D, FF)), full((FF, D)), full((1, D))],
        out_specs=[tok, tok, tok, full((ndev, rows, D))],
        out_shape=[sds((n_tok, D), bf)] * 3 + [sds((ndev, rows, D), bf)],
        scratch_shapes=[pltpu.VMEM((D, FF), f32), pltpu.VMEM((D, FF), f32), pltpu.VMEM((D, D), f32)],
        compiler_params=pltpu.CompilerParams(
            vmem_limit_bytes=VMEM_LIMIT, dimension_semantics=("arbitrary",)
        ),
    )(lens, x, att, cot, wo, wu, wd, gm)


class Scatter:
    @staticmethod
    def scratch(dims, rows, width):
        nz, nx, ny, nc = dims
        most = max(nx, ny)
        half = (rows // 2, width) if rows % 32 == 0 else (rows, width // 2)
        return [
            pltpu.VMEM((nc - 1, nz, nx, ny, rows, width), bf),
            pltpu.VMEM((nz, nx, ny, rows, width), bf),
            pltpu.VMEM((nx - 1, nz, ny) + half, bf),
            pltpu.VMEM((ny - 1, nz, nx) + half, bf),
            pltpu.VMEM((2, nz, most) + half, bf),
            pltpu.VMEM((ny - 1, nz) + half, bf),
            pltpu.VMEM((nx - 1, nz) + half, bf),
            pltpu.VMEM((nz, rows, width), bf),
            pltpu.VMEM((nz - 1, rows, width), bf),
        ]

    @staticmethod
    def copies(dims):
        nz, nx, ny, nc = dims
        return (nc - 1) + 2 * (nx - 1) + 2 * (ny - 1) + (nz - 1)

    def __init__(self, pc, cp, g, mine, out, scratch):
        self.pc, self.mine, self.out, self.bufs = pc, mine, out, scratch
        got1, held1, got2a, got2b, held2, got3a, got3b, held3, got4 = scratch
        a, b = self.a, self.b = shares(*g.shape[-2:])
        every = slice(None)
        self.one = [
            cp.make(g.at[:, :, :, to], got1.at[o - 1], got1.at[o - 1], pc.at(c=to))
            for o, to, _ in pc.partners("c")
        ]
        self.two = [
            cp.make(held1.at[(every, to, every) + a], got2a.at[o - 1], got2a.at[o - 1], pc.at(x=to))
            for o, to, _ in pc.partners("x")
        ] + [
            cp.make(held1.at[(every, every, to) + b], got2b.at[o - 1], got2b.at[o - 1], pc.at(y=to))
            for o, to, _ in pc.partners("y")
        ]
        self.three = [
            cp.make(held2.at[0, :, to], got3a.at[o - 1], got3a.at[o - 1], pc.at(y=to))
            for o, to, _ in pc.partners("y")
        ] + [
            cp.make(held2.at[1, :, to], got3b.at[o - 1], got3b.at[o - 1], pc.at(x=to))
            for o, to, _ in pc.partners("x")
        ]
        self.four = [
            cp.make(held3.at[to], got4.at[o - 1], got4.at[o - 1], pc.at(z=to)) for o, to, _ in pc.partners("z")
        ]

    @staticmethod
    def total(acc, got, n):
        if n == 2:
            return acc + got[0]
        acc = acc.astype(f32)
        for o in range(n - 1):
            acc = acc + got[o].astype(f32)
        return acc

    def step(self, k):
        pc = self.pc
        got1, held1, got2a, got2b, held2, got3a, got3b, held3, got4 = self.bufs
        every = slice(None)
        if k == 0:
            start(self.one)
        elif k == 1:
            finish(self.one)
            for z in range(pc.nz):
                for x in range(pc.nx):
                    acc = self.mine(z, x)
                    for o in range(pc.nc - 1):
                        acc = acc + got1[o, z, x]
                    held1[z, x] = acc
            start(self.two)
        elif k == 2:
            finish(self.two)
            held2[0, :, : pc.ny] = self.total(held1[(every, pc.x, every) + self.a], got2a, pc.nx).astype(bf)
            held2[1, :, : pc.nx] = self.total(held1[(every, every, pc.y) + self.b], got2b, pc.ny).astype(bf)
            start(self.three)
        elif k == 3:
            finish(self.three)
            held3[(every,) + self.a] = self.total(held2[0, :, pc.y], got3a, pc.ny).astype(bf)
            held3[(every,) + self.b] = self.total(held2[1, :, pc.x], got3b, pc.nx).astype(bf)
            start(self.four)
        else:
            finish(self.four)
            self.out[...] = self.total(held3[pc.z], got4, pc.nz).astype(f32)


def back_kernel(dims, slots, pack, near, *refs):
    refs = list(refs)

    def take(n):
        out = refs[:n]
        del refs[:n]
        return out

    x_ref, q_ref, k_ref, v_ref, da_ref, lse_ref, dmid_ref, mean_ref, ks_ref, vs_ref = take(10)
    wq_ref, wk_ref, wv_ref, ga_ref = take(4)
    (g1_ref,) = take(1) if near else (None,)
    (din_ref,) = take(1)
    outs = take(2 if near else 1)
    aq, ak, av, dq_ref, dk_ref, dv_ref, dks_ref, dvs_ref, far_ref = take(9)
    far_send, far_got = take(2), take(2)
    if near:
        (g2_ref, own1) = take(2)
        bufs1, bufs2 = take(9), take(9)
        (own_sem,) = take(1)
    send_sem, recv_sem = take(2)
    T, D = x_ref.shape
    spt, nseq = slots // SPAN, T // slots
    pc = Place(dims)
    cp = Copies(send_sem, recv_sem)
    seq, dp = lax.axis_index("seq"), lax.axis_index("dp")
    seqn = pc.ny * pc.nc
    spans_all, seqs, _ = mean_ref.shape
    i, n = pl.program_id(0), pl.num_programs(0) // 2
    far = []
    for send, got in zip(far_send, far_got):
        far.append([])
        for o in range(1, seqn):
            to = (seq + o) % seqn
            far[-1].append(cp.make(send.at[:, pl.ds(to * spt, spt)], got.at[o - 1], got.at[o - 1], (dp, to)))
    if near:
        own_copy = pltpu.make_async_copy(g1_ref.at[:, :, :, pc.c], own1, own_sem.at[0])
        big = Scatter(pc, cp, g1_ref, lambda z, x: own1[z, x], outs[0], bufs1)
        small = Scatter(pc, cp, g2_ref, lambda z, x: g2_ref[z, x, :, pc.c], outs[1], bufs2)

    seq_peers = [(dp, (seq + o) % seqn) for o in range(1, seqn)]
    zx = [pc.at(**{a: to}) for a in ("z", "x") for _, to, _ in pc.partners(a)]

    @pl.when(i == 0)
    def _():
        pc.greet(zx + seq_peers)
        if near:
            own_copy.start()
        for acc in (aq, ak, av):
            acc[...] = jnp.zeros_like(acc)
        pc.meet(zx + seq_peers)
        if near:
            big.step(0)
            own_copy.wait()

    if near:
        for k, at in ((1, 1), (2, n // 2), (3, n - 1), (4, n + n // 3)):

            @pl.when(i == at)
            def _(k=k):
                big.step(k)

    ga = ga_ref[...]

    groups = ((0, seqs - nseq), (seqs - nseq, seqs))

    def send_far(g):
        lo, hi = groups[g]
        for t in range(spans_all):
            far_send[g][0, t] = dks_ref[lo:hi, t, :].astype(bf)
            far_send[g][1, t] = dvs_ref[lo:hi, t, :].astype(bf)
        start(far[g])

    @pl.when(i == n - 1)
    def _():
        send_far(0)

    @pl.when(i < n)
    def _():
        tok = pl.ds(pl.multiple_of(i * T, T), T)
        sub = T // 1
        xt = (unit_rows(x_ref)[0] * ga).astype(bf).T
        cuts = [(k, h) for k in range(3) for h in (slice(0, D // 2), slice(D // 2, D))]

        def gather_terms(b):
            rows = pl.ds(pl.multiple_of(i * T + b * sub, sub), sub)

            def part(k, h):
                (aq, ak, av)[k][:, h] += dot(xt[:, b * sub : (b + 1) * sub], (dq_ref, dk_ref, dv_ref)[k][rows, h])

            return [partial(part, k, h) for k, h in cuts]

        each = sub // SPAN * (D // 128)
        beside = {}
        for b in range(1 - 1):
            beside.update(spread_out(gather_terms(b), (b + 1) * each + 4, (b + 2) * each + 4))
        attend_backward(slots, i, seq, spans_all, q_ref, k_ref, v_ref, da_ref, ks_ref, vs_ref, lse_ref,
                        dq_ref.at[tok], dk_ref.at[tok], dv_ref.at[tok], dks_ref, dvs_ref, beside)
        for work in gather_terms(1 - 1):
            work()

    @pl.when(i == n - 1)
    def _():
        send_far(1)
        mean = mean_ref[...].astype(f32)
        terms = [jnp.zeros((D, D), f32)] * 2
        for g, (lo, hi) in enumerate(groups):
            mb = (mean[:, lo:hi].reshape(spans_all * (hi - lo), D) * ga).astype(bf)
            for h in range(2):
                terms[h] = terms[h] + dot(mb, far_send[g][h].reshape(spans_all * (hi - lo), D), 0, 0)
        rows = D // pack
        parts = (aq[...], ak[...] + terms[0], av[...] + terms[1])
        for j, part in enumerate(parts):
            if near:
                g2_ref[:, :, :, :, j * rows : (j + 1) * rows, :] = part.astype(bf).reshape(dims + (rows, D))
            else:
                outs[0][j] = part
        if near:
            small.step(0)

    def products(j):
        tok = pl.ds(pl.multiple_of(j * T, T), T)
        dxn = dot(dq_ref[tok, :], wq_ref[...], 1, 1)
        dxn = dxn + dot(dk_ref[tok, :], wk_ref[...], 1, 1)
        return dxn + dot(dv_ref[tok, :], wv_ref[...], 1, 1)

    def to_input(j, dxn):
        parts = []
        for s in range(T // SPAN):
            row = far_ref[s % spt, pl.ds(j * nseq + s // spt, 1), :]
            parts.append(dxn[s * SPAN : (s + 1) * SPAN] + row)
        gd = jnp.concatenate(parts, axis=0) * ga
        xr, r = unit_rows(x_ref)
        coef = jnp.mean(gd * xr, axis=1, keepdims=True)
        din_ref[...] = (dmid_ref[...].astype(f32) + r * (gd - xr * coef)).astype(bf)

    @pl.when(i == n)
    def _():
        dxn = products(0)
        for g, (lo, hi) in enumerate(groups):
            finish(far[g])
            tot = []
            for h in range(2):
                acc = far_send[g][h, pl.ds(seq * spt, spt)].astype(f32)
                for o in range(seqn - 1):
                    acc = acc + far_got[g][o, h].astype(f32)
                tot.append(acc.astype(bf).reshape(spt * (hi - lo), D))
            rows = dot(tot[0], wk_ref[...], 1, 1) + dot(tot[1], wv_ref[...], 1, 1)
            far_ref[:, lo:hi, :] = (rows * (1.0 / SPAN)).reshape(spt, hi - lo, D)
        to_input(0, dxn)

    if near:
        for k, at in ((1, 1), (2, n // 2), (3, 2 * n // 3)):

            @pl.when(i == n + at)
            def _(k=k):
                small.step(k)

    @pl.when(i > n)
    def _():
        to_input(i - n, products(i - n))

    if near:

        @pl.when(i == 2 * n - 1)
        def _():
            small.step(4)


def attend_backward(slots, i, seq, spans_all, q_ref, k_ref, v_ref, da_ref, ks_ref, vs_ref, lse_ref,
                    dq_ref, dk_ref, dv_ref, dks_ref, dvs_ref, beside):
    T, D = q_ref.shape
    spt, nseq = slots // SPAN, T // slots
    causal = causal_mask()
    t_row = lax.broadcasted_iota(jnp.int32, (FARP, 2 * SPAN), 0)

    def where(u):
        s, p = u
        return slice(s * SPAN, (s + 1) * SPAN), slice(p * 128, (p + 1) * 128), i * nseq + s // spt

    def scores(u):
        rows, ln, sq = where(u)
        ke = jnp.concatenate([k_ref[rows, ln], ks_ref[sq, :, ln]], axis=0)
        ve = jnp.concatenate([v_ref[rows, ln], vs_ref[sq, :, ln]], axis=0)
        qbd, dbd = pair_diag(q_ref[rows, ln]), pair_diag(da_ref[rows, ln])
        return dot(ke, qbd, 1, 1), dot(ve, dbd, 1, 1)

    def weigh(u, got):
        sc, dp = got
        rows, p = where(u)[0], u[1]
        far = t_row < (seq * spt + u[0] % spt)
        lse = jnp.concatenate([lse_ref[2 * p : 2 * p + 1, rows], lse_ref[2 * p + 1 : 2 * p + 2, rows]], axis=1)
        pn = jnp.where(causal, jnp.exp(sc[:SPAN] - lse), 0.0)
        pf = jnp.where(far, jnp.exp(sc[SPAN:] - lse), 0.0)
        dpn, dpf = dp[:SPAN], dp[SPAN:]
        delta = jnp.sum(pn * dpn, axis=0, keepdims=True) + jnp.sum(pf * dpf, axis=0, keepdims=True)
        dsn, dsf = (pn * (dpn - delta)).astype(bf), (pf * (dpf - delta)).astype(bf)
        return pn.astype(bf), pf.astype(bf), dsn, dsf

    def combine(u, pn, pf, dsn, dsf):
        rows, ln, sq = where(u)
        qbd, dbd = pair_diag(q_ref[rows, ln]), pair_diag(da_ref[rows, ln])
        dv = dot(jnp.concatenate([pn, pf], axis=0), dbd)
        ds = jnp.concatenate([dsn, dsf], axis=0)
        dk = dot(ds, qbd)
        ke = jnp.concatenate([k_ref[rows, ln], ks_ref[sq, :, ln]], axis=0)
        dq = dot(ke, ds, 0, 0)
        dq = jnp.concatenate([dq[:HD, :SPAN], dq[HD:, SPAN:]], axis=0) * (HD**-0.5)
        dq_ref[rows, ln] = dq.astype(bf).T
        dk_ref[rows, ln] = dk[:SPAN].astype(bf)
        dv_ref[rows, ln] = dv[:SPAN].astype(bf)
        fk, fv = dk[SPAN : SPAN + spans_all], dv[SPAN : SPAN + spans_all]
        if u[0] % spt == 0:
            dks_ref[sq, :, ln] = fk
            dvs_ref[sq, :, ln] = fv
        else:
            dks_ref[sq, :, ln] += fk
            dvs_ref[sq, :, ln] += fv

    units = [(s, p) for s in range(T // SPAN) for p in range(D // 128)]
    staged(units, scores, weigh, combine, beside)


def back_call(dims, slots, block, pack, near, x, q, k, v, da, lse, dmid, mean, ks, vs, wq, wk, wv, ga, g1):
    n_tok, D = x.shape
    nz, nx, ny, nc = dims
    n = n_tok // block
    spt, nseq = slots // SPAN, block // slots
    spans_all, seqs, _ = mean.shape
    seqn = ny * nc
    vm = pltpu.VMEM
    early = pl.BlockSpec((block, D), lambda i: (jnp.minimum(i, n - 1), 0))
    late = pl.BlockSpec((block, D), lambda i: (jnp.maximum(i - n, 0), 0))
    rows2 = D // pack * 3
    in_specs = (
        [pl.BlockSpec((block, D), lambda i: (i % n, 0))]
        + [early] * 4
        + [pl.BlockSpec((H, block), lambda i: (0, jnp.minimum(i, n - 1))), late]
        + [full(mean.shape), full(ks.shape), full(vs.shape)]
        + [full((D, D))] * 3
        + [full((1, D))]
    )
    args = [x, q, k, v, da, lse, dmid, mean, ks, vs, wq, wk, wv, ga]
    out_specs, out_shape = [late], [sds((n_tok, D), bf)]
    scratch = [vm((D, D), f32)] * 3 + [vm((n_tok, D), bf)] * 3 + [vm((seqs, spans_all, D), f32)] * 2
    scratch += [
        vm((spt, seqs, D), f32),
        vm((2, spans_all, seqs - nseq, D), bf),
        vm((2, spans_all, nseq, D), bf),
        vm((max(seqn - 1, 1), 2, spt, seqs - nseq, D), bf),
        vm((max(seqn - 1, 1), 2, spt, nseq, D), bf),
    ]
    copies = 2 * (seqn - 1)
    if near:
        rows1 = g1.shape[1]
        args.append(g1.reshape(dims + g1.shape[1:]))
        in_specs.append(pl.BlockSpec(memory_space=pl.ANY))
        out_specs += [full((rows1, D)), full((rows2, D))]
        out_shape += [sds((rows1, D), f32), sds((rows2, D), f32)]
        scratch += [vm(dims + (rows2, D), bf), vm((nz, nx, ny, rows1, D), bf)]
        scratch += Scatter.scratch(dims, rows1, D) + Scatter.scratch(dims, rows2, D)
        scratch.append(pltpu.SemaphoreType.DMA((1,)))
        copies += 2 * Scatter.copies(dims)
    else:
        out_specs.append(full((3, D, D)))
        out_shape.append(sds((3, D, D), f32))
    scratch += [pltpu.SemaphoreType.DMA((max(copies, 1),))] * 2
    return pl.pallas_call(
        partial(back_kernel, dims, slots, pack, near),
        grid=(2 * n,),
        in_specs=in_specs,
        out_specs=out_specs,
        out_shape=out_shape,
        scratch_shapes=scratch,
        compiler_params=pltpu.CompilerParams(
            vmem_limit_bytes=VMEM_LIMIT, collective_id=1, has_side_effects=True,
            dimension_semantics=("arbitrary",),
        ),
    )(*args)


def last_kernel(rd, rf, din_ref, m_ref, a_ref, wq_ref, wk_ref, wv_ref, wu_ref, ga_ref, gm_ref,
                out_ref, gq_ref, gk_ref, gv_ref, go_ref, gu_ref, gd_ref, gga_ref, ggm_ref):
    out_ref[...] = din_ref[...].astype(f32)
    D = out_ref.shape[1]
    FF = gu_ref.shape[1]

    @pl.when(pl.program_id(0) == 0)
    def _():
        attn = jnp.zeros((rd, 1), f32)
        for j, (w_ref, g_ref) in enumerate(((wq_ref, gq_ref), (wk_ref, gk_ref), (wv_ref, gv_ref))):
            g = a_ref[j * rd : (j + 1) * rd, :]
            g_ref[...] = g
            attn = attn + jnp.sum(g * w_ref[...].astype(f32), axis=1, keepdims=True)
        go_ref[...] = m_ref[:rd, :]
        up = jnp.zeros((rd, 1), f32)
        for j in range(FF // D):
            g = m_ref[rd * (j + 1) : rd * (j + 2), :]
            gu_ref[:, j * D : (j + 1) * D] = g
            up = up + jnp.sum(g * wu_ref[:, j * D : (j + 1) * D].astype(f32), axis=1, keepdims=True)
        gd_ref[...] = m_ref[rd * (FF // D + 1) :, :]
        for total, gain, out in ((attn, ga_ref, gga_ref), (up, gm_ref, ggm_ref)):
            row = jnp.broadcast_to(total, (rd, 128)).T[:1, :]
            out[...] = row[:, :rd] / gain[...].astype(f32)


def last_call(block, din, sums_m, sums_a, wq, wk, wv, wu, ga, gm):
    n_tok, D = din.shape
    rd, FF = wu.shape
    rf = sums_m.shape[0] - rd * (FF // D + 1)
    tok = pl.BlockSpec((block, D), lambda i: (i, 0))
    args = [sums_m, sums_a, wq, wk, wv, wu, ga, gm]
    shapes = [(rd, D)] * 4 + [(rd, FF), (rf, D), (1, rd), (1, rd)]
    return pl.pallas_call(
        partial(last_kernel, rd, rf),
        grid=(n_tok // block,),
        in_specs=[tok] + [full(a.shape) for a in args],
        out_specs=[tok] + [full(s) for s in shapes],
        out_shape=[sds((n_tok, D), f32)] + [sds(s, f32) for s in shapes],
        compiler_params=pltpu.CompilerParams(
            vmem_limit_bytes=VMEM_LIMIT, dimension_semantics=("arbitrary",)
        ),
    )(din, *args)


def body(dims, inputs, lengths, cotangent, w_query, w_key, w_value, w_out, w_up, w_down, gain_attn, gain_mlp):
    seqs, slots, D = inputs.shape
    nz, nx, ny, nc = dims
    ndev = nz * nx * ny * nc
    FF = w_up.shape[1]
    rd, rf = w_query.shape[0], w_down.shape[0]
    n_tok = seqs * slots
    block = 1024
    x = inputs.reshape(n_tok, D)
    cot = cotangent.reshape(n_tok, D)
    gains = [g.reshape(1, rd) for g in (gain_attn, gain_mlp)]
    everyone = ("dp", "seq")
    near = rd % 16 == 0 and n_tok // block >= 6
    if near:
        w_first, w_later = (w_query, w_key, w_value), (w_up, w_down, w_out)
    else:
        wq, wk, wv, wu, wd, wo = (
            lax.all_gather(w, everyone, axis=0, tiled=True)
            for w in (w_query, w_key, w_value, w_up, w_down, w_out)
        )
        w_first, w_later = (wq, wk, wv), ()
    q, k, v, att, lse, ks, vs, mean, ga, gm, *later = front_call(dims, slots, block, x, w_first, w_later, gains, near)
    if near:
        wq, wk, wv, wu, wd, wo = (w.reshape(-1, w.shape[-1]) for w in later)
    pack = ndev if near else 32
    output, datt, dmid, sums_m = mlp_call(512, slots, block, pack, lengths, x, att, cot, wo, wu, wd, gm)
    grad_in, *sums = back_call(
        dims, slots, block, pack, near, x, q, k, v, datt, lse, dmid, mean, ks, vs, wq, wk, wv, ga, sums_m
    )
    if near:
        grad_in, g_q, g_k, g_v, g_out, g_up, g_down, g_ga, g_gm = last_call(
            n_tok // 3, grad_in, *sums, w_query, w_key, w_value, w_up, *gains
        )
        g_ga, g_gm = g_ga.reshape(rd), g_gm.reshape(rd)
    else:
        pd, pf = D // pack, FF // pack
        last = pd * (FF // D + 1) + pf

        def scattered(a):
            return lax.psum_scatter(a.astype(f32), everyone, scatter_dimension=0, tiled=True)

        g_out = scattered(sums_m[:, :pd].reshape(D, D))
        g_up = scattered(
            jnp.concatenate([sums_m[:, pd * (j + 1) : pd * (j + 2)].reshape(D, D) for j in range(FF // D)], axis=1)
        )
        g_down = scattered(sums_m[:, pd * (FF // D + 1) : last].reshape(FF, D))
        g_q, g_k, g_v = (scattered(sums[0][j]) for j in range(3))
        g_ga = jnp.sum(
            w_query.astype(f32) * g_q + w_key.astype(f32) * g_k + w_value.astype(f32) * g_v, axis=1
        ) / gain_attn.astype(f32)
        g_gm = jnp.sum(w_up.astype(f32) * g_up, axis=1) / gain_mlp.astype(f32)
        grad_in = grad_in.astype(f32)
    return (
        output.reshape(inputs.shape), grad_in.reshape(inputs.shape),
        g_q, g_k, g_v, g_out, g_up, g_down, g_ga, g_gm,
    )


def solution(mesh):
    dp, seq = mesh.shape["dp"], mesh.shape["seq"]
    nx = max(d for d in range(1, dp + 1) if dp % d == 0 and d * d <= dp)
    nc = 2 if seq % 2 == 0 else 1
    dims = (dp // nx, nx, seq // nc, nc)
    rows, vec = P(("dp", "seq"), None), P(("dp", "seq"))
    tokens = P("dp", "seq", None)
    return jax.shard_map(
        partial(body, dims),
        mesh=mesh,
        in_specs=(tokens, P("dp"), tokens) + (rows,) * 6 + (vec,) * 2,
        out_specs=(tokens, tokens) + (rows,) * 6 + (vec,) * 2,
        check_vma=False,
    )
```
